128 devices in a mesh: head: 4 (over y_hi, core), req: 32 (over z, x, y_lo).
Axes of the slice: x: 4, y: 4 (y_hi: 2, y_lo: 2; y = y_hi * 2 + y_lo), z: 4, core: 2. Of those that a mesh axis runs over, the one named last changes fastest.
Arguments:
- learner_acceptance_matrix: float32 [2048, 2048], P(('head', 'req')), may hold values from -0.125 to 0.125
- learner_address_matrix: float32 [2048, 2048], P(('head', 'req')), may hold values from -0.125 to 0.125
- learner_content_matrix: float32 [2048, 2048], P(('head', 'req')), may hold values from -0.125 to 0.125
- learner_gating_matrix: float32 [2048, 2048], P(('head', 'req')), may hold values from -0.125 to 0.125
- learner_result_matrix: float32 [2048, 2048], P(('head', 'req')), may hold values from -0.125 to 0.125
- fading_narrowing_matrix: bfloat16 [2048, 64], replicated, may hold values from -0.125 to 0.125
- fading_widening_matrix: bfloat16 [64, 2048], P(None, 'head'), may hold values from -0.75 to 0.75
- feature_fading_speed: float32 [2048], P('head'), may hold values from 0.001 to 0.5
- current_reward: float32 [2048], P('head'), may hold values from -1 to 1
- symbol_blending_factors: float32 [5, 2048], replicated, may hold values from 0 to 1
- group_scaling_factor: float32 [2048], P('head'), may hold values from 0.5 to 1.5
- group_scaling_offset: float32 [2048], P('head'), may hold values from -1.75 to 1.75
- request_hidden_entries: bfloat16 [64, 512, 2048], P('req', None, 'head'), may hold values from -6 to 6
- request_valid_count: int32 [64], P('req'), may hold values from 1 to 512, 24576 in all
- request_destination_place: int32 [64], P('req'), may hold values from 0 to 2047, as said below
- newest_symbol_hidden: bfloat16 [2048, 2048], P('req', 'head'), may hold values from -6 to 6
- preceding_hidden_entry: bfloat16 [2048, 2048], P('req', 'head'), may hold values from -6 to 6
- place_memory_matrix: float32 [2048, 32, 64, 64], P('req', 'head'), may hold values from -6 to 6
- place_newness_marks: int32 [2048], P('req'), may hold values 0 or 1
Outputs:
- prompt_hidden: bfloat16 [64, 512, 2048], P('req', None, 'head')
- decode_hidden: bfloat16 [2048, 2048], P('req', 'head')
- new_state: float32 [2048, 32, 64, 64], P('req', 'head')
- new_shift: bfloat16 [2048, 2048], P('req', 'head')
The draws below stay inside these ranges and needn't reach their ends.
Inputs may be any that keep to these rules, and one draw needn't show every extreme that they name: Prompt p's slot is one of the 64 slots of the same index of req as prompt p, that is p // 2 == request_destination_place[p] // 64; the slots are distinct. `request_valid_count`: the longest prompt has exactly 512 live tokens.
All inputs are finite; a program needn't handle non-finite values. No bound on the sum of `request_valid_count` or of `place_newness_marks` on one device may be relied on, other than what follows from the above.
Results may differ from the reference program's by a relative error of at most 0.033.
Values may be sent and summed in bfloat16 or wider, within the bound.
No kernel may reach another device: no remote copies, remote signals or barrier semaphores. Data moves between devices by JAX's collectives and lax.ppermute only.
A program may use at most 256 MiB of HBM per device.

```python
import math
import jax
import jax.numpy as jnp
import numpy as np
from jax import lax

EMBEDDING_SIZE = 2048
H = 32
HS = 64
DECAY_RANK = 64
L = 512
PROMPT_DEV = 2
REQ_DEV = 64
PROMPTS = 64
SLOTS = 2048
N_HEAD = 4
N_REQ = 32


def draw_request_destination_place(key, part):
    devices = PROMPTS // PROMPT_DEV
    key_list = jax.random.split(jax.random.fold_in(key, 7), devices)
    orders = jax.vmap(lambda single_key: jax.random.permutation(single_key, REQ_DEV))(key_list)
    targets = jax.random.randint(jax.random.fold_in(key, 11), (devices,), 0, REQ_DEV)
    targets = targets.at[0].set(0).at[devices - 1].set(REQ_DEV - 1)
    chosen = orders[:, :PROMPT_DEV]
    offsets = (chosen - chosen[:, :1] + targets[:, None]) % REQ_DEV
    base_rows = jnp.arange(devices, dtype=jnp.int32)[:, None] * REQ_DEV
    return (base_rows + offsets).reshape(PROMPTS).astype(jnp.int32)


def set_ends(result, stream_key, least, high):
    place = [jax.random.randint(jax.random.fold_in(stream_key, axis), (), 0, length) for axis, length in enumerate(result.shape)]
    main_axis = result.shape.index(max(result.shape))
    neighbour = place[:main_axis] + [(place[main_axis] + 1) % result.shape[main_axis]] + place[main_axis + 1:]
    return result.at[tuple(place)].set(least).at[tuple(neighbour)].set(high)


def block_scale(key, extent, cuts, low, top_value):
    def one(dim, shards_of):
        steps = jax.random.uniform(jax.random.fold_in(jax.random.fold_in(key, 6), dim), (shards_of,), jnp.float32, low / len(cuts), top_value / len(cuts))
        return jnp.repeat(jnp.exp(steps), extent[dim] // shards_of).reshape((-1,) + (1,) * (len(extent) - dim - 1))

    level = one(*cuts[0])
    for cut in cuts[1:]:
        level = level * one(*cut)
    return level


def split_up(number_of, total, bound, slope):
    weights = [(1 << 20) // math.isqrt(rank ** slope) + 1 for rank in range(2, number_of + 1)]
    rest, counts = total - bound - (number_of - 1), [1] * (number_of - 1)
    while rest > 0:
        candidates = [i for i in range(number_of - 1) if counts[i] < bound]
        whole, budget = sum([weights[i] for i in candidates]), rest
        for i in candidates:
            more = min(bound - counts[i], max(1, budget * weights[i] // whole), rest)
            counts[i] = counts[i] + more
            rest = rest - more
    return np.array([bound] + counts)


def ragged_sizes(stream_key, count, total, most, lean):
    if count == 2:
        one = jax.random.randint(stream_key, (), max(1, total - most), min(most, total - 1) + 1)
        return jnp.stack([one, total - one])
    sizes = jnp.asarray(split_up(count, total, most, lean), jnp.int32)
    pairs = (count - 1) // 2
    donor, taker = sizes[1:1 + 2 * pairs:2], sizes[2:2 + 2 * pairs:2]
    room = jnp.minimum(donor - 1, most - taker)
    shifted = jax.random.randint(jax.random.fold_in(stream_key, 1), (pairs,), 0, 1 << 20) % (room + 1)
    sizes = sizes.at[1:1 + 2 * pairs:2].set(donor - shifted).at[2:2 + 2 * pairs:2].set(taker + shifted)
    return sizes[jax.random.permutation(jax.random.fold_in(stream_key, 2), count)]


def gaussian(stream_key, dims, deviation, limit, cuts=(), kind=jnp.bfloat16):
    drawn = deviation * jax.random.normal(stream_key, dims, jnp.float32)
    if cuts:
        drawn = drawn * block_scale(stream_key, dims, cuts, -0.22, 0.18)
    return jnp.clip(drawn, -limit, limit).astype(kind)


def setup_inputs(seed: int = 0) -> dict:
    keys = jax.random.split(jax.random.key(seed), 20)
    return {
        "learner_acceptance_matrix": gaussian(keys[0], (EMBEDDING_SIZE, EMBEDDING_SIZE), EMBEDDING_SIZE ** -0.5, 0.125, ((0, 128),), jnp.float32),
        "learner_address_matrix": gaussian(keys[1], (EMBEDDING_SIZE, EMBEDDING_SIZE), EMBEDDING_SIZE ** -0.5, 0.125, ((0, 128),), jnp.float32),
        "learner_content_matrix": gaussian(keys[2], (EMBEDDING_SIZE, EMBEDDING_SIZE), EMBEDDING_SIZE ** -0.5, 0.125, ((0, 128),), jnp.float32),
        "learner_gating_matrix": gaussian(keys[3], (EMBEDDING_SIZE, EMBEDDING_SIZE), EMBEDDING_SIZE ** -0.5, 0.125, ((0, 128),), jnp.float32),
        "learner_result_matrix": gaussian(keys[4], (EMBEDDING_SIZE, EMBEDDING_SIZE), EMBEDDING_SIZE ** -0.5, 0.125, ((0, 128),), jnp.float32),
        "fading_narrowing_matrix": gaussian(keys[5], (EMBEDDING_SIZE, DECAY_RANK), EMBEDDING_SIZE ** -0.5, 0.125),
        "fading_widening_matrix": gaussian(keys[6], (DECAY_RANK, EMBEDDING_SIZE), DECAY_RANK ** -0.5, 0.75, ((1, 4),)),
        "feature_fading_speed": jnp.clip(jnp.exp(math.log(0.5) - 6.214608 * jax.random.uniform(keys[7], (EMBEDDING_SIZE,), jnp.float32) ** block_scale(keys[7], (EMBEDDING_SIZE,), ((0, 4),), -0.2, 0.2)), 0.001, 0.5),
        "current_reward": jnp.clip(jax.random.uniform(keys[8], (EMBEDDING_SIZE,), jnp.float32, -1.0, 1.0) * block_scale(keys[8], (EMBEDDING_SIZE,), ((0, 4),), -0.4, 0.0), -1.0, 1.0),
        "symbol_blending_factors": jnp.clip(jax.random.uniform(keys[9], (5, EMBEDDING_SIZE), jnp.float32, 0.0, 1.0), 0.0, 1.0),
        "group_scaling_factor": jnp.clip(1.0 + 0.1 * jax.random.normal(keys[10], (EMBEDDING_SIZE,), jnp.float32), 0.5, 1.5),
        "group_scaling_offset": gaussian(keys[11], (EMBEDDING_SIZE,), 0.3, 1.75, ((0, 4),), jnp.float32),
        "request_hidden_entries": gaussian(keys[12], (PROMPTS, L, EMBEDDING_SIZE), 1.0, 6.0, ((0, 32), (2, 4))),
        "request_valid_count": ragged_sizes(keys[13], PROMPTS, PROMPTS * L * 3 // 4, L, 1).astype(jnp.int32),
        "request_destination_place": draw_request_destination_place(jax.random.fold_in(keys[19], 71), 0),
        "newest_symbol_hidden": gaussian(keys[15], (SLOTS, EMBEDDING_SIZE), 1.0, 6.0, ((0, 32), (1, 4))),
        "preceding_hidden_entry": gaussian(keys[16], (SLOTS, EMBEDDING_SIZE), 1.0, 6.0, ((0, 32), (1, 4))),
        "place_memory_matrix": gaussian(keys[17], (SLOTS, H, HS, HS), 1.0, 6.0, ((0, 32), (1, 4)), jnp.float32),
        "place_newness_marks": set_ends((jax.random.randint(keys[18], (SLOTS,), 0, 4) < 1).astype(jnp.int32), jax.random.fold_in(keys[18], 1), 0, 1),
    }


NORM_EPS = 0.00064

def project(left, right):
    return jnp.dot(left, right, preferred_element_type=jnp.float32)

def make_inputs(present, earlier, symbol_blending_factors, w_recept, w_key, w_value, w_gate, fading_narrowing_matrix, fading_widening_matrix, feature_fading_speed):
    current = present.astype(jnp.float32)
    previous = earlier.astype(jnp.float32)
    mixed_rows = [(current + (previous - current) * symbol_blending_factors[number]).astype(jnp.bfloat16) for number in range(5)]
    acceptance_entries = project(mixed_rows[0], w_recept).astype(jnp.bfloat16)
    address_entry_tile = project(mixed_rows[1], w_key).astype(jnp.bfloat16)
    content_entries = project(mixed_rows[2], w_value).astype(jnp.bfloat16)
    lowrank = jnp.tanh(project(mixed_rows[3], fading_narrowing_matrix)).astype(jnp.bfloat16)
    fading_exponent_log = -feature_fading_speed * jnp.exp(project(lowrank, fading_widening_matrix))
    gate_rows = jax.nn.silu(project(mixed_rows[4], w_gate))
    return (acceptance_entries.astype(jnp.float32), address_entry_tile.astype(jnp.float32), content_entries.astype(jnp.float32), fading_exponent_log, gate_rows)

def group_norm(outputs, group_scaling_factor, group_scaling_offset, gate_rows):
    center = outputs - lax.optimization_barrier(jnp.mean(outputs, axis=-1, keepdims=True))
    spread = lax.optimization_barrier(jnp.mean(center * center, axis=-1, keepdims=True))
    normed = (center / jnp.sqrt(spread + NORM_EPS)).reshape(outputs.shape[0], -1)
    return ((normed * group_scaling_factor + group_scaling_offset) * gate_rows).astype(jnp.bfloat16)

def head_sum(normed, w_output):
    block_width = normed.shape[1] // N_HEAD
    running = jnp.zeros((normed.shape[0], w_output.shape[1]), jnp.float32)
    for group_index in range(N_HEAD):
        lower_col = group_index * block_width
        partial_sum = project(normed[:, lower_col:lower_col + block_width], w_output[lower_col:lower_col + block_width])
        rounded = lax.optimization_barrier(partial_sum.astype(jnp.bfloat16))
        running = running + rounded.astype(jnp.float32)
    return running

def reference(learner_acceptance_matrix, learner_address_matrix, learner_content_matrix, learner_gating_matrix, learner_result_matrix, fading_narrowing_matrix, fading_widening_matrix, feature_fading_speed, current_reward, symbol_blending_factors, group_scaling_factor, group_scaling_offset, request_hidden_entries, request_valid_count, request_destination_place, newest_symbol_hidden, preceding_hidden_entry, place_memory_matrix, place_newness_marks):
    w_recept = learner_acceptance_matrix.astype(jnp.bfloat16)
    w_key = learner_address_matrix.astype(jnp.bfloat16)
    w_value = learner_content_matrix.astype(jnp.bfloat16)
    w_gate = learner_gating_matrix.astype(jnp.bfloat16)
    w_output = learner_result_matrix.astype(jnp.bfloat16)
    prompt_count, length, model_width = request_hidden_entries.shape
    group_count_all, group_breadth = (place_memory_matrix.shape[1], place_memory_matrix.shape[2])
    group_reward = current_reward.reshape(group_count_all, group_breadth)
    earlier = jnp.concatenate([jnp.zeros_like(request_hidden_entries[:, :1]), request_hidden_entries[:, :-1]], axis=1)
    acceptance_entries, address_entry_tile, content_entries, fading_exponent_log, gate_rows = make_inputs(request_hidden_entries.reshape(-1, model_width), earlier.reshape(-1, model_width), symbol_blending_factors, w_recept, w_key, w_value, w_gate, fading_narrowing_matrix, fading_widening_matrix, feature_fading_speed)
    positions = lax.broadcasted_iota(jnp.int32, (prompt_count, length), 1)
    live_mask = (positions < request_valid_count[:, None]).astype(jnp.float32).reshape(-1, 1)
    address_entry_tile = address_entry_tile * live_mask
    fading_exponent_log = fading_exponent_log * live_mask

    def shaped(array):
        return array.reshape(prompt_count, length, group_count_all, group_breadth).transpose(1, 0, 2, 3)

    def advance(running_memory, inputs):
        acceptance_array, address_array, content_array, w = inputs
        dyadic_matrix = address_array[..., :, None] * content_array[..., None, :]
        result_entry_amount = jnp.einsum('rnu,rnux->rnx', acceptance_array, running_memory + group_reward[..., :, None] * dyadic_matrix, precision=lax.Precision.HIGHEST)
        next_state = jnp.exp(w)[..., None] * running_memory + dyadic_matrix
        return (next_state, result_entry_amount)
    start_state = jnp.zeros((prompt_count, group_count_all, group_breadth, group_breadth), jnp.float32)
    final_state, outputs = lax.scan(advance, start_state, (shaped(acceptance_entries), shaped(address_entry_tile), shaped(content_entries), shaped(fading_exponent_log)))
    outputs = outputs.transpose(1, 0, 2, 3).reshape(-1, group_count_all, group_breadth)
    normed = group_norm(outputs, group_scaling_factor, group_scaling_offset, gate_rows)
    prompt_sum = head_sum(normed, w_output)
    prompt_hidden = (prompt_sum * live_mask).astype(jnp.bfloat16).reshape(prompt_count, length, model_width)
    select = (positions == request_valid_count[:, None] - 1).astype(jnp.float32)
    last_tokens = lax.optimization_barrier(jnp.sum(request_hidden_entries.astype(jnp.float32) * select[..., None], axis=1)).astype(jnp.bfloat16)
    fresh_mask = place_newness_marks == 1
    prior = jnp.where(fresh_mask[:, None], jnp.zeros_like(preceding_hidden_entry), preceding_hidden_entry)
    acceptance_each_group, address_each_group, value_per_head, decay_d, gate_d = make_inputs(newest_symbol_hidden, prior, symbol_blending_factors, w_recept, w_key, w_value, w_gate, fading_narrowing_matrix, fading_widening_matrix, feature_fading_speed)

    def blocked(array):
        return array.reshape((N_REQ, REQ_DEV) + array.shape[1:])

    def decode_block(inputs):
        acceptance_array, address_array, content_array, w, flags, states = inputs
        acceptance_array = acceptance_array.reshape(-1, group_count_all, group_breadth)
        address_array = address_array.reshape(-1, group_count_all, group_breadth)
        content_array = content_array.reshape(-1, group_count_all, group_breadth)
        w = w.reshape(-1, group_count_all, group_breadth)
        segment_opening = jnp.where((flags == 1)[:, None, None, None], jnp.zeros_like(states), states)
        result_entry_amount = jnp.einsum('lkh,lkhs->lks', acceptance_array, segment_opening, precision=lax.Precision.HIGHEST) + lax.optimization_barrier(jnp.sum(acceptance_array * group_reward * address_array, axis=-1, keepdims=True)) * content_array
        next_state = jnp.exp(w)[..., None] * segment_opening + address_array[..., :, None] * content_array[..., None, :]
        return (result_entry_amount, next_state)
    decode_out, next_states = lax.map(decode_block, (blocked(acceptance_each_group), blocked(address_each_group), blocked(value_per_head), blocked(decay_d), blocked(place_newness_marks), blocked(place_memory_matrix)))
    decode_out = decode_out.reshape(-1, group_count_all, group_breadth)
    decode_sum = head_sum(group_norm(decode_out, group_scaling_factor, group_scaling_offset, gate_d), w_output)
    prompt_taken = jnp.zeros((newest_symbol_hidden.shape[0],), jnp.float32).at[request_destination_place].set(1.0)
    decode_hidden = (decode_sum * (1.0 - prompt_taken)[:, None]).astype(jnp.bfloat16)
    new_state = next_states.reshape(place_memory_matrix.shape).at[request_destination_place].set(final_state)
    new_shift = newest_symbol_hidden.at[request_destination_place].set(last_tokens)
    return (prompt_hidden, decode_hidden, new_state, new_shift)
```

```python
import functools

import jax
import jax.numpy as jnp
import numpy as np
from jax import lax
from jax.experimental import pallas as pl
from jax.experimental.pallas import tpu as pltpu
from jax.sharding import PartitionSpec as P

NORM_EPS = 0.00064
N_HEAD, N_REQ = 4, 32
CH = 64
BF = jnp.bfloat16
F32 = jnp.float32


def req_perm(move):
    pairs = []
    for i in range(N_REQ):
        z, x, yl = move(i // 8, (i // 2) % 4, i % 2)
        pairs.append((i, (z % 4) * 8 + (x % 4) * 2 + yl % 2))
    return pairs


def from_z(d):
    return req_perm(lambda z, x, yl: (z - d, x, yl))


def from_x(d):
    return req_perm(lambda z, x, yl: (z, x - d, yl))


def rolled(rel, pos):
    odd = (pos & 1) == 1
    high = (pos & 2) == 2
    step = [jnp.where(odd, rel[(i - 1) % 4], rel[i]) for i in range(4)]
    return [jnp.where(high, step[(i - 2) % 4], step[i]) for i in range(4)]


def ring_small(own, source, pos):
    rel = [own] + [lax.ppermute(own, "req", source(d)) for d in (1, 2, 3)]
    return rolled(rel, pos)


def ring_big(blocks, source):
    plus = [lax.ppermute(b, "req", source(1)) for b in blocks]
    minus = [lax.ppermute(b, "req", source(3)) for b in blocks[::-1]][::-1]
    far = [
        lax.ppermute(plus[0], "req", source(1)),
        lax.ppermute(minus[1], "req", source(3)),
    ]
    return [list(blocks), plus, far, minus]


def gather_columns(matrices, place):
    h, z, x, yl = place
    nm = len(matrices)
    stacked = jnp.stack([m.astype(BF) for m in matrices])
    rows, width = stacked.shape[1], stacked.shape[2] // N_HEAD
    recv = {}
    for dh in range(4):
        part = lax.dynamic_slice_in_dim(stacked, (h ^ dh) * width, width, 2)
        for dy in range(2):
            if dh == 0 and dy == 0:
                recv[dh, dy] = part
                continue
            pairs = [
                (a * N_REQ + q, (a ^ dh) * N_REQ + (q ^ dy))
                for a in range(N_HEAD)
                for q in range(N_REQ)
            ]
            recv[dh, dy] = lax.ppermute(part, ("head", "req"), pairs)
    both = []
    for dh in range(4):
        a, b = recv[dh, 0], recv[dh, 1]
        first = yl == 0
        both.append(jnp.stack([jnp.where(first, a, b), jnp.where(first, b, a)], axis=1))
    odd, high = (h & 1) == 1, (h & 2) == 2
    step = [jnp.where(odd, both[i ^ 1], both[i]) for i in range(4)]
    held = [jnp.where(high, step[i ^ 2], step[i]) for i in range(4)]
    first_half = jnp.stack(held[:2], axis=1)
    second_half = jnp.stack(held[2:], axis=1)
    along_x = ring_small(first_half, from_x, x)
    along_z = ring_small(second_half, from_z, z)

    def regroup(parts, b):
        return jnp.stack([p[:, b] for p in parts], axis=1).reshape(nm, 4, 2 * rows, width)

    a_rel = ring_big([regroup(along_x, b) for b in range(2)], from_z)
    b_rel = ring_big([regroup(along_z, b) for b in range(2)], from_x)
    return [a_rel[d][b] for d in range(4) for b in range(2)] + [
        b_rel[d][b] for d in range(4) for b in range(2)
    ]


def weight_copies(pieces, m, place_ref, buf, sem):
    z, x = place_ref[1], place_ref[2]
    out = []
    for d in range(4):
        for b in range(2):
            zd = lax.rem(z + d, 4)
            xd = lax.rem(x + d, 4)
            out.append(pltpu.make_async_copy(pieces[2 * d + b].at[m], buf.at[b * 4 + zd], sem))
            out.append(
                pltpu.make_async_copy(
                    pieces[8 + 2 * d + b].at[m],
                    buf.at[pl.ds((2 + b) * 4, 4), xd],
                    sem,
                )
            )
    return out


def project_kernel(place_ref, *refs, first, count, gated):
    xs, pieces = refs[:4], refs[4:20]
    rest = refs[20:]
    if gated:
        pre_ref, rest = rest[0], rest[1:]
    out_ref, buf, sem = rest
    i, j = pl.program_id(0), pl.program_id(1)

    def start(m, slot):
        for copy in weight_copies(pieces, m, place_ref, buf.at[slot], sem.at[slot]):
            copy.start()

    @pl.when(jnp.logical_and(i == 0, j == 0))
    def _():
        start(first, 0)

    slot = lax.rem(i, 2)

    @pl.when(j == 0)
    def _():
        if count > 1:

            @pl.when(i + 1 < count)
            def _():
                start(first + i + 1, 1 - slot)

        pltpu.make_async_copy(buf.at[slot], buf.at[slot], sem.at[slot]).wait()

    h = place_ref[0]
    total = None
    for d in range(4):
        block = h ^ d
        w = buf[slot, pl.ds(block * 4, 4)].reshape(512, 512)
        term = jnp.dot(xs[d][0], w, preferred_element_type=F32)
        total = term if total is None else total + term
    if gated:
        gate = total / (1.0 + jnp.exp(-total))
        total = gate * pre_ref[...].astype(F32)
        out_ref[...] = total.astype(out_ref.dtype)
    else:
        out_ref[0] = total.astype(out_ref.dtype)


def project_pieces(place, xs, pieces, first, count, x_first, tile, pre=None):
    rows = xs[0].shape[1]
    gated = pre is not None
    any_spec = pl.BlockSpec(memory_space=pl.ANY)
    x_spec = pl.BlockSpec((1, tile, 512), lambda i, j, s: (i + x_first, j, 0))
    if gated:
        out_shape = jax.ShapeDtypeStruct((rows, 512), BF)
        out_spec = pl.BlockSpec((tile, 512), lambda i, j, s: (j, 0))
        extra = [pl.BlockSpec((tile, 512), lambda i, j, s: (j, 0))]
        extra_args = [pre]
    else:
        out_shape = jax.ShapeDtypeStruct((count, rows, 512), BF)
        out_spec = pl.BlockSpec((1, tile, 512), lambda i, j, s: (i, j, 0))
        extra, extra_args = [], []
    return pl.pallas_call(
        functools.partial(project_kernel, first=first, count=count, gated=gated),
        out_shape=out_shape,
        grid_spec=pltpu.PrefetchScalarGridSpec(
            num_scalar_prefetch=1,
            grid=(count, rows // tile),
            in_specs=[x_spec] * 4 + [any_spec] * 16 + extra,
            out_specs=out_spec,
            scratch_shapes=[
                pltpu.VMEM((min(count, 2), 16, 4, 32, 512), BF),
                pltpu.SemaphoreType.DMA((min(count, 2),)),
            ],
        ),
        compiler_params=pltpu.CompilerParams(
            dimension_semantics=("arbitrary", "arbitrary"), vmem_limit_bytes=40 << 20
        ),
        name="project",
    )(place, *xs, *pieces, *extra_args)


def span_tables():
    t = np.arange(CH)
    blocks = []
    size = 4
    while size <= CH:
        start = (t // size) * size
        mid = start + size // 2
        m = np.zeros((CH, CH), np.float32)
        for i in range(CH):
            if i >= mid[i]:
                m[i, mid[i] : i] = 1.0
            else:
                m[i, i + 1 : mid[i]] = 1.0
        blocks.append(m)
        size *= 2
    before = (t[None, :] < t[:, None]).astype(np.float32)
    after = (t[None, :] > t[:, None]).astype(np.float32)
    whole = np.ones((8, CH), np.float32)
    table = np.concatenate(blocks + [before, after, whole])
    return np.concatenate([table, table], axis=1)


LEVELS = int(np.log2(CH))


def wkv_kernel(
    count_ref, table_ref, r_ref, k_ref, v_ref, w_ref, vec_ref, start_ref, out_ref, state_ref, *, prompts, t0
):
    c = pl.program_id(0)

    @pl.when(c == 0)
    def _():
        state_ref[...] = start_ref[...]

    table = table_ref[...]
    row = lax.broadcasted_iota(jnp.int32, (CH, 512), 0)
    lane = lax.broadcasted_iota(jnp.int32, (CH, 128), 1)
    low = lane < 64
    arow = lax.broadcasted_iota(jnp.int32, (CH, 2 * CH), 0)
    acol = lax.broadcasted_iota(jnp.int32, (CH, 2 * CH), 1) & (CH - 1)
    diff = arow ^ acol
    causal = arow > acol
    srow = lax.broadcasted_iota(jnp.int32, (128, 128), 0) < 64
    scol = lax.broadcasted_iota(jnp.int32, (128, 128), 1) < 64
    same_head = srow == scol
    mean_of = jnp.where(same_head, 1.0 / 64, 0.0).astype(BF)
    mean_two = jnp.concatenate([mean_of, mean_of], axis=0)
    reward, scale, offset = vec_ref[0:1], vec_ref[1:2], vec_ref[2:3]
    contract_lanes = (((1,), (1,)), ((), ()))
    contract_rows = (((0,), (0,)), ((), ()))

    def both_heads(a):
        zero = jnp.zeros_like(a)
        return jnp.concatenate([jnp.where(low, a, zero), jnp.where(low, zero, a)], axis=0)

    for p in range(prompts):
        live = (row + (c * CH + t0)) < count_ref[p]
        r = r_ref[0, p].astype(F32)
        k = jnp.where(live, k_ref[0, p].astype(F32), 0.0)
        v = v_ref[0, p]
        w = w_ref[p]
        w_hi = w.astype(BF)
        w_lo = (w - w_hi.astype(F32)).astype(BF)
        sums = jnp.dot(table, jnp.concatenate([w_hi, w_lo], axis=0), preferred_element_type=F32)
        factors = jnp.exp(sums)
        r_dec = (r * factors[(LEVELS - 1) * CH : LEVELS * CH]).astype(BF)
        k_dec = (k * factors[LEVELS * CH : (LEVELS + 1) * CH]).astype(BF)
        whole = factors[(LEVELS + 1) * CH : (LEVELS + 1) * CH + 1]
        r_own = r * reward
        r_hi = r_own.astype(BF)
        r_lo = (r_own - r_hi.astype(F32)).astype(BF)
        k_bf = k.astype(BF)
        mixed = [jnp.where((row & 1) == 1, r, k).astype(BF)]
        for level in range(1, LEVELS):
            pick = jnp.where((row & (1 << level)) != 0, r, k)
            mixed.append((pick * factors[(level - 1) * CH : level * CH]).astype(BF))
        for q in range(4):
            cols = slice(128 * q, 128 * q + 128)
            keys = both_heads(k_bf[:, cols])
            scores = lax.dot_general(
                jnp.concatenate([r_hi[:, cols], r_lo[:, cols]], axis=1),
                jnp.concatenate([keys, keys], axis=1),
                contract_lanes,
                preferred_element_type=F32,
            )
            scores = jnp.where(diff == 0, scores, 0.0)
            for level in range(LEVELS):
                a = mixed[level][:, cols]
                s = lax.dot_general(a, both_heads(a), contract_lanes, preferred_element_type=F32)
                here = jnp.logical_and(causal, (diff >> level) == 1)
                scores = jnp.where(here, s, scores)
            vq = v[:, cols]
            state = state_ref[p, q]
            y = jnp.dot(scores.astype(BF), both_heads(vq), preferred_element_type=F32)
            y = y + lax.dot_general(
                r_dec[:, cols], state.astype(BF), contract_lanes, preferred_element_type=F32
            )
            added = lax.dot_general(vq, k_dec[:, cols], contract_rows, preferred_element_type=F32)
            state_ref[p, q] = state * whole[:, cols] + jnp.where(same_head, added, 0.0)
            y_hi = y.astype(BF)
            y_lo = (y - y_hi.astype(F32)).astype(BF)
            mean = jnp.dot(
                jnp.concatenate([y_hi, y_lo], axis=1), mean_two, preferred_element_type=F32
            )
            center = y - mean
            spread = jnp.dot((center * center).astype(BF), mean_of, preferred_element_type=F32)
            normed = center * lax.rsqrt(spread + NORM_EPS)
            out_ref[p, :, cols] = (normed * scale[:, cols] + offset[:, cols]).astype(out_ref.dtype)


def wkv(counts, rkv, log_decay, vectors, start, t0, t1):
    prompts = rkv.shape[1]
    table = jnp.asarray(span_tables(), BF)
    c0 = t0 // CH

    def part(n):
        return pl.BlockSpec((1, prompts, CH, 512), lambda c, s: (n, 0, c + c0, 0))

    return pl.pallas_call(
        functools.partial(wkv_kernel, prompts=prompts, t0=t0),
        out_shape=(
            jax.ShapeDtypeStruct((prompts, t1 - t0, 512), BF),
            jax.ShapeDtypeStruct((prompts, 4, 128, 128), F32),
        ),
        grid_spec=pltpu.PrefetchScalarGridSpec(
            num_scalar_prefetch=1,
            grid=((t1 - t0) // CH,),
            in_specs=[
                pl.BlockSpec(table.shape, lambda c, s: (0, 0)),
                part(0),
                part(1),
                part(2),
                pl.BlockSpec((prompts, CH, 512), lambda c, s: (0, c + c0, 0)),
                pl.BlockSpec((8, 512), lambda c, s: (0, 0)),
                pl.BlockSpec((prompts, 4, 128, 128), lambda c, s: (0, 0, 0, 0)),
            ],
            out_specs=(
                pl.BlockSpec((prompts, CH, 512), lambda c, s: (0, c, 0)),
                pl.BlockSpec((prompts, 4, 128, 128), lambda c, s: (0, 0, 0, 0)),
            ),
        ),
        compiler_params=pltpu.CompilerParams(
            dimension_semantics=("arbitrary",), vmem_limit_bytes=40 << 20
        ),
        name="wkv",
    )(counts, table, rkv, rkv, rkv, log_decay, vectors, start)


def states_of(packed):
    prompts = packed.shape[0]
    even = packed[:, :, :64, :64]
    odd = packed[:, :, 64:, 64:]
    return jnp.stack([even, odd], axis=2).reshape(prompts, 8, 64, 64).swapaxes(2, 3)


def on_device(
    learner_acceptance_matrix,
    learner_address_matrix,
    learner_content_matrix,
    learner_gating_matrix,
    learner_result_matrix,
    fading_narrowing_matrix,
    fading_widening_matrix,
    feature_fading_speed,
    current_reward,
    symbol_blending_factors,
    group_scaling_factor,
    group_scaling_offset,
    request_hidden_entries,
    request_valid_count,
    request_destination_place,
    newest_symbol_hidden,
    preceding_hidden_entry,
    place_memory_matrix,
    place_newness_marks,
):
    h = lax.axis_index("head")
    req = lax.axis_index("req")
    z, x, yl = req // 8, (req // 2) % 4, req % 2
    spot = (h, z, x, yl)
    place = jnp.stack([h, z, x, yl]).astype(jnp.int32)
    prompts, length, width = request_hidden_entries.shape
    slots, groups, breadth = place_memory_matrix.shape[:3]
    tokens = prompts * length
    rows = tokens + slots
    fresh = place_newness_marks == 1

    pieces = gather_columns(
        [learner_acceptance_matrix, learner_address_matrix, learner_content_matrix], spot
    )
    late_pieces = gather_columns([learner_gating_matrix, learner_result_matrix], spot)

    prior = jnp.where(fresh[:, None], jnp.zeros_like(preceding_hidden_entry), preceding_hidden_entry)
    own = jnp.concatenate(
        [request_hidden_entries.reshape(tokens, width), newest_symbol_hidden, prior], axis=0
    )
    yh_swap = [(i, i ^ 2) for i in range(4)]
    core_swap = [(i, i ^ 1) for i in range(4)]
    far = lax.ppermute(own, "head", yh_swap)
    side = lax.ppermute(own, "head", core_swap)
    far_side = lax.ppermute(far, "head", core_swap)
    blocks = [own, side, far, far_side]

    xs, low = [], None
    for d in range(4):
        at = (h ^ d) * width
        mu = lax.dynamic_slice_in_dim(symbol_blending_factors, at, width, 1)
        seq = blocks[d][:tokens].reshape(prompts, length, width)
        current = blocks[d][:rows].astype(F32)
        before = jnp.concatenate([jnp.zeros_like(seq[:, :1]), seq[:, :-1]], axis=1)
        previous = jnp.concatenate([before.reshape(tokens, width), blocks[d][rows:]], axis=0)
        step = previous.astype(F32) - current
        mixed = (current[None] + step[None] * mu[:, None, :]).astype(BF)
        xs.append(mixed)
        narrow = lax.dynamic_slice_in_dim(fading_narrowing_matrix, at, width, 0)
        term = jnp.dot(mixed[3], narrow, preferred_element_type=F32)
        low = term if low is None else low + term
    lowrank = jnp.tanh(low).astype(BF)
    log_decay = -feature_fading_speed * jnp.exp(
        jnp.dot(lowrank, fading_widening_matrix, preferred_element_type=F32)
    )
    positions = lax.broadcasted_iota(jnp.int32, (prompts, length), 1)
    live = (positions < request_valid_count[:, None]).astype(F32)
    prompt_decay = log_decay[:tokens].reshape(prompts, length, width) * live[..., None]

    rkv = project_pieces(place, xs, pieces, 0, 3, 0, rows // 4)

    vectors = jnp.concatenate(
        [
            jnp.stack([current_reward, group_scaling_factor, group_scaling_offset]),
            jnp.zeros((5, width), F32),
        ]
    )
    start = jnp.zeros((prompts, groups // 2, 128, 128), F32)
    sequences = rkv[:, :tokens].reshape(3, prompts, length, width)
    pre, packed = wkv(request_valid_count, sequences, prompt_decay, vectors, start, 0, length)
    final_state = states_of(packed)

    one = rkv[:, tokens:].astype(F32).reshape(3, slots, groups, breadth)
    r_d, k_d, v_d = one[0], one[1], one[2]
    decay_d = jnp.exp(log_decay[tokens:]).reshape(slots, groups, breadth)
    reward = current_reward.reshape(groups, breadth)
    begin = jnp.where(fresh[:, None, None, None], 0.0, place_memory_matrix)
    y_d = (
        jnp.sum(r_d[..., None] * begin, axis=2)
        + jnp.sum(r_d * reward * k_d, axis=-1, keepdims=True) * v_d
    )
    next_state = decay_d[..., None] * begin + k_d[..., None] * v_d[..., None, :]
    center = y_d - jnp.mean(y_d, axis=-1, keepdims=True)
    spread = jnp.mean(center * center, axis=-1, keepdims=True)
    pre_d = (center / jnp.sqrt(spread + NORM_EPS)).reshape(slots, width)
    pre_d = pre_d * group_scaling_factor + group_scaling_offset

    pre_all = jnp.concatenate([pre.reshape(tokens, width), pre_d.astype(BF)], axis=0)
    normed = project_pieces(place, xs, late_pieces, 0, 1, 4, rows // 4, pre=pre_all)
    normed_far = lax.ppermute(normed, "head", yh_swap)
    normed_side = lax.ppermute(normed, "head", core_swap)
    normed_far_side = lax.ppermute(normed_far, "head", core_swap)
    parts = [a[None] for a in (normed, normed_side, normed_far, normed_far_side)]
    result = project_pieces(place, parts, late_pieces, 1, 1, 0, rows // 4)[0]

    prompt_hidden = (
        result[:tokens].reshape(prompts, length, width) * live[..., None].astype(BF)
    )
    select = (positions == request_valid_count[:, None] - 1).astype(F32)
    last_tokens = jnp.sum(
        request_hidden_entries.astype(F32) * select[..., None], axis=1
    ).astype(BF)
    offsets = request_destination_place - req * slots
    slot_ids = lax.broadcasted_iota(jnp.int32, (slots,), 0)
    new_state = next_state
    new_shift = newest_symbol_hidden
    taken = jnp.zeros((slots,), jnp.bool_)
    for n in range(prompts):
        hit = slot_ids == offsets[n]
        new_state = jnp.where(hit[:, None, None, None], final_state[n], new_state)
        new_shift = jnp.where(hit[:, None], last_tokens[n], new_shift)
        taken = taken | hit
    decode_hidden = jnp.where(taken[:, None], jnp.zeros((), BF), result[tokens:])
    return (prompt_hidden, decode_hidden, new_state, new_shift)


def solution(mesh):
    in_specs = (
        P(("head", "req"), None),
        P(("head", "req"), None),
        P(("head", "req"), None),
        P(("head", "req"), None),
        P(("head", "req"), None),
        P(),
        P(None, "head"),
        P("head"),
        P("head"),
        P(),
        P("head"),
        P("head"),
        P("req", None, "head"),
        P("req"),
        P("req"),
        P("req", "head"),
        P("req", "head"),
        P("req", "head", None, None),
        P("req"),
    )
    out_specs = (
        P("req", None, "head"),
        P("req", "head"),
        P("req", "head", None, None),
        P("req", "head"),
    )
    return jax.shard_map(
        on_device, mesh=mesh, in_specs=in_specs, out_specs=out_specs, check_vma=False
    )
```

```python
import functools

import jax
import jax.numpy as jnp
import numpy as np
from jax import lax
from jax.experimental import pallas as pl
from jax.experimental.pallas import tpu as pltpu
from jax.sharding import Mesh
from jax.sharding import PartitionSpec as P

NORM_EPS = 0.00064
N_HEAD = 4
CH = 64
BF = jnp.bfloat16
F32 = jnp.float32


STEPS = (("x", 1), ("z", 1), ("x", 3), ("z", 3))


def swap(a, axes, bits):
    sizes = {"x": 4, "z": 4, "yl": 2, "head": 4}
    names = ("yh", "core") if axes == "head" else axes
    return lax.ppermute(a, names, [(i, i ^ bits) for i in range(sizes[axes])])


def order_of(part):
    return [STEPS[(part + n) % 4] for n in range(4)]


def after(value, other):
    return lax.optimization_barrier((value, other))[0]


def column_blocks(matrices, h):
    stacked = jnp.stack([m.astype(BF) for m in matrices])
    width = stacked.shape[2] // N_HEAD
    parts = [lax.dynamic_slice_in_dim(stacked, (h ^ d) * width, width, 2) for d in range(4)]
    return [parts[0]] + [swap(parts[d], "head", d) for d in (1, 2, 3)]


def with_neighbour(own, yl):
    other = swap(own, "yl", 1)
    first = yl == 0
    return jnp.concatenate(
        [jnp.where(first, own, other), jnp.where(first, other, own)], axis=-2
    )


ANY = pl.BlockSpec(memory_space=pl.ANY)


def cost(flops, nbytes, trans=0):
    return pl.CostEstimate(flops=flops, bytes_accessed=nbytes, transcendentals=trans)


def params(axes):
    return pltpu.CompilerParams(
        dimension_semantics=("arbitrary",) * axes, vmem_limit_bytes=48 << 20
    )


def axis_dim(axis):
    return 0 if axis == "z" else 1


def places(p, n, place_ref):
    axis, bits = order_of(p)[n]
    pos = place_ref[1] if axis == "z" else place_ref[2]
    seen = [b for name, b in order_of(p)[:n] if name == axis]
    offsets = [0] + seen
    return [pos ^ o for o in offsets], [pos ^ bits ^ o for o in offsets]


def part_of(ref, dim, i, lot):
    return ref.at[i, :, lot] if dim == 0 else ref.at[:, i, lot]


def pack_kernel(place_ref, *refs, n, lot):
    owns, recvs, outs, sem = refs[:4], refs[4:8], refs[8:12], refs[12]
    copies = []
    for p in range(4):
        dim = axis_dim(order_of(p)[n][0])
        own_at, recv_at = places(p, n, place_ref)
        if len(own_at) == 1:
            own_at, recv_at = [0], [1]
        for src, at in ((owns[p], own_at), (recvs[p], recv_at)):
            for i, j in enumerate(at):
                source = part_of(src, dim, i, lot)
                target = part_of(outs[p], dim, j, slice(None))
                copies.append(pltpu.make_async_copy(source, target, sem.at[len(copies)]))
    for copy in copies:
        copy.start()
    for copy in copies:
        copy.wait()


def pack(place, owns, recvs, n, lot):
    shapes = []
    for p in range(4):
        shape = list(owns[p].shape)
        shape[axis_dim(order_of(p)[n][0])] *= 2
        shape[2] = lot.stop - lot.start
        shapes.append(jax.ShapeDtypeStruct(tuple(shape), BF))
    return pl.pallas_call(
        functools.partial(pack_kernel, n=n, lot=lot),
        out_shape=shapes,
        grid_spec=pltpu.PrefetchScalarGridSpec(
            num_scalar_prefetch=1,
            grid=(1,),
            in_specs=[ANY] * 8,
            out_specs=[pl.BlockSpec(a.shape, lambda i, s: (0, 0, 0, 0, 0)) for a in shapes],
            scratch_shapes=[pltpu.SemaphoreType.DMA((16,))],
        ),
        compiler_params=params(1),
        cost_estimate=cost(0, 8 << 20),
        name="pack",
    )(place, *owns, *recvs)


def swap_all(owns, n):
    return [swap(owns[p], *order_of(p)[n]) for p in range(4)]


def copy_weights(pieces, m, place_ref, buf, sem):
    for p in range(4):
        dim = axis_dim(order_of(p)[3][0])
        own_at, recv_at = places(p, 3, place_ref)
        for src, at in ((pieces[p], own_at), (pieces[p + 4], recv_at)):
            for i, j in enumerate(at):
                target = buf.at[p * 4 + j] if dim == 0 else buf.at[pl.ds(p * 4, 4), j]
                pltpu.make_async_copy(part_of(src, dim, i, m), target, sem).start()


def wait_weights(buf, sem):
    pltpu.make_async_copy(buf, buf, sem).wait()


def mix_kernel(place_ref, count_ref, *refs, d, length):
    hid_ref, mu_ref, narrow_ref = refs[:3]
    refs = refs[3:]
    if d > 0:
        low_in, refs = refs[0], refs[2:]
    if d == 3:
        widen_ref, speed_ref, refs = refs[0], refs[1], refs[2:]
    x_ref, low_ref, cur_ref, step_ref = refs
    i = pl.program_id(0)
    rows = cur_ref.shape[0]
    slots = hid_ref.shape[0] - rows
    tokens = rows - slots

    @pl.when(i == 0)
    def _():
        cur = hid_ref[:rows].astype(F32)
        cur_ref[...] = cur
        seq = cur[:tokens]
        at = lax.broadcasted_iota(jnp.int32, seq.shape, 0)
        before = jnp.where((at & (length - 1)) == 0, 0.0, pltpu.roll(seq, 1, 0))
        step_ref[:tokens] = before - seq
        step_ref[tokens:] = hid_ref[rows:].astype(F32) - cur[tokens:]

    mixed = (cur_ref[...] + step_ref[...] * mu_ref[pl.ds(i, 1), :]).astype(BF)
    x_ref[0] = mixed

    @pl.when(i == 3)
    def _():
        low = jnp.dot(mixed, narrow_ref[...], preferred_element_type=F32)
        if d > 0:
            low = low + low_in[...]
        if d < 3:
            low_ref[...] = low
        else:
            lowrank = jnp.tanh(low).astype(BF)
            rate = jnp.exp(jnp.dot(lowrank, widen_ref[...], preferred_element_type=F32))
            log_decay = -speed_ref[...] * rate
            at = lax.broadcasted_iota(jnp.int32, (rows, 512), 0)
            limit = jnp.where(
                at < length,
                count_ref[0],
                jnp.where(at < 2 * length, count_ref[1] + length, rows),
            )
            low_ref[...] = jnp.where(at < limit, log_decay, 0.0)


def mix(place, counts, hidden, d, mu, narrow, low, held, widen, speed, slots, length):
    rows = hidden.shape[0] - slots
    once = lambda i, s, c: (0, 0)
    args = [hidden, mu, narrow]
    specs = [
        pl.BlockSpec(hidden.shape, once),
        pl.BlockSpec((5, 512), lambda i, s, c: (0, s[0] ^ d)),
        pl.BlockSpec((512, 64), lambda i, s, c: (s[0] ^ d, 0)),
    ]
    alias = {}
    if d > 0:
        args += [low, held]
        specs += [pl.BlockSpec(low.shape, once), ANY]
        alias = {6: 0}
    wide = 64
    if d == 3:
        args += [widen, speed]
        specs += [pl.BlockSpec(widen.shape, once), pl.BlockSpec(speed.shape, once)]
        wide = 512
    return pl.pallas_call(
        functools.partial(mix_kernel, d=d, length=length),
        out_shape=(
            jax.ShapeDtypeStruct((5, rows, 2048), BF),
            jax.ShapeDtypeStruct((rows, wide), F32),
        ),
        grid_spec=pltpu.PrefetchScalarGridSpec(
            num_scalar_prefetch=2,
            grid=(5,),
            in_specs=specs,
            out_specs=(
                pl.BlockSpec((1, rows, 512), lambda i, s, c: (i, 0, d)),
                pl.BlockSpec((rows, wide), once),
            ),
            scratch_shapes=[pltpu.VMEM((rows, 512), F32), pltpu.VMEM((rows, 512), F32)],
        ),
        input_output_aliases=alias,
        compiler_params=params(1),
        cost_estimate=cost(20 * rows * 512, 12 * rows * 512),
        name="mix",
    )(place, counts, *args)


def rkv_kernel(place_ref, x_ref, *refs):
    pieces = refs[:8]
    out_ref, buf, sem = refs[8:]
    i, j = pl.program_id(0), pl.program_id(1)
    slot = lax.rem(i, 2)

    @pl.when(jnp.logical_and(i == 0, j == 0))
    def _():
        copy_weights(pieces, 0, place_ref, buf.at[0], sem.at[0])

    @pl.when(j == 0)
    def _():
        @pl.when(i < 2)
        def _():
            copy_weights(pieces, i + 1, place_ref, buf.at[1 - slot], sem.at[1 - slot])

        wait_weights(buf.at[slot], sem.at[slot])

    w = buf[slot].reshape(2048, 512)
    out_ref[0] = jnp.dot(x_ref[0], w, preferred_element_type=F32).astype(out_ref.dtype)


def project_rkv(place, mixed, pieces, tile):
    rows = mixed.shape[1]
    return pl.pallas_call(
        rkv_kernel,
        out_shape=jax.ShapeDtypeStruct((3, rows, 512), BF),
        grid_spec=pltpu.PrefetchScalarGridSpec(
            num_scalar_prefetch=1,
            grid=(3, rows // tile),
            in_specs=[pl.BlockSpec((1, tile, 2048), lambda i, j, s: (i, j, 0))] + [ANY] * 8,
            out_specs=pl.BlockSpec((1, tile, 512), lambda i, j, s: (i, j, 0)),
            scratch_shapes=[
                pltpu.VMEM((2, 16, 4, 32, 512), BF),
                pltpu.SemaphoreType.DMA((2,)),
            ],
        ),
        compiler_params=params(2),
        cost_estimate=cost(6 * rows * 2048 * 512, 24 << 20),
        name="project_rkv",
    )(place, mixed, *pieces)


def gate_kernel(place_ref, x_ref, *refs):
    pieces = refs[:8]
    out_ref, buf, sem = refs[8:]

    @pl.when(pl.program_id(0) == 0)
    def _():
        copy_weights(pieces, 0, place_ref, buf, sem)
        wait_weights(buf, sem)

    total = jnp.dot(x_ref[0], buf[...].reshape(2048, 512), preferred_element_type=F32)
    out_ref[...] = (total / (1.0 + jnp.exp(-total))).astype(out_ref.dtype)


def project_gate(place, mixed, pieces, tile):
    rows = mixed.shape[1]
    return pl.pallas_call(
        gate_kernel,
        out_shape=jax.ShapeDtypeStruct((rows, 512), BF),
        grid_spec=pltpu.PrefetchScalarGridSpec(
            num_scalar_prefetch=1,
            grid=(rows // tile,),
            in_specs=[pl.BlockSpec((1, tile, 2048), lambda j, s: (4, j, 0))] + [ANY] * 8,
            out_specs=pl.BlockSpec((tile, 512), lambda j, s: (j, 0)),
            scratch_shapes=[pltpu.VMEM((16, 4, 32, 512), BF), pltpu.SemaphoreType.DMA(())],
        ),
        compiler_params=params(1),
        cost_estimate=cost(2 * rows * 2048 * 512, 8 << 20),
        name="project_gate",
    )(place, mixed, *pieces)


def result_kernel(place_ref, count_ref, *refs, spans, t0, decode, chained):
    lots = len(spans)
    xs, pieces = refs[: 4 * lots], refs[4 * lots : 4 * lots + 8]
    rest = refs[4 * lots + 8 + (1 if chained else 0) :]
    out_ref, rest = rest[0], rest[1:]
    if decode:
        decode_ref, rest = rest[0], rest[1:]
    buf, sem = rest
    copy_weights(pieces, 1, place_ref, buf, sem)
    wait_weights(buf, sem)
    start = 0
    for lot, span in enumerate(spans):
        total = None
        for d in range(4):
            w = buf[4 * d : 4 * d + 4].reshape(512, 512)
            term = jnp.dot(xs[4 * lot + d][...], w, preferred_element_type=F32)
            total = term if total is None else total + term
        at = lax.broadcasted_iota(jnp.int32, (span, 512), 0) + (t0 + start)
        for p in range(2):
            own = jnp.where(at < count_ref[p], total[p * span : (p + 1) * span], 0.0)
            out_ref[p, start : start + span] = own.astype(out_ref.dtype)
        start += span
        if decode:
            decode_ref[...] = total[2 * span :].astype(decode_ref.dtype)


def project_result(place, counts, xs, pieces, spans, t0, decode, earlier, length):
    rows = xs[0].shape[0]
    span = sum(spans)
    once = lambda i, s, c: (0, 0)
    out_shape = [jax.ShapeDtypeStruct((2, length, 512), BF)]
    out_specs = [pl.BlockSpec((2, span, 512), lambda i, s, c: (0, t0 // span, 0))]
    if decode:
        out_shape.append(jax.ShapeDtypeStruct((rows - 2 * span, 512), BF))
        out_specs.append(pl.BlockSpec((rows - 2 * span, 512), once))
    chained = earlier is not None
    return pl.pallas_call(
        functools.partial(result_kernel, spans=spans, t0=t0, decode=decode, chained=chained),
        out_shape=out_shape,
        grid_spec=pltpu.PrefetchScalarGridSpec(
            num_scalar_prefetch=2,
            grid=(1,),
            in_specs=[pl.BlockSpec(a.shape, once) for a in xs] + [ANY] * (9 if chained else 8),
            out_specs=out_specs,
            scratch_shapes=[pltpu.VMEM((16, 4, 32, 512), BF), pltpu.SemaphoreType.DMA(())],
        ),
        input_output_aliases={2 + len(xs) + 8: 0} if chained else {},
        compiler_params=params(1),
        cost_estimate=cost(4 * span * 2048 * 512, 8 << 20),
        name="project_result",
    )(place, counts, *xs, *pieces, *([earlier] if chained else []))


SLOT_BLOCK = 16


def head_mask(value):
    row = lax.broadcasted_iota(jnp.int32, (128, 128), 0) < 64
    col = lax.broadcasted_iota(jnp.int32, (128, 128), 1) < 64
    return jnp.where(row == col, value, 0.0).astype(BF)


def in_two(a):
    hi = a.astype(BF)
    return jnp.concatenate([hi, (a - hi.astype(F32)).astype(BF)], axis=1)


def decode_kernel(
    keep_ref, s_ref, r_ref, k_ref, v_ref, w_ref, g_ref, vec_ref,
    state_ref, out_ref, rt_ref, kt_ref, dt_ref, y_ref,
):
    g = pl.program_id(0)

    @pl.when(g == 0)
    def _():
        r = r_ref[0].astype(F32)
        k = k_ref[0].astype(F32)
        decay = jnp.exp(w_ref[...])
        for q in range(4):
            cols = slice(128 * q, 128 * q + 128)

            def turned(a):
                t = jnp.transpose(a[:, cols])
                return jnp.concatenate([t[:64], t[64:]], axis=1)

            rt_ref[q] = turned(r).astype(BF)
            kt_ref[q] = turned(k).astype(BF)
            dt_ref[q] = in_two(turned(decay))

    here = pl.ds(pl.multiple_of(g * SLOT_BLOCK, SLOT_BLOCK), SLOT_BLOCK)
    v = v_ref[0, here].astype(F32)
    row = lax.broadcasted_iota(jnp.int32, (128, 128), 0)
    low = lax.broadcasted_iota(jnp.int32, (128, 128), 1) < 64
    for s in range(SLOT_BLOCK):
        slot = g * SLOT_BLOCK + s
        hit = row == jnp.where(low, slot, slot + 64)
        pick = jnp.where(hit, 1.0, 0.0).astype(BF)
        kept = jnp.where(hit, keep_ref[slot].astype(F32), 0.0).astype(BF)
        r_b = jnp.dot(rt_ref[...].reshape(256, 128), kept, preferred_element_type=F32)
        k_b = jnp.dot(kt_ref[...].reshape(256, 128), pick, preferred_element_type=F32)
        d_b = jnp.dot(
            dt_ref[...].reshape(256, 256),
            jnp.concatenate([kept, kept], axis=0),
            preferred_element_type=F32,
        )
        for q in range(4):
            span = slice(64 * q, 64 * q + 64)
            cols = slice(128 * q, 128 * q + 128)
            state = jnp.concatenate([s_ref[s, 2 * q], s_ref[s, 2 * q + 1]], axis=1)
            after_it = d_b[span] * state + k_b[span] * v[s : s + 1, cols]
            state_ref[s, 2 * q] = after_it[:, :64]
            state_ref[s, 2 * q + 1] = after_it[:, 64:]
            y_ref[s : s + 1, cols] = jnp.sum(r_b[span] * state, axis=0, keepdims=True)
    r = r_ref[0, here].astype(F32)
    k = k_ref[0, here].astype(F32)
    reward, scale, offset = vec_ref[0:1], vec_ref[1:2], vec_ref[2:3]
    own = r * reward * k
    ones = jnp.concatenate([head_mask(1.0)] * 2, axis=0)
    mean_of = jnp.concatenate([head_mask(1.0 / 64)] * 2, axis=0)
    for q in range(4):
        cols = slice(128 * q, 128 * q + 128)
        total = jnp.dot(in_two(own[:, cols]), ones, preferred_element_type=F32)
        y = y_ref[:, cols] + total * v[:, cols]
        center = y - jnp.dot(in_two(y), mean_of, preferred_element_type=F32)
        spread = jnp.dot(in_two(center * center), mean_of, preferred_element_type=F32)
        normed = center * lax.rsqrt(spread + NORM_EPS) * scale[:, cols] + offset[:, cols]
        out_ref[:, cols] = (normed * g_ref[here, cols].astype(F32)).astype(out_ref.dtype)


def decode_step(states, keep, rkv, log_decay, gate, vectors):
    slots = states.shape[0]
    at = rkv.shape[1] // slots - 1

    def part(n):
        return pl.BlockSpec((1, slots, 512), lambda g, s: (n, at, 0))

    flat = pl.BlockSpec((slots, 512), lambda g, s: (at, 0))
    big = pl.BlockSpec((SLOT_BLOCK, 8, 64, 64), lambda g, s: (g, 0, 0, 0))
    return pl.pallas_call(
        decode_kernel,
        out_shape=(
            jax.ShapeDtypeStruct(states.shape, F32),
            jax.ShapeDtypeStruct((slots, 512), BF),
        ),
        grid_spec=pltpu.PrefetchScalarGridSpec(
            num_scalar_prefetch=1,
            grid=(slots // SLOT_BLOCK,),
            in_specs=[big, part(0), part(1), part(2), flat, flat]
            + [pl.BlockSpec((8, 512), lambda g, s: (0, 0))],
            out_specs=(big, pl.BlockSpec((SLOT_BLOCK, 512), lambda g, s: (g, 0))),
            scratch_shapes=[
                pltpu.VMEM((4, 64, 128), BF),
                pltpu.VMEM((4, 64, 128), BF),
                pltpu.VMEM((4, 64, 256), BF),
                pltpu.VMEM((SLOT_BLOCK, 512), F32),
            ],
        ),
        compiler_params=params(1),
        cost_estimate=cost(1 << 27, 36 << 20),
        name="decode_step",
    )(keep, states, rkv, rkv, rkv, log_decay, gate, vectors)


def span_tables():
    t = np.arange(CH)
    blocks = []
    size = 4
    while size <= CH:
        start = (t // size) * size
        mid = start + size // 2
        m = np.zeros((CH, CH), np.float32)
        for i in range(CH):
            if i >= mid[i]:
                m[i, mid[i] : i] = 1.0
            else:
                m[i, i + 1 : mid[i]] = 1.0
        blocks.append(m)
        size *= 2
    before = (t[None, :] < t[:, None]).astype(np.float32)
    after = (t[None, :] > t[:, None]).astype(np.float32)
    whole = np.ones((8, CH), np.float32)
    table = np.concatenate(blocks + [before, after, whole])
    return np.concatenate([table, table], axis=1)


LEVELS = int(np.log2(CH))


def wkv_kernel(
    count_ref, table_ref, r_ref, k_ref, v_ref, w_ref, g_ref, vec_ref, start_ref, *outs, t0, last
):
    c, p = pl.program_id(0), pl.program_id(1)
    out_ref, state_ref = outs[0], outs[1]

    @pl.when(c == 0)
    def _():
        state_ref[p] = start_ref[p]

    table = table_ref[...]
    row = lax.broadcasted_iota(jnp.int32, (CH, 512), 0)
    lane = lax.broadcasted_iota(jnp.int32, (CH, 128), 1)
    low = lane < 64
    arow = lax.broadcasted_iota(jnp.int32, (CH, 2 * CH), 0)
    acol = lax.broadcasted_iota(jnp.int32, (CH, 2 * CH), 1) & (CH - 1)
    diff = arow ^ acol
    causal = arow > acol
    srow = lax.broadcasted_iota(jnp.int32, (128, 128), 0) < 64
    scol = lax.broadcasted_iota(jnp.int32, (128, 128), 1) < 64
    same_head = srow == scol
    mean_of = jnp.where(same_head, 1.0 / 64, 0.0).astype(BF)
    mean_two = jnp.concatenate([mean_of, mean_of], axis=0)
    reward, scale, offset = vec_ref[0:1], vec_ref[1:2], vec_ref[2:3]
    contract_lanes = (((1,), (1,)), ((), ()))
    contract_rows = (((0,), (0,)), ((), ()))

    def both_heads(a):
        zero = jnp.zeros_like(a)
        return jnp.concatenate([jnp.where(low, a, zero), jnp.where(low, zero, a)], axis=0)

    live = (row + (c * CH + t0)) < count_ref[p]
    r = r_ref[0].astype(F32)
    k = jnp.where(live, k_ref[0].astype(F32), 0.0)
    v = v_ref[0]
    w = w_ref[...]
    w_hi = w.astype(BF)
    w_lo = (w - w_hi.astype(F32)).astype(BF)
    sums = jnp.dot(table, jnp.concatenate([w_hi, w_lo], axis=0), preferred_element_type=F32)
    factors = jnp.exp(sums)
    r_dec = (r * factors[(LEVELS - 1) * CH : LEVELS * CH]).astype(BF)
    k_dec = (k * factors[LEVELS * CH : (LEVELS + 1) * CH]).astype(BF)
    whole = factors[(LEVELS + 1) * CH : (LEVELS + 1) * CH + 1]
    r_own = r * reward
    r_hi = r_own.astype(BF)
    r_lo = (r_own - r_hi.astype(F32)).astype(BF)
    k_bf = k.astype(BF)
    mixed = [jnp.where((row & 1) == 1, r, k).astype(BF)]
    for level in range(1, LEVELS):
        pick = jnp.where((row & (1 << level)) != 0, r, k)
        mixed.append((pick * factors[(level - 1) * CH : level * CH]).astype(BF))
    for q in range(4):
        cols = slice(128 * q, 128 * q + 128)
        keys = both_heads(k_bf[:, cols])
        scores = lax.dot_general(
            jnp.concatenate([r_hi[:, cols], r_lo[:, cols]], axis=1),
            jnp.concatenate([keys, keys], axis=1),
            contract_lanes,
            preferred_element_type=F32,
        )
        scores = jnp.where(diff == 0, scores, 0.0)
        for level in range(LEVELS):
            a = mixed[level][:, cols]
            s = lax.dot_general(a, both_heads(a), contract_lanes, preferred_element_type=F32)
            here = jnp.logical_and(causal, (diff >> level) == 1)
            scores = jnp.where(here, s, scores)
        vq = v[:, cols]
        state = state_ref[p, q]
        y = jnp.dot(scores.astype(BF), both_heads(vq), preferred_element_type=F32)
        y = y + lax.dot_general(
            r_dec[:, cols], state.astype(BF), contract_lanes, preferred_element_type=F32
        )
        added = lax.dot_general(vq, k_dec[:, cols], contract_rows, preferred_element_type=F32)
        state_ref[p, q] = state * whole[:, cols] + jnp.where(same_head, added, 0.0)
        y_hi = y.astype(BF)
        y_lo = (y - y_hi.astype(F32)).astype(BF)
        mean = jnp.dot(
            jnp.concatenate([y_hi, y_lo], axis=1), mean_two, preferred_element_type=F32
        )
        center = y - mean
        spread = jnp.dot((center * center).astype(BF), mean_of, preferred_element_type=F32)
        normed = center * lax.rsqrt(spread + NORM_EPS)
        gate = g_ref[:, cols].astype(F32)
        out_ref[0, :, cols] = ((normed * scale[:, cols] + offset[:, cols]) * gate).astype(
            out_ref.dtype
        )

    if last:
        final_ref = outs[2]

        @pl.when(c == pl.num_programs(0) - 1)
        def _():
            for q in range(4):
                turned = jnp.transpose(state_ref[p, q])
                final_ref[0, 2 * q] = turned[:64, :64]
                final_ref[0, 2 * q + 1] = turned[64:, 64:]


def wkv(counts, rkv, log_decay, gate, vectors, start, t0, t1, length):
    prompts = start.shape[0]
    table = jnp.asarray(span_tables(), BF)
    c0, per = t0 // CH, length // CH
    last = t1 == length

    def part(n):
        return pl.BlockSpec((1, CH, 512), lambda c, p, s: (n, p * per + c + c0, 0))

    flat = pl.BlockSpec((CH, 512), lambda c, p, s: (p * per + c + c0, 0))
    held = pl.BlockSpec((prompts, 4, 128, 128), lambda c, p, s: (0, 0, 0, 0))
    out_shape = [
        jax.ShapeDtypeStruct((prompts, t1 - t0, 512), BF),
        jax.ShapeDtypeStruct((prompts, 4, 128, 128), F32),
    ]
    out_specs = [pl.BlockSpec((1, CH, 512), lambda c, p, s: (p, c, 0)), held]
    if last:
        out_shape.append(jax.ShapeDtypeStruct((prompts, 8, 64, 64), F32))
        out_specs.append(pl.BlockSpec((1, 8, 64, 64), lambda c, p, s: (p, 0, 0, 0)))
    return pl.pallas_call(
        functools.partial(wkv_kernel, t0=t0, last=last),
        out_shape=out_shape,
        grid_spec=pltpu.PrefetchScalarGridSpec(
            num_scalar_prefetch=1,
            grid=((t1 - t0) // CH, prompts),
            in_specs=[
                pl.BlockSpec(table.shape, lambda c, p, s: (0, 0)),
                part(0),
                part(1),
                part(2),
                flat,
                flat,
                pl.BlockSpec((8, 512), lambda c, p, s: (0, 0)),
                held,
            ],
            out_specs=out_specs,
        ),
        compiler_params=params(2),
        cost_estimate=cost((t1 - t0) * 80_000_000, (t1 - t0) << 17),
        name="wkv",
    )(counts, table, rkv, rkv, rkv, log_decay, gate, vectors, start)


def on_device(
    learner_acceptance_matrix,
    learner_address_matrix,
    learner_content_matrix,
    learner_gating_matrix,
    learner_result_matrix,
    fading_narrowing_matrix,
    fading_widening_matrix,
    feature_fading_speed,
    current_reward,
    symbol_blending_factors,
    group_scaling_factor,
    group_scaling_offset,
    request_hidden_entries,
    request_valid_count,
    request_destination_place,
    newest_symbol_hidden,
    preceding_hidden_entry,
    place_memory_matrix,
    place_newness_marks,
):
    h = lax.axis_index("yh") * 2 + lax.axis_index("core")
    z, x, yl = lax.axis_index("z"), lax.axis_index("x"), lax.axis_index("yl")
    req = z * 8 + x * 2 + yl
    place = jnp.stack([h, z, x, yl]).astype(jnp.int32)
    prompts, length, width = request_hidden_entries.shape
    slots, groups, breadth = place_memory_matrix.shape[:3]
    tokens = prompts * length
    rows = tokens + slots
    keep = place_newness_marks != 1
    counts = request_valid_count

    blocks = column_blocks(
        [
            learner_acceptance_matrix,
            learner_address_matrix,
            learner_content_matrix,
            learner_gating_matrix,
            learner_result_matrix,
        ],
        h,
    )
    hidden = request_hidden_entries.reshape(tokens, width)
    prior = jnp.where(keep[:, None], preceding_hidden_entry, jnp.zeros((), BF))
    hidden, newest, prior = after((hidden, newest_symbol_hidden, prior), blocks[1])
    own = jnp.concatenate([hidden, newest, prior], axis=0)
    by_row = with_neighbour(jnp.stack(blocks), yl)
    side = swap(own, "head", 1)
    far = swap(own, "head", 2)
    far_side = swap(far, "head", 1)

    def mixes(piece, d, mixed, low):
        return mix(
            place,
            counts,
            piece,
            d,
            symbol_blending_factors,
            fading_narrowing_matrix,
            low,
            mixed,
            fading_widening_matrix,
            feature_fading_speed[None],
            slots,
            length,
        )

    every, first, second = slice(0, 5), slice(0, 3), slice(3, 5)
    held = [by_row[p][None, None] for p in range(4)]
    recv = swap_all(held, 0)
    mixed, low = mixes(own, 0, None, None)
    held = pack(place, held, after(recv, low), 0, every)
    recv = swap_all(held, 1)
    mixed, low = mixes(side, 1, mixed, low)
    held = pack(place, held, after(recv, low), 1, every)
    recv = swap_all(held, 2)
    mixed, low = mixes(far, 2, mixed, low)
    recv = after(recv, low)
    early = pack(place, held, recv, 2, first)
    early_recv = swap_all(early, 3)
    late = pack(place, held, recv, 2, second)
    mixed, log_decay = mixes(far_side, 3, mixed, low)
    early_recv = after(early_recv, log_decay)
    late_recv = swap_all(after(late, early_recv), 3)
    early = list(early) + early_recv
    late = list(late) + late_recv

    rkv = project_rkv(place, mixed, early, rows // 2)
    gate = project_gate(place, mixed, late, rows // 2)
    small = jnp.stack([current_reward, group_scaling_factor, group_scaling_offset])
    vectors = jnp.concatenate([small, jnp.zeros((5, width), F32)])
    new_state, normed_d = decode_step(
        place_memory_matrix, keep.astype(jnp.int32), rkv, log_decay, gate, vectors
    )
    state = jnp.zeros((prompts, groups // 2, 128, 128), F32)
    sent = []
    t0 = 0
    for t1 in (256, 384, 512):
        out = wkv(counts, rkv, log_decay, gate, vectors, state, t0, t1, length)
        state = out[1]
        normed = out[0].reshape(prompts * (t1 - t0), width)
        if t0 == 0:
            normed = jnp.concatenate([normed, normed_d], axis=0)
        n_side = swap(normed, "head", 1)
        n_far = swap(normed, "head", 2)
        n_far_side = swap(n_far, "head", 1)
        sent.append([normed, n_side, n_far, n_far_side])
        t0 = t1
    result, decode_all = project_result(
        place, counts, sent[0], late, (256,), 0, True, None, length
    )
    (result,) = project_result(
        place, counts, sent[1] + sent[2], late, (128, 128), 256, False, result, length
    )
    prompt_hidden = result
    final_state = out[2]

    offsets = request_destination_place - req * slots
    slot_ids = lax.broadcasted_iota(jnp.int32, (slots,), 0)
    new_shift = newest_symbol_hidden
    taken = jnp.zeros((slots,), jnp.bool_)
    for n in range(prompts):
        new_state = lax.dynamic_update_slice(
            new_state, final_state[n : n + 1], (offsets[n], 0, 0, 0)
        )
        last_token = lax.dynamic_slice(
            request_hidden_entries, (n, counts[n] - 1, 0), (1, 1, width)
        )[0]
        new_shift = lax.dynamic_update_slice(new_shift, last_token, (offsets[n], 0))
        taken = taken | (slot_ids == offsets[n])
    decode_hidden = jnp.where(taken[:, None], jnp.zeros((), BF), decode_all)
    return (prompt_hidden, decode_hidden, new_state, new_shift)


def solution(mesh):
    split = Mesh(mesh.devices.reshape(2, 2, 4, 4, 2), ("yh", "core", "z", "x", "yl"))
    head = ("yh", "core")
    req = ("z", "x", "yl")
    row_shard = P(head + req, None)
    in_specs = (
        row_shard,
        row_shard,
        row_shard,
        row_shard,
        row_shard,
        P(),
        P(None, head),
        P(head),
        P(head),
        P(),
        P(head),
        P(head),
        P(req, None, head),
        P(req),
        P(req),
        P(req, head),
        P(req, head),
        P(req, head, None, None),
        P(req),
    )
    out_specs = (
        P(req, None, head),
        P(req, head),
        P(req, head, None, None),
        P(req, head),
    )
    return jax.shard_map(
        on_device, mesh=split, in_specs=in_specs, out_specs=out_specs, check_vma=False
    )
```

```python
import functools

import jax
import jax.numpy as jnp
import numpy as np
from jax import lax
from jax.experimental import pallas as pl
from jax.experimental.pallas import tpu as pltpu
from jax.sharding import Mesh
from jax.sharding import PartitionSpec as P

NORM_EPS = 0.00064
N_HEAD = 4
CH = 64
BF = jnp.bfloat16
F32 = jnp.float32


STEPS = (("x", 1), ("z", 1), ("x", 3), ("z", 3))


def swap(a, axes, bits):
    sizes = {"x": 4, "z": 4, "yl": 2, "head": 4}
    names = ("yh", "core") if axes == "head" else axes
    return lax.ppermute(a, names, [(i, i ^ bits) for i in range(sizes[axes])])


def order_of(part):
    return [STEPS[(part + n) % 4] for n in range(4)]


def after(value, other):
    return lax.optimization_barrier((value, other))[0]


ANY = pl.BlockSpec(memory_space=pl.ANY)


def in_hbm(*arrays):
    return [pltpu.with_memory_space_constraint(a, pltpu.HBM) for a in arrays]


def cost(flops, nbytes, trans=0):
    return pl.CostEstimate(flops=flops, bytes_accessed=nbytes, transcendentals=trans)


def params(axes):
    return pltpu.CompilerParams(
        dimension_semantics=("arbitrary",) * axes, vmem_limit_bytes=48 << 20
    )


def split_kernel(place_ref, keep_ref, count_ref, spot_ref, *refs):
    mats, hid, newest, prior = refs[:5], refs[5], refs[6], refs[7]
    outs, own_ref, shift_ref = refs[8:12], refs[12], refs[13]
    buf, old, sem = refs[14:]
    tokens, slots = hid.shape[0], newest.shape[0]
    copies = [pltpu.make_async_copy(mats[m], buf.at[m], sem.at[m]) for m in range(5)]
    copies += [
        pltpu.make_async_copy(prior, old, sem.at[5]),
        pltpu.make_async_copy(newest, own_ref.at[pl.ds(tokens, slots)], sem.at[6]),
        pltpu.make_async_copy(hid, own_ref.at[pl.ds(0, tokens)], sem.at[7]),
    ]
    for copy in copies:
        copy.start()
    row = lax.broadcasted_iota(jnp.int32, (slots, 512), 0)
    keep = jnp.zeros((slots, 512), F32)
    for n in range(slots):
        keep = jnp.where(row == n, keep_ref[n].astype(F32), keep)
    for m in range(5):
        copies[m].wait()
    for d in range(4):
        at = pl.multiple_of((place_ref[0] ^ d) * 512, 512)
        for m in range(5):
            outs[d][m] = buf[m, :, pl.ds(at, 512)].astype(BF)
    copies[5].wait()
    kept = jnp.where(keep > 0.5, old[...].astype(F32), 0.0)
    own_ref[tokens + slots :] = kept.astype(BF)
    copies[6].wait()
    copies[7].wait()
    shift = own_ref[tokens : tokens + slots].astype(F32)
    few = lax.broadcasted_iota(jnp.int32, (16, 512), 0)
    for p in range(2):
        at = p * (tokens // 2) + count_ref[p] - 1
        base = pl.multiple_of((at >> 4) << 4, 16)
        near = own_ref[pl.ds(base, 16)].astype(F32)
        last = jnp.sum(jnp.where(few == (at & 15), near, 0.0), axis=0, keepdims=True)
        shift = jnp.where(row == spot_ref[p], last, shift)
    shift_ref[...] = shift.astype(BF)


def split(place, keep, counts, spots, matrices, hidden, newest, prior):
    rows, width = matrices[0].shape[0], matrices[0].shape[1] // N_HEAD
    shape = (len(matrices), rows, width)
    total = hidden.shape[0] + 2 * newest.shape[0]
    hbm = pl.BlockSpec(memory_space=pltpu.HBM)
    out = pl.pallas_call(
        split_kernel,
        out_shape=[jax.ShapeDtypeStruct(shape, BF)] * 4
        + [jax.ShapeDtypeStruct((total, width), BF), jax.ShapeDtypeStruct(newest.shape, BF)],
        grid_spec=pltpu.PrefetchScalarGridSpec(
            num_scalar_prefetch=4,
            grid=(1,),
            in_specs=[hbm] * 8,
            out_specs=[pl.BlockSpec(shape, lambda i, *s: (0, 0, 0))] * 4
            + [
                pl.BlockSpec((total, width), lambda i, *s: (0, 0)),
                pl.BlockSpec(newest.shape, lambda i, *s: (0, 0)),
            ],
            scratch_shapes=[
                pltpu.VMEM((5,) + matrices[0].shape, F32),
                pltpu.VMEM(newest.shape, BF),
                pltpu.SemaphoreType.DMA((8,)),
            ],
        ),
        compiler_params=params(1),
        name="split",
    )(place, keep, counts, spots, *in_hbm(*matrices, hidden, newest, prior))
    return out[:4], out[4], out[5]


def in_order(own, other, yl):
    first = yl == 0
    return jnp.concatenate(
        [jnp.where(first, own, other), jnp.where(first, other, own)], axis=-2
    )


def axis_dim(axis):
    return 0 if axis == "z" else 1


def places(p, n, place_ref):
    axis, bits = order_of(p)[n]
    pos = place_ref[1] if axis == "z" else place_ref[2]
    seen = [b for name, b in order_of(p)[:n] if name == axis]
    offsets = [0] + seen
    return [pos ^ o for o in offsets], [pos ^ bits ^ o for o in offsets]


def part_of(ref, dim, i, lot):
    return ref.at[i, :, lot] if dim == 0 else ref.at[:, i, lot]


def pack_kernel(place_ref, *refs, n, lot):
    owns, recvs, outs, sem = refs[:4], refs[4:8], refs[8:12], refs[12]
    copies = []
    for p in range(4):
        dim = axis_dim(order_of(p)[n][0])
        own_at, recv_at = places(p, n, place_ref)
        if len(own_at) == 1:
            own_at, recv_at = [0], [1]
        for src, at in ((owns[p], own_at), (recvs[p], recv_at)):
            for i, j in enumerate(at):
                source = part_of(src, dim, i, lot)
                target = part_of(outs[p], dim, j, slice(None))
                copies.append(pltpu.make_async_copy(source, target, sem.at[len(copies)]))
    for copy in copies:
        copy.start()
    for copy in copies:
        copy.wait()


def pack(place, owns, recvs, n, lot):
    shapes = []
    for p in range(4):
        shape = list(owns[p].shape)
        shape[axis_dim(order_of(p)[n][0])] *= 2
        shape[2] = lot.stop - lot.start
        shapes.append(jax.ShapeDtypeStruct(tuple(shape), BF))
    return pl.pallas_call(
        functools.partial(pack_kernel, n=n, lot=lot),
        out_shape=shapes,
        grid_spec=pltpu.PrefetchScalarGridSpec(
            num_scalar_prefetch=1,
            grid=(1,),
            in_specs=[ANY] * 8,
            out_specs=[pl.BlockSpec(a.shape, lambda i, s: (0, 0, 0, 0, 0)) for a in shapes],
            scratch_shapes=[pltpu.SemaphoreType.DMA((16,))],
        ),
        compiler_params=params(1),
        cost_estimate=cost(0, 8 << 20),
        name="pack",
    )(place, *in_hbm(*owns, *recvs))


def swap_all(owns, n):
    return [swap(owns[p], *order_of(p)[n]) for p in range(4)]


def copy_weights(pieces, m, place_ref, buf, sem):
    for p in range(4):
        dim = axis_dim(order_of(p)[3][0])
        own_at, recv_at = places(p, 3, place_ref)
        for src, at in ((pieces[p], own_at), (pieces[p + 4], recv_at)):
            for i, j in enumerate(at):
                target = buf.at[p * 4 + j] if dim == 0 else buf.at[pl.ds(p * 4, 4), j]
                pltpu.make_async_copy(part_of(src, dim, i, m), target, sem).start()


def wait_weights(buf, sem):
    pltpu.make_async_copy(buf, buf, sem).wait()


def mix_kernel(place_ref, count_ref, *refs, d, length):
    hid_ref, mu_ref, narrow_ref = refs[:3]
    refs = refs[3:]
    if d > 0:
        low_in, refs = refs[0], refs[2:]
    if d == 3:
        widen_ref, speed_ref, refs = refs[0], refs[1], refs[2:]
    x_ref, low_ref, cur_ref, step_ref = refs
    i = pl.program_id(0)
    rows = cur_ref.shape[0]
    slots = hid_ref.shape[0] - rows
    tokens = rows - slots

    @pl.when(i == 0)
    def _():
        cur = hid_ref[:rows].astype(F32)
        cur_ref[...] = cur
        seq = cur[:tokens]
        at = lax.broadcasted_iota(jnp.int32, seq.shape, 0)
        before = jnp.where((at & (length - 1)) == 0, 0.0, pltpu.roll(seq, 1, 0))
        step_ref[:tokens] = before - seq
        step_ref[tokens:] = hid_ref[rows:].astype(F32) - cur[tokens:]

    mixed = (cur_ref[...] + step_ref[...] * mu_ref[pl.ds(i, 1), :]).astype(BF)
    x_ref[0] = mixed

    @pl.when(i == 3)
    def _():
        low = lax.dot_general(
            mixed, narrow_ref[...], (((1,), (1,)), ((), ())), preferred_element_type=F32
        )
        if d > 0:
            low = low + low_in[...]
        if d < 3:
            low_ref[...] = low
        else:
            lowrank = jnp.tanh(low).astype(BF)
            rate = jnp.exp(jnp.dot(lowrank, widen_ref[...], preferred_element_type=F32))
            log_decay = -speed_ref[...] * rate
            at = lax.broadcasted_iota(jnp.int32, (rows, 512), 0)
            limit = jnp.where(
                at < length,
                count_ref[0],
                jnp.where(at < 2 * length, count_ref[1] + length, rows),
            )
            low_ref[...] = jnp.where(at < limit, log_decay, 0.0)


def mix(place, counts, hidden, d, mu, narrow, low, held, widen, speed, slots, length):
    rows = hidden.shape[0] - slots
    once = lambda i, s, c: (0, 0)
    args = in_hbm(hidden, mu, narrow)
    specs = [
        pl.BlockSpec(hidden.shape, once),
        pl.BlockSpec((5, 512), lambda i, s, c: (0, s[0] ^ d)),
        pl.BlockSpec((64, 512), lambda i, s, c: (0, s[0] ^ d)),
    ]
    alias = {}
    if d > 0:
        args += in_hbm(low, held)
        specs += [pl.BlockSpec(low.shape, once), ANY]
        alias = {6: 0}
    wide = 64
    if d == 3:
        args += in_hbm(widen, speed)
        specs += [pl.BlockSpec(widen.shape, once), pl.BlockSpec(speed.shape, once)]
        wide = 512
    return pl.pallas_call(
        functools.partial(mix_kernel, d=d, length=length),
        out_shape=(
            jax.ShapeDtypeStruct((5, rows, 2048), BF),
            jax.ShapeDtypeStruct((rows, wide), F32),
        ),
        grid_spec=pltpu.PrefetchScalarGridSpec(
            num_scalar_prefetch=2,
            grid=(5,),
            in_specs=specs,
            out_specs=(
                pl.BlockSpec((1, rows, 512), lambda i, s, c: (i, 0, d)),
                pl.BlockSpec((rows, wide), once),
            ),
            scratch_shapes=[pltpu.VMEM((rows, 512), F32), pltpu.VMEM((rows, 512), F32)],
        ),
        input_output_aliases=alias,
        compiler_params=params(1),
        cost_estimate=cost(20 * rows * 512, 12 * rows * 512),
        name="mix",
    )(place, counts, *args)


def rkv_kernel(place_ref, x_ref, *refs):
    pieces = refs[:8]
    out_ref, buf, sem = refs[8:]
    i, j = pl.program_id(0), pl.program_id(1)
    slot = lax.rem(i, 2)

    @pl.when(jnp.logical_and(i == 0, j == 0))
    def _():
        copy_weights(pieces, 0, place_ref, buf.at[0], sem.at[0])

    @pl.when(j == 0)
    def _():
        @pl.when(i < 2)
        def _():
            copy_weights(pieces, i + 1, place_ref, buf.at[1 - slot], sem.at[1 - slot])

        wait_weights(buf.at[slot], sem.at[slot])

    w = buf[slot].reshape(2048, 512)
    out_ref[0] = jnp.dot(x_ref[0], w, preferred_element_type=F32).astype(out_ref.dtype)


def project_rkv(place, mixed, pieces, tile):
    rows = mixed.shape[1]
    return pl.pallas_call(
        rkv_kernel,
        out_shape=jax.ShapeDtypeStruct((3, rows, 512), BF),
        grid_spec=pltpu.PrefetchScalarGridSpec(
            num_scalar_prefetch=1,
            grid=(3, rows // tile),
            in_specs=[pl.BlockSpec((1, tile, 2048), lambda i, j, s: (i, j, 0))] + [ANY] * 8,
            out_specs=pl.BlockSpec((1, tile, 512), lambda i, j, s: (i, j, 0)),
            scratch_shapes=[
                pltpu.VMEM((2, 16, 4, 32, 512), BF),
                pltpu.SemaphoreType.DMA((2,)),
            ],
        ),
        compiler_params=params(2),
        cost_estimate=cost(6 * rows * 2048 * 512, 24 << 20),
        name="project_rkv",
    )(place, mixed, *pieces)


def gate_kernel(place_ref, x_ref, *refs):
    pieces = refs[:8]
    out_ref, buf, sem = refs[8:]

    @pl.when(pl.program_id(0) == 0)
    def _():
        copy_weights(pieces, 0, place_ref, buf, sem)
        wait_weights(buf, sem)

    total = jnp.dot(x_ref[0], buf[...].reshape(2048, 512), preferred_element_type=F32)
    out_ref[...] = (total / (1.0 + jnp.exp(-total))).astype(out_ref.dtype)


def project_gate(place, mixed, pieces, tile):
    rows = mixed.shape[1]
    return pl.pallas_call(
        gate_kernel,
        out_shape=jax.ShapeDtypeStruct((rows, 512), BF),
        grid_spec=pltpu.PrefetchScalarGridSpec(
            num_scalar_prefetch=1,
            grid=(rows // tile,),
            in_specs=[pl.BlockSpec((1, tile, 2048), lambda j, s: (4, j, 0))] + [ANY] * 8,
            out_specs=pl.BlockSpec((tile, 512), lambda j, s: (j, 0)),
            scratch_shapes=[pltpu.VMEM((16, 4, 32, 512), BF), pltpu.SemaphoreType.DMA(())],
        ),
        compiler_params=params(1),
        cost_estimate=cost(2 * rows * 2048 * 512, 8 << 20),
        name="project_gate",
    )(place, mixed, *pieces)


def result_kernel(place_ref, count_ref, spot_ref, *refs, spans, t0, slot0, chained):
    lots = len(spans)
    xs, pieces = refs[: 4 * lots], refs[4 * lots : 4 * lots + 8]
    rest = refs[4 * lots + 8 + (2 if chained else 0) :]
    out_ref, slot_ref, buf, sem = rest
    copy_weights(pieces, 1, place_ref, buf, sem)
    wait_weights(buf, sem)
    start = slot = 0
    for lot, span in enumerate(spans):
        total = None
        for d in range(4):
            w = buf[4 * d : 4 * d + 4].reshape(512, 512)
            term = jnp.dot(xs[4 * lot + d][...], w, preferred_element_type=F32)
            total = term if total is None else total + term
        at = lax.broadcasted_iota(jnp.int32, (span, 512), 0) + (t0 + start)
        for p in range(2):
            own = jnp.where(at < count_ref[p], total[p * span : (p + 1) * span], 0.0)
            out_ref[p, start : start + span] = own.astype(out_ref.dtype)
        start += span
        more = total.shape[0] - 2 * span
        which = lax.broadcasted_iota(jnp.int32, (more, 512), 0) + (slot0 + slot)
        taken = jnp.logical_or(which == spot_ref[0], which == spot_ref[1])
        own = jnp.where(taken, 0.0, total[2 * span :])
        slot_ref[slot : slot + more] = own.astype(slot_ref.dtype)
        slot += more


def project_result(place, counts, spots, xs, pieces, spans, t0, earlier, length, all_slots):
    span = sum(spans)
    slots = sum(xs[4 * n].shape[0] - 2 * spans[n] for n in range(len(spans)))
    once = lambda i, *s: (0, 0)
    chained = earlier is not None
    block = t0 // span
    return pl.pallas_call(
        functools.partial(
            result_kernel, spans=spans, t0=t0, slot0=block * slots, chained=chained
        ),
        out_shape=[
            jax.ShapeDtypeStruct((2, length, 512), BF),
            jax.ShapeDtypeStruct((all_slots, 512), BF),
        ],
        grid_spec=pltpu.PrefetchScalarGridSpec(
            num_scalar_prefetch=3,
            grid=(1,),
            in_specs=[pl.BlockSpec(a.shape, once) for a in xs] + [ANY] * (10 if chained else 8),
            out_specs=[
                pl.BlockSpec((2, span, 512), lambda i, *s: (0, block, 0)),
                pl.BlockSpec((slots, 512), lambda i, *s: (block, 0)),
            ],
            scratch_shapes=[pltpu.VMEM((16, 4, 32, 512), BF), pltpu.SemaphoreType.DMA(())],
        ),
        input_output_aliases={3 + len(xs) + 8: 0, 3 + len(xs) + 9: 1} if chained else {},
        compiler_params=params(1),
        cost_estimate=cost(4 * span * 2048 * 512, 8 << 20),
        name="project_result",
    )(place, counts, spots, *xs, *pieces, *(earlier if chained else []))


SLOT_BLOCK = 8


def head_mask(value):
    row = lax.broadcasted_iota(jnp.int32, (128, 128), 0) < 64
    col = lax.broadcasted_iota(jnp.int32, (128, 128), 1) < 64
    return jnp.where(row == col, value, 0.0).astype(BF)


def in_two(a):
    hi = a.astype(BF)
    return jnp.concatenate([hi, (a - hi.astype(F32)).astype(BF)], axis=1)


def turn_decode(r_ref, k_ref, w_ref, rt_ref, kt_ref, dt_ref):
    r = r_ref[0].astype(F32)
    k = k_ref[0].astype(F32)
    decay = jnp.exp(w_ref[...])
    for q in range(4):
        cols = slice(128 * q, 128 * q + 128)

        def turned(a):
            t = jnp.transpose(a[:, cols])
            return jnp.concatenate([t[:64], t[64:]], axis=1)

        rt_ref[q] = turned(r).astype(BF)
        kt_ref[q] = turned(k).astype(BF)
        dt_ref[q] = in_two(turned(decay))


def decode_slots(
    first, keep_ref, s_ref, r_ref, k_ref, v_ref, g_ref, vec_ref, next_ref, rt_ref, kt_ref, dt_ref,
    y_ref,
):
    here = pl.ds(pl.multiple_of(first, SLOT_BLOCK), SLOT_BLOCK)
    v = v_ref[0, here].astype(F32)
    row = lax.broadcasted_iota(jnp.int32, (128, 128), 0)
    low = lax.broadcasted_iota(jnp.int32, (128, 128), 1) < 64
    for s in range(SLOT_BLOCK):
        slot = first + s
        hit = row == jnp.where(low, slot, slot + 64)
        pick = jnp.where(hit, 1.0, 0.0).astype(BF)
        kept = jnp.where(hit, keep_ref[slot].astype(F32), 0.0).astype(BF)
        r_b = jnp.dot(rt_ref[...].reshape(256, 128), kept, preferred_element_type=F32)
        k_b = jnp.dot(kt_ref[...].reshape(256, 128), pick, preferred_element_type=F32)
        d_b = jnp.dot(
            dt_ref[...].reshape(256, 256),
            jnp.concatenate([kept, kept], axis=0),
            preferred_element_type=F32,
        )
        for q in range(4):
            span = slice(64 * q, 64 * q + 64)
            cols = slice(128 * q, 128 * q + 128)
            state = jnp.concatenate([s_ref[s, 2 * q], s_ref[s, 2 * q + 1]], axis=1)
            after_it = d_b[span] * state + k_b[span] * v[s : s + 1, cols]
            next_ref[s, 2 * q] = after_it[:, :64]
            next_ref[s, 2 * q + 1] = after_it[:, 64:]
            y_ref[s : s + 1, cols] = jnp.sum(r_b[span] * state, axis=0, keepdims=True)
    r = r_ref[0, here].astype(F32)
    k = k_ref[0, here].astype(F32)
    reward, scale, offset = vec_ref[0:1], vec_ref[1:2], vec_ref[2:3]
    own = r * reward * k
    ones = jnp.concatenate([head_mask(1.0)] * 2, axis=0)
    mean_of = jnp.concatenate([head_mask(1.0 / 64)] * 2, axis=0)
    out = []
    for q in range(4):
        cols = slice(128 * q, 128 * q + 128)
        total = jnp.dot(in_two(own[:, cols]), ones, preferred_element_type=F32)
        y = y_ref[:, cols] + total * v[:, cols]
        center = y - jnp.dot(in_two(y), mean_of, preferred_element_type=F32)
        spread = jnp.dot(in_two(center * center), mean_of, preferred_element_type=F32)
        normed = center * lax.rsqrt(spread + NORM_EPS) * scale[:, cols] + offset[:, cols]
        out.append((normed * g_ref[here, cols].astype(F32)).astype(BF))
    return jnp.concatenate(out, axis=1)


def span_tables():
    t = np.arange(CH)
    blocks = []
    size = 4
    while size <= CH:
        start = (t // size) * size
        mid = start + size // 2
        m = np.zeros((CH, CH), np.float32)
        for i in range(CH):
            if i >= mid[i]:
                m[i, mid[i] : i] = 1.0
            else:
                m[i, i + 1 : mid[i]] = 1.0
        blocks.append(m)
        size *= 2
    before = (t[None, :] < t[:, None]).astype(np.float32)
    after = (t[None, :] > t[:, None]).astype(np.float32)
    whole = np.ones((8, CH), np.float32)
    table = np.concatenate(blocks + [before, after, whole])
    return np.concatenate([table, table], axis=1)


LEVELS = int(np.log2(CH))


def wkv_kernel(
    count_ref, keep_ref, table_ref, *refs, t0, span, slot0, last, chained, prompts
):
    ins, refs = refs[: 5 * prompts], refs[5 * prompts :]
    vec_ref, start_ref, slots_ref, rd_ref, kd_ref, vd_ref, wd_ref, gd_ref = refs[:8]
    refs = refs[9:] if chained else refs[8:]
    out_ref, state_ref, next_ref = refs[:3]
    turned = refs[-4:-1]
    y_ref = refs[-1]
    c = pl.program_id(0)

    @pl.when(c == 0)
    def _():
        state_ref[...] = start_ref[...]
        turn_decode(rd_ref, kd_ref, wd_ref, *turned)

    table = table_ref[...]
    row = lax.broadcasted_iota(jnp.int32, (CH, 512), 0)
    low = lax.broadcasted_iota(jnp.int32, (CH, 128), 1) < 64
    arow = lax.broadcasted_iota(jnp.int32, (CH, 2 * CH), 0)
    acol = lax.broadcasted_iota(jnp.int32, (CH, 2 * CH), 1) & (CH - 1)
    diff = arow ^ acol
    causal = arow > acol
    same_head = (lax.broadcasted_iota(jnp.int32, (128, 128), 0) < 64) == (
        lax.broadcasted_iota(jnp.int32, (128, 128), 1) < 64
    )
    mean_of = head_mask(1.0 / 64)
    mean_two = jnp.concatenate([mean_of, mean_of], axis=0)
    reward, scale, offset = vec_ref[0:1], vec_ref[1:2], vec_ref[2:3]
    contract_lanes = (((1,), (1,)), ((), ()))
    contract_rows = (((0,), (0,)), ((), ()))

    def both_heads(a):
        zero = jnp.zeros_like(a)
        return jnp.concatenate([jnp.where(low, a, zero), jnp.where(low, zero, a)], axis=0)

    def lanes_dot(a, b):
        return lax.dot_general(a, b, contract_lanes, preferred_element_type=F32)

    def dot(a, b):
        return jnp.dot(a, b, preferred_element_type=F32)

    streams = [(p, q) for p in range(prompts) for q in range(4)]
    cols = [slice(128 * q, 128 * q + 128) for q in range(4)]
    keys, own, mixed, r_dec, k_dec, whole, values = {}, {}, {}, {}, {}, {}, {}
    for p in range(prompts):
        r_ref, k_ref, v_ref, w_ref, g_ref = ins[5 * p : 5 * p + 5]
        live = (row + (c * CH + t0)) < count_ref[p]
        r = r_ref[0].astype(F32)
        k = jnp.where(live, k_ref[0].astype(F32), 0.0)
        values[p] = v_ref[0]
        w = w_ref[...]
        w_hi = w.astype(BF)
        w_lo = (w - w_hi.astype(F32)).astype(BF)
        factors = jnp.exp(dot(table, jnp.concatenate([w_hi, w_lo], axis=0)))
        r_dec[p] = (r * factors[(LEVELS - 1) * CH : LEVELS * CH]).astype(BF)
        k_dec[p] = (k * factors[LEVELS * CH : (LEVELS + 1) * CH]).astype(BF)
        whole[p] = factors[(LEVELS + 1) * CH : (LEVELS + 1) * CH + 1]
        weighted = r * reward
        hi = weighted.astype(BF)
        own[p] = (hi, (weighted - hi.astype(F32)).astype(BF))
        keys[p] = k.astype(BF)
        mixed[p] = [jnp.where((row & 1) == 1, r, k).astype(BF)]
        for level in range(1, LEVELS):
            pick = jnp.where((row & (1 << level)) != 0, r, k)
            mixed[p].append((pick * factors[(level - 1) * CH : level * CH]).astype(BF))
    scores = {}
    for p, q in streams:
        key = both_heads(keys[p][:, cols[q]])
        s = lanes_dot(
            jnp.concatenate([half[:, cols[q]] for half in own[p]], axis=1),
            jnp.concatenate([key, key], axis=1),
        )
        scores[p, q] = jnp.where(diff == 0, s, 0.0)
    for level in range(LEVELS):
        here = jnp.logical_and(causal, (diff >> level) == 1)
        for p, q in streams:
            a = mixed[p][level][:, cols[q]]
            scores[p, q] = jnp.where(here, lanes_dot(a, both_heads(a)), scores[p, q])
    y = {}
    for p, q in streams:
        v = values[p][:, cols[q]]
        state = state_ref[p, q]
        y[p, q] = dot(scores[p, q].astype(BF), both_heads(v)) + lanes_dot(
            r_dec[p][:, cols[q]], state.astype(BF)
        )
        added = lax.dot_general(v, k_dec[p][:, cols[q]], contract_rows, preferred_element_type=F32)
        state_ref[p, q] = state * whole[p][:, cols[q]] + jnp.where(same_head, added, 0.0)
    center = {n: y[n] - dot(in_two(y[n]), mean_two) for n in streams}
    spread = {n: dot((center[n] * center[n]).astype(BF), mean_of) for n in streams}
    for p, q in streams:
        normed = center[p, q] * lax.rsqrt(spread[p, q] + NORM_EPS)
        gate = ins[5 * p + 4][:, cols[q]].astype(F32)
        at = pl.multiple_of(p * span + c * CH, CH)
        out_ref[pl.ds(at, CH), cols[q]] = (
            (normed * scale[:, cols[q]] + offset[:, cols[q]]) * gate
        ).astype(out_ref.dtype)

    done = decode_slots(
        slot0 + c * SLOT_BLOCK, keep_ref, slots_ref, rd_ref, kd_ref, vd_ref, gd_ref, vec_ref,
        next_ref, *turned, y_ref,
    )
    at = pl.multiple_of(prompts * span + c * SLOT_BLOCK, SLOT_BLOCK)
    out_ref[pl.ds(at, SLOT_BLOCK), :] = done

    if last:
        final_ref = refs[3]

        @pl.when(c == pl.num_programs(0) - 1)
        def _():
            for p, q in streams:
                whole_state = jnp.transpose(state_ref[p, q])
                final_ref[p, 2 * q] = whole_state[:64, :64]
                final_ref[p, 2 * q + 1] = whole_state[64:, 64:]


def wkv(counts, keep, rkv, log_decay, gate, vectors, start, states, earlier, t0, t1, length):
    prompts, slots = start.shape[0], states.shape[0]
    table = jnp.asarray(span_tables(), BF)
    c0, per, span = t0 // CH, length // CH, t1 - t0
    chunks = span // CH
    last, chained = t1 == length, earlier is not None
    at = prompts * length // slots

    def part(n, p):
        return pl.BlockSpec((1, CH, 512), lambda c, s, k: (n, p * per + c + c0, 0))

    def flat(p):
        return pl.BlockSpec((CH, 512), lambda c, s, k: (p * per + c + c0, 0))

    def slot_part(n):
        return pl.BlockSpec((1, slots, 512), lambda c, s, k: (n, at, 0))

    slot_flat = pl.BlockSpec((slots, 512), lambda c, s, k: (at, 0))
    big = pl.BlockSpec((SLOT_BLOCK, 8, 64, 64), lambda c, s, k: (c + c0, 0, 0, 0))
    held = pl.BlockSpec((prompts, 4, 128, 128), lambda c, s, k: (0, 0, 0, 0))
    rows = prompts * span + chunks * SLOT_BLOCK
    out_shape = [
        jax.ShapeDtypeStruct((rows, 512), BF),
        jax.ShapeDtypeStruct((prompts, 4, 128, 128), F32),
        jax.ShapeDtypeStruct(states.shape, F32),
    ]
    out_specs = [pl.BlockSpec((rows, 512), lambda c, s, k: (0, 0)), held, big]
    if last:
        out_shape.append(jax.ShapeDtypeStruct((prompts, 8, 64, 64), F32))
        out_specs.append(pl.BlockSpec((prompts, 8, 64, 64), lambda c, s, k: (0, 0, 0, 0)))
    ins, specs = [], []
    for p in range(prompts):
        ins += [rkv, rkv, rkv, log_decay, gate]
        specs += [part(0, p), part(1, p), part(2, p), flat(p), flat(p)]
    ins += [vectors, start, states, rkv, rkv, rkv, log_decay, gate]
    specs += [pl.BlockSpec((8, 512), lambda c, s, k: (0, 0)), held, big]
    specs += [slot_part(0), slot_part(1), slot_part(2), slot_flat, slot_flat]
    alias = {}
    if chained:
        ins.append(earlier)
        specs.append(ANY)
        alias = {2 + len(ins): 2}
    return pl.pallas_call(
        functools.partial(
            wkv_kernel,
            t0=t0,
            span=span,
            slot0=c0 * SLOT_BLOCK,
            last=last,
            chained=chained,
            prompts=prompts,
        ),
        out_shape=out_shape,
        grid_spec=pltpu.PrefetchScalarGridSpec(
            num_scalar_prefetch=2,
            grid=(chunks,),
            in_specs=[pl.BlockSpec(table.shape, lambda c, s, k: (0, 0))] + specs,
            out_specs=out_specs,
            scratch_shapes=[
                pltpu.VMEM((4, 64, 128), BF),
                pltpu.VMEM((4, 64, 128), BF),
                pltpu.VMEM((4, 64, 256), BF),
                pltpu.VMEM((SLOT_BLOCK, 512), F32),
            ],
        ),
        input_output_aliases=alias,
        compiler_params=params(1),
        cost_estimate=cost(span * 80_000_000, span << 17),
        name="wkv",
    )(counts, keep, table, *ins)


def on_device(
    learner_acceptance_matrix,
    learner_address_matrix,
    learner_content_matrix,
    learner_gating_matrix,
    learner_result_matrix,
    fading_narrowing_matrix,
    fading_widening_matrix,
    feature_fading_speed,
    current_reward,
    symbol_blending_factors,
    group_scaling_factor,
    group_scaling_offset,
    request_hidden_entries,
    request_valid_count,
    request_destination_place,
    newest_symbol_hidden,
    preceding_hidden_entry,
    place_memory_matrix,
    place_newness_marks,
):
    h = lax.axis_index("yh") * 2 + lax.axis_index("core")
    z, x, yl = lax.axis_index("z"), lax.axis_index("x"), lax.axis_index("yl")
    req = z * 8 + x * 2 + yl
    place = jnp.stack([h, z, x, yl]).astype(jnp.int32)
    prompts, length, width = request_hidden_entries.shape
    slots, groups, breadth = place_memory_matrix.shape[:3]
    tokens = prompts * length
    rows = tokens + slots
    keep = place_newness_marks != 1
    counts = request_valid_count

    spots = request_destination_place - req * slots
    parts, own, new_shift = split(
        place,
        keep.astype(jnp.int32),
        counts,
        spots,
        [
            learner_acceptance_matrix,
            learner_address_matrix,
            learner_content_matrix,
            learner_gating_matrix,
            learner_result_matrix,
        ],
        request_hidden_entries.reshape(tokens, width),
        newest_symbol_hidden,
        preceding_hidden_entry,
    )
    blocks = [parts[0]] + [swap(parts[d], "head", d) for d in (1, 2, 3)]
    side = swap(own, "head", 1)
    far = swap(after(own, blocks[3]), "head", 2)
    stacked = jnp.stack(blocks)
    neighbour = swap(stacked, "yl", 1)
    far_side = swap(far, "head", 1)

    def mixes(piece, d, mixed, low):
        return mix(
            place,
            counts,
            piece,
            d,
            symbol_blending_factors,
            fading_narrowing_matrix.T,
            low,
            mixed,
            fading_widening_matrix,
            feature_fading_speed[None],
            slots,
            length,
        )

    every, first, second = slice(0, 5), slice(0, 3), slice(3, 5)
    mixed, low = mixes(own, 0, None, None)
    neighbour, side, low = lax.optimization_barrier((neighbour, side, low))
    by_row = in_order(stacked, neighbour, yl)
    held = [by_row[p][None, None] for p in range(4)]
    recv = swap_all(held, 0)
    held = pack(place, held, recv, 0, every)
    recv = swap_all(held, 1)
    mixed, low = mixes(side, 1, mixed, low)
    held = pack(place, held, after(recv, low), 1, every)
    recv = swap_all(held, 2)
    mixed, low = mixes(far, 2, mixed, low)
    recv = after(recv, low)
    early = pack(place, held, recv, 2, first)
    early_recv = swap_all(early, 3)
    mixed, log_decay = mixes(far_side, 3, mixed, low)
    late = pack(place, held, after(recv, log_decay), 2, second)
    early_recv = after(early_recv, log_decay)
    late_recv = swap_all(after(late, early_recv), 3)
    early = list(early) + early_recv
    late = list(late) + late_recv

    rkv = project_rkv(place, mixed, early, rows)
    gate = project_gate(place, mixed, late, rows // 2)
    small = jnp.stack([current_reward, group_scaling_factor, group_scaling_offset])
    vectors = jnp.concatenate([small, jnp.zeros((5, width), F32)])
    state = jnp.zeros((prompts, groups // 2, 128, 128), F32)
    sent = []
    t0 = 0
    new_state = None
    kept = keep.astype(jnp.int32)
    for t1 in (256, 384, 512):
        out = wkv(
            counts,
            kept,
            rkv,
            log_decay,
            gate,
            vectors,
            state,
            place_memory_matrix,
            new_state,
            t0,
            t1,
            length,
        )
        normed, state, new_state = out[:3]
        n_side = swap(normed, "head", 1)
        n_far = swap(normed, "head", 2)
        if t1 == length:
            result = project_result(
                place, counts, spots, sent[0], late, (256,), 0, None, length, slots
            )
            n_far = after(n_far, result[1])
        n_far_side = swap(n_far, "head", 1)
        sent.append([normed, n_side, n_far, n_far_side])
        t0 = t1
    prompt_hidden, decode_hidden = project_result(
        place, counts, spots, sent[1] + sent[2], late, (128, 128), 256, result, length, slots
    )
    final_state = out[3]
    for n in range(prompts):
        new_state = lax.dynamic_update_slice(new_state, final_state[n : n + 1], (spots[n], 0, 0, 0))
    return (prompt_hidden, decode_hidden, new_state, new_shift)


def solution(mesh):
    split = Mesh(mesh.devices.reshape(2, 2, 4, 4, 2), ("yh", "core", "z", "x", "yl"))
    head = ("yh", "core")
    req = ("z", "x", "yl")
    row_shard = P(head + req, None)
    in_specs = (
        row_shard,
        row_shard,
        row_shard,
        row_shard,
        row_shard,
        P(),
        P(None, head),
        P(head),
        P(head),
        P(),
        P(head),
        P(head),
        P(req, None, head),
        P(req),
        P(req),
        P(req, head),
        P(req, head),
        P(req, head, None, None),
        P(req),
    )
    out_specs = (
        P(req, None, head),
        P(req, head),
        P(req, head, None, None),
        P(req, head),
    )
    return jax.shard_map(
        on_device, mesh=split, in_specs=in_specs, out_specs=out_specs, check_vma=False
    )
```

```python
import functools

import jax
import jax.numpy as jnp
import numpy as np
from jax import lax
from jax.experimental import pallas as pl
from jax.experimental.pallas import tpu as pltpu
from jax.sharding import Mesh
from jax.sharding import PartitionSpec as P

NORM_EPS = 0.00064
N_HEAD = 4
CH = 64
BF = jnp.bfloat16
F32 = jnp.float32


STEPS = (("x", 1), ("z", 1), ("x", 3), ("z", 3))


def swap(a, axes, bits):
    sizes = {"x": 4, "z": 4, "yl": 2, "head": 4}
    names = ("yh", "core") if axes == "head" else axes
    return lax.ppermute(a, names, [(i, i ^ bits) for i in range(sizes[axes])])


def order_of(part):
    return [STEPS[(part + n) % 4] for n in range(4)]


def after(value, other):
    return lax.optimization_barrier((value, other))[0]


ANY = pl.BlockSpec(memory_space=pl.ANY)


def in_hbm(*arrays):
    return [pltpu.with_memory_space_constraint(a, pltpu.HBM) for a in arrays]


def cost(flops, nbytes, trans=0):
    return pl.CostEstimate(flops=flops, bytes_accessed=nbytes, transcendentals=trans)


def params(axes):
    return pltpu.CompilerParams(
        dimension_semantics=("arbitrary",) * axes, vmem_limit_bytes=48 << 20
    )


def kept_of(fresh_ref, n):
    return jnp.where(fresh_ref[n] == 1, 0.0, 1.0)


def slot_of(place_ref, spot_ref, p):
    return spot_ref[p] - (place_ref[1] * 8 + place_ref[2] * 2 + place_ref[3]) * 64


def split_kernel(place_ref, keep_ref, count_ref, spot_ref, *refs):
    mats, hid, newest, prior = refs[:5], refs[5], refs[6], refs[7]
    outs, own_ref, shift_ref = refs[8:12], refs[12], refs[13]
    buf, old, sem = refs[14:]
    tokens, slots = hid.shape[0], newest.shape[0]
    copies = [pltpu.make_async_copy(mats[m], buf.at[m], sem.at[m]) for m in range(5)]
    copies += [
        pltpu.make_async_copy(prior, old, sem.at[5]),
        pltpu.make_async_copy(newest, own_ref.at[pl.ds(tokens, slots)], sem.at[6]),
        pltpu.make_async_copy(hid, own_ref.at[pl.ds(0, tokens)], sem.at[7]),
    ]
    for copy in copies:
        copy.start()
    row = lax.broadcasted_iota(jnp.int32, (slots, 512), 0)
    keep = jnp.zeros((slots, 512), F32)
    for n in range(slots):
        keep = jnp.where(row == n, kept_of(keep_ref, n), keep)
    for m in range(5):
        copies[m].wait()
    for d in range(4):
        at = pl.multiple_of((place_ref[0] ^ d) * 512, 512)
        for m in range(5):
            outs[d][m] = buf[m, :, pl.ds(at, 512)].astype(BF)
    copies[5].wait()
    kept = jnp.where(keep > 0.5, old[...].astype(F32), 0.0)
    own_ref[tokens + slots :] = kept.astype(BF)
    copies[6].wait()
    copies[7].wait()
    shift = own_ref[tokens : tokens + slots].astype(F32)
    few = lax.broadcasted_iota(jnp.int32, (16, 512), 0)
    for p in range(2):
        at = p * (tokens // 2) + count_ref[p] - 1
        base = pl.multiple_of((at >> 4) << 4, 16)
        near = own_ref[pl.ds(base, 16)].astype(F32)
        last = jnp.sum(jnp.where(few == (at & 15), near, 0.0), axis=0, keepdims=True)
        shift = jnp.where(row == slot_of(place_ref, spot_ref, p), last, shift)
    shift_ref[...] = shift.astype(BF)


def split(place, keep, counts, spots, matrices, hidden, newest, prior):
    rows, width = matrices[0].shape[0], matrices[0].shape[1] // N_HEAD
    shape = (len(matrices), rows, width)
    total = hidden.shape[0] + 2 * newest.shape[0]
    hbm = pl.BlockSpec(memory_space=pltpu.HBM)
    out = pl.pallas_call(
        split_kernel,
        out_shape=[jax.ShapeDtypeStruct(shape, BF)] * 4
        + [jax.ShapeDtypeStruct((total, width), BF), jax.ShapeDtypeStruct(newest.shape, BF)],
        grid_spec=pltpu.PrefetchScalarGridSpec(
            num_scalar_prefetch=4,
            grid=(1,),
            in_specs=[hbm] * 8,
            out_specs=[pl.BlockSpec(shape, lambda i, *s: (0, 0, 0))] * 4
            + [
                pl.BlockSpec((total, width), lambda i, *s: (0, 0)),
                pl.BlockSpec(newest.shape, lambda i, *s: (0, 0)),
            ],
            scratch_shapes=[
                pltpu.VMEM((5,) + matrices[0].shape, F32),
                pltpu.VMEM(newest.shape, BF),
                pltpu.SemaphoreType.DMA((8,)),
            ],
        ),
        compiler_params=params(1),
        name="split",
    )(place, keep, counts, spots, *in_hbm(*matrices, hidden, newest, prior))
    return out[:4], out[4], out[5]


def in_order(own, other, yl):
    first = yl == 0
    return jnp.concatenate(
        [jnp.where(first, own, other), jnp.where(first, other, own)], axis=-2
    )


def axis_dim(axis):
    return 0 if axis == "z" else 1


def places(p, n, place_ref):
    axis, bits = order_of(p)[n]
    pos = place_ref[1] if axis == "z" else place_ref[2]
    seen = [b for name, b in order_of(p)[:n] if name == axis]
    offsets = [0] + seen
    return [pos ^ o for o in offsets], [pos ^ bits ^ o for o in offsets]


def part_of(ref, dim, i, lot):
    return ref.at[i, :, lot] if dim == 0 else ref.at[:, i, lot]


def pack_kernel(place_ref, *refs, n, lot):
    owns, recvs, outs, sem = refs[:4], refs[4:8], refs[8:12], refs[12]
    copies = []
    for p in range(4):
        dim = axis_dim(order_of(p)[n][0])
        own_at, recv_at = places(p, n, place_ref)
        if len(own_at) == 1:
            own_at, recv_at = [0], [1]
        for src, at in ((owns[p], own_at), (recvs[p], recv_at)):
            for i, j in enumerate(at):
                source = part_of(src, dim, i, lot)
                target = part_of(outs[p], dim, j, slice(None))
                copies.append(pltpu.make_async_copy(source, target, sem.at[len(copies)]))
    for copy in copies:
        copy.start()
    for copy in copies:
        copy.wait()


def pack(place, owns, recvs, n, lot):
    shapes = []
    for p in range(4):
        shape = list(owns[p].shape)
        shape[axis_dim(order_of(p)[n][0])] *= 2
        shape[2] = lot.stop - lot.start
        shapes.append(jax.ShapeDtypeStruct(tuple(shape), BF))
    return pl.pallas_call(
        functools.partial(pack_kernel, n=n, lot=lot),
        out_shape=shapes,
        grid_spec=pltpu.PrefetchScalarGridSpec(
            num_scalar_prefetch=1,
            grid=(1,),
            in_specs=[ANY] * 8,
            out_specs=[pl.BlockSpec(a.shape, lambda i, s: (0, 0, 0, 0, 0)) for a in shapes],
            scratch_shapes=[pltpu.SemaphoreType.DMA((16,))],
        ),
        compiler_params=params(1),
        cost_estimate=cost(0, 8 << 20),
        name="pack",
    )(place, *(in_hbm(*owns, *recvs) if n == 2 else (*owns, *recvs)))


def swap_all(owns, n):
    return [swap(owns[p], *order_of(p)[n]) for p in range(4)]


def copy_weights(pieces, m, place_ref, buf, sem):
    for p in range(4):
        dim = axis_dim(order_of(p)[3][0])
        own_at, recv_at = places(p, 3, place_ref)
        for src, at in ((pieces[p], own_at), (pieces[p + 4], recv_at)):
            for i, j in enumerate(at):
                target = buf.at[p * 4 + j] if dim == 0 else buf.at[pl.ds(p * 4, 4), j]
                pltpu.make_async_copy(part_of(src, dim, i, m), target, sem).start()


def wait_weights(buf, sem):
    pltpu.make_async_copy(buf, buf, sem).wait()


def mix_kernel(place_ref, count_ref, *refs, d, length):
    hid_ref, mu_ref, narrow_ref = refs[:3]
    refs = refs[3:]
    if d > 0:
        low_in, refs = refs[0], refs[2:]
    if d == 3:
        widen_ref, speed_ref, refs = refs[0], refs[1], refs[2:]
    x_ref, low_ref, cur_ref, step_ref = refs
    i = pl.program_id(0)
    rows = cur_ref.shape[0]
    slots = hid_ref.shape[0] - rows
    tokens = rows - slots

    @pl.when(i == 0)
    def _():
        cur = hid_ref[:rows].astype(F32)
        cur_ref[...] = cur
        seq = cur[:tokens]
        at = lax.broadcasted_iota(jnp.int32, seq.shape, 0)
        before = jnp.where((at & (length - 1)) == 0, 0.0, pltpu.roll(seq, 1, 0))
        step_ref[:tokens] = before - seq
        step_ref[tokens:] = hid_ref[rows:].astype(F32) - cur[tokens:]

    mixed = (cur_ref[...] + step_ref[...] * mu_ref[pl.ds(i, 1), :]).astype(BF)
    x_ref[0] = mixed

    @pl.when(i == 3)
    def _():
        low = lax.dot_general(
            mixed, narrow_ref[...], (((1,), (1,)), ((), ())), preferred_element_type=F32
        )
        if d > 0:
            low = low + low_in[...]
        if d < 3:
            low_ref[...] = low
        else:
            lowrank = jnp.tanh(low).astype(BF)
            rate = jnp.exp(jnp.dot(lowrank, widen_ref[...], preferred_element_type=F32))
            log_decay = -speed_ref[...] * rate
            at = lax.broadcasted_iota(jnp.int32, (rows, 512), 0)
            limit = jnp.where(
                at < length,
                count_ref[0],
                jnp.where(at < 2 * length, count_ref[1] + length, rows),
            )
            low_ref[...] = jnp.where(at < limit, log_decay, 0.0)


def mix(place, counts, hidden, d, mu, narrow, low, held, widen, speed, slots, length):
    rows = hidden.shape[0] - slots
    once = lambda i, s, c: (0, 0)
    args = [hidden] + in_hbm(mu, narrow)
    specs = [
        pl.BlockSpec(hidden.shape, once),
        pl.BlockSpec((5, 512), lambda i, s, c: (0, s[0] ^ d)),
        pl.BlockSpec((64, 512), lambda i, s, c: (0, s[0] ^ d)),
    ]
    alias = {}
    if d > 0:
        args += [low, held]
        specs += [pl.BlockSpec(low.shape, once), ANY]
        alias = {6: 0}
    wide = 64
    if d == 3:
        args += in_hbm(widen, speed)
        specs += [pl.BlockSpec(widen.shape, once), pl.BlockSpec(speed.shape, once)]
        wide = 512
    return pl.pallas_call(
        functools.partial(mix_kernel, d=d, length=length),
        out_shape=(
            jax.ShapeDtypeStruct((5, rows, 2048), BF),
            jax.ShapeDtypeStruct((rows, wide), F32),
        ),
        grid_spec=pltpu.PrefetchScalarGridSpec(
            num_scalar_prefetch=2,
            grid=(5,),
            in_specs=specs,
            out_specs=(
                pl.BlockSpec((1, rows, 512), lambda i, s, c: (i, 0, d)),
                pl.BlockSpec((rows, wide), once),
            ),
            scratch_shapes=[pltpu.VMEM((rows, 512), F32), pltpu.VMEM((rows, 512), F32)],
        ),
        input_output_aliases=alias,
        compiler_params=params(1),
        cost_estimate=cost(20 * rows * 512, 12 * rows * 512),
        name="mix",
    )(place, counts, *args)


def rkv_kernel(place_ref, x_ref, *refs):
    pieces = refs[:8]
    out_ref, buf, sem = refs[8:]
    i, j = pl.program_id(0), pl.program_id(1)
    slot = lax.rem(i, 2)

    @pl.when(jnp.logical_and(i == 0, j == 0))
    def _():
        copy_weights(pieces, 0, place_ref, buf.at[0], sem.at[0])

    @pl.when(j == 0)
    def _():
        @pl.when(i < 2)
        def _():
            copy_weights(pieces, i + 1, place_ref, buf.at[1 - slot], sem.at[1 - slot])

        wait_weights(buf.at[slot], sem.at[slot])

    w = buf[slot].reshape(2048, 512)
    out_ref[0] = jnp.dot(x_ref[0], w, preferred_element_type=F32).astype(out_ref.dtype)


def project_rkv(place, mixed, pieces, tile):
    rows = mixed.shape[1]
    return pl.pallas_call(
        rkv_kernel,
        out_shape=jax.ShapeDtypeStruct((3, rows, 512), BF),
        grid_spec=pltpu.PrefetchScalarGridSpec(
            num_scalar_prefetch=1,
            grid=(3, rows // tile),
            in_specs=[pl.BlockSpec((1, tile, 2048), lambda i, j, s: (i, j, 0))] + [ANY] * 8,
            out_specs=pl.BlockSpec((1, tile, 512), lambda i, j, s: (i, j, 0)),
            scratch_shapes=[
                pltpu.VMEM((2, 16, 4, 32, 512), BF),
                pltpu.SemaphoreType.DMA((2,)),
            ],
        ),
        compiler_params=params(2),
        cost_estimate=cost(6 * rows * 2048 * 512, 24 << 20),
        name="project_rkv",
    )(place, mixed, *pieces)


def gate_kernel(place_ref, x_ref, *refs):
    pieces = refs[:8]
    out_ref, buf, sem = refs[8:]

    @pl.when(pl.program_id(0) == 0)
    def _():
        copy_weights(pieces, 0, place_ref, buf, sem)
        wait_weights(buf, sem)

    total = jnp.dot(x_ref[0], buf[...].reshape(2048, 512), preferred_element_type=F32)
    out_ref[...] = (total / (1.0 + jnp.exp(-total))).astype(out_ref.dtype)


def project_gate(place, mixed, pieces, tile):
    rows = mixed.shape[1]
    return pl.pallas_call(
        gate_kernel,
        out_shape=jax.ShapeDtypeStruct((rows, 512), BF),
        grid_spec=pltpu.PrefetchScalarGridSpec(
            num_scalar_prefetch=1,
            grid=(rows // tile,),
            in_specs=[pl.BlockSpec((1, tile, 2048), lambda j, s: (4, j, 0))] + [ANY] * 8,
            out_specs=pl.BlockSpec((tile, 512), lambda j, s: (j, 0)),
            scratch_shapes=[pltpu.VMEM((16, 4, 32, 512), BF), pltpu.SemaphoreType.DMA(())],
        ),
        compiler_params=params(1),
        cost_estimate=cost(2 * rows * 2048 * 512, 8 << 20),
        name="project_gate",
    )(place, mixed, *pieces)


def result_kernel(place_ref, count_ref, spot_ref, *refs, spans, t0, slot0, chained):
    lots = len(spans)
    xs, pieces = refs[: 4 * lots], refs[4 * lots : 4 * lots + 8]
    rest = refs[4 * lots + 8 + (2 if chained else 0) :]
    out_ref, slot_ref, buf, sem = rest
    copy_weights(pieces, 1, place_ref, buf, sem)
    wait_weights(buf, sem)
    start = slot = 0
    for lot, span in enumerate(spans):
        total = None
        for d in range(4):
            w = buf[4 * d : 4 * d + 4].reshape(512, 512)
            term = jnp.dot(xs[4 * lot + d][...], w, preferred_element_type=F32)
            total = term if total is None else total + term
        at = lax.broadcasted_iota(jnp.int32, (span, 512), 0) + (t0 + start)
        for p in range(2):
            own = jnp.where(at < count_ref[p], total[p * span : (p + 1) * span], 0.0)
            out_ref[p, start : start + span] = own.astype(out_ref.dtype)
        start += span
        more = total.shape[0] - 2 * span
        which = lax.broadcasted_iota(jnp.int32, (more, 512), 0) + (slot0 + slot)
        taken = jnp.logical_or(
            which == slot_of(place_ref, spot_ref, 0), which == slot_of(place_ref, spot_ref, 1)
        )
        own = jnp.where(taken, 0.0, total[2 * span :])
        slot_ref[slot : slot + more] = own.astype(slot_ref.dtype)
        slot += more


def project_result(place, counts, spots, xs, pieces, spans, t0, earlier, length, all_slots):
    span = sum(spans)
    slots = sum(xs[4 * n].shape[0] - 2 * spans[n] for n in range(len(spans)))
    once = lambda i, *s: (0, 0)
    chained = earlier is not None
    block = t0 // span
    return pl.pallas_call(
        functools.partial(
            result_kernel, spans=spans, t0=t0, slot0=block * slots, chained=chained
        ),
        out_shape=[
            jax.ShapeDtypeStruct((2, length, 512), BF),
            jax.ShapeDtypeStruct((all_slots, 512), BF),
        ],
        grid_spec=pltpu.PrefetchScalarGridSpec(
            num_scalar_prefetch=3,
            grid=(1,),
            in_specs=[pl.BlockSpec(a.shape, once) for a in xs] + [ANY] * (10 if chained else 8),
            out_specs=[
                pl.BlockSpec((2, span, 512), lambda i, *s: (0, block, 0)),
                pl.BlockSpec((slots, 512), lambda i, *s: (block, 0)),
            ],
            scratch_shapes=[pltpu.VMEM((16, 4, 32, 512), BF), pltpu.SemaphoreType.DMA(())],
        ),
        input_output_aliases={3 + len(xs) + 8: 0, 3 + len(xs) + 9: 1} if chained else {},
        compiler_params=params(1),
        cost_estimate=cost(4 * span * 2048 * 512, 8 << 20),
        name="project_result",
    )(place, counts, spots, *xs, *in_hbm(*pieces), *(earlier if chained else []))


SLOT_BLOCK = 8


def head_mask(value):
    row = lax.broadcasted_iota(jnp.int32, (128, 128), 0) < 64
    col = lax.broadcasted_iota(jnp.int32, (128, 128), 1) < 64
    return jnp.where(row == col, value, 0.0).astype(BF)


def in_two(a):
    hi = a.astype(BF)
    return jnp.concatenate([hi, (a - hi.astype(F32)).astype(BF)], axis=1)


def turn_decode(r_ref, k_ref, w_ref, rt_ref, kt_ref, dt_ref):
    r = r_ref[0].astype(F32)
    k = k_ref[0].astype(F32)
    decay = jnp.exp(w_ref[...])
    for q in range(4):
        cols = slice(128 * q, 128 * q + 128)

        def turned(a):
            t = jnp.transpose(a[:, cols])
            return jnp.concatenate([t[:64], t[64:]], axis=1)

        rt_ref[q] = turned(r).astype(BF)
        kt_ref[q] = turned(k).astype(BF)
        dt_ref[q] = in_two(turned(decay))


def decode_slots(
    first, keep_ref, s_ref, r_ref, k_ref, v_ref, g_ref, vec_ref, next_ref, rt_ref, kt_ref, dt_ref,
    y_ref,
):
    here = pl.ds(pl.multiple_of(first, SLOT_BLOCK), SLOT_BLOCK)
    v = v_ref[0, here].astype(F32)
    row = lax.broadcasted_iota(jnp.int32, (128, 128), 0)
    low = lax.broadcasted_iota(jnp.int32, (128, 128), 1) < 64
    for s in range(SLOT_BLOCK):
        slot = first + s
        hit = row == jnp.where(low, slot, slot + 64)
        pick = jnp.where(hit, 1.0, 0.0).astype(BF)
        kept = jnp.where(hit, kept_of(keep_ref, slot), 0.0).astype(BF)
        r_b = jnp.dot(rt_ref[...].reshape(256, 128), kept, preferred_element_type=F32)
        k_b = jnp.dot(kt_ref[...].reshape(256, 128), pick, preferred_element_type=F32)
        d_b = jnp.dot(
            dt_ref[...].reshape(256, 256),
            jnp.concatenate([kept, kept], axis=0),
            preferred_element_type=F32,
        )
        for q in range(4):
            span = slice(64 * q, 64 * q + 64)
            cols = slice(128 * q, 128 * q + 128)
            state = jnp.concatenate([s_ref[s, 2 * q], s_ref[s, 2 * q + 1]], axis=1)
            after_it = d_b[span] * state + k_b[span] * v[s : s + 1, cols]
            next_ref[s, 2 * q] = after_it[:, :64]
            next_ref[s, 2 * q + 1] = after_it[:, 64:]
            y_ref[s : s + 1, cols] = jnp.sum(r_b[span] * state, axis=0, keepdims=True)
    r = r_ref[0, here].astype(F32)
    k = k_ref[0, here].astype(F32)
    reward, scale, offset = vec_ref[0:1], vec_ref[1:2], vec_ref[2:3]
    own = r * reward * k
    ones = jnp.concatenate([head_mask(1.0)] * 2, axis=0)
    mean_of = jnp.concatenate([head_mask(1.0 / 64)] * 2, axis=0)
    out = []
    for q in range(4):
        cols = slice(128 * q, 128 * q + 128)
        total = jnp.dot(in_two(own[:, cols]), ones, preferred_element_type=F32)
        y = y_ref[:, cols] + total * v[:, cols]
        center = y - jnp.dot(in_two(y), mean_of, preferred_element_type=F32)
        spread = jnp.dot(in_two(center * center), mean_of, preferred_element_type=F32)
        normed = center * lax.rsqrt(spread + NORM_EPS) * scale[:, cols] + offset[:, cols]
        out.append((normed * g_ref[here, cols].astype(F32)).astype(BF))
    return jnp.concatenate(out, axis=1)


def place_kernel(place_ref, spot_ref, final_ref, _, state_ref, sem):
    copies = [
        pltpu.make_async_copy(
            final_ref.at[p], state_ref.at[slot_of(place_ref, spot_ref, p)], sem.at[p]
        )
        for p in range(2)
    ]
    for copy in copies:
        copy.start()
    for copy in copies:
        copy.wait()


def place_states(place, spots, final, states):
    return pl.pallas_call(
        place_kernel,
        out_shape=jax.ShapeDtypeStruct(states.shape, F32),
        grid_spec=pltpu.PrefetchScalarGridSpec(
            num_scalar_prefetch=2,
            grid=(1,),
            in_specs=[pl.BlockSpec(final.shape, lambda i, *s: (0, 0, 0, 0)), ANY],
            out_specs=ANY,
            scratch_shapes=[pltpu.SemaphoreType.DMA((2,))],
        ),
        input_output_aliases={3: 0},
        compiler_params=params(1),
        cost_estimate=cost(0, 2 << 20),
        name="place_states",
    )(place, spots, final, states)


def span_tables():
    t = np.arange(CH)
    blocks = []
    size = 4
    while size <= CH:
        start = (t // size) * size
        mid = start + size // 2
        m = np.zeros((CH, CH), np.float32)
        for i in range(CH):
            if i >= mid[i]:
                m[i, mid[i] : i] = 1.0
            else:
                m[i, i + 1 : mid[i]] = 1.0
        blocks.append(m)
        size *= 2
    before = (t[None, :] < t[:, None]).astype(np.float32)
    after = (t[None, :] > t[:, None]).astype(np.float32)
    whole = np.ones((8, CH), np.float32)
    table = np.concatenate(blocks + [before, after, whole])
    return np.concatenate([table, table], axis=1)


LEVELS = int(np.log2(CH))


def wkv_kernel(
    count_ref, keep_ref, table_ref, *refs, t0, span, slot0, last, chained, prompts
):
    ins, refs = refs[: 5 * prompts], refs[5 * prompts :]
    vec_ref, start_ref, slots_ref, rd_ref, kd_ref, vd_ref, wd_ref, gd_ref = refs[:8]
    refs = refs[9:] if chained else refs[8:]
    out_ref, state_ref, next_ref = refs[:3]
    turned = refs[-4:-1]
    y_ref = refs[-1]
    c = pl.program_id(0)

    @pl.when(c == 0)
    def _():
        state_ref[...] = start_ref[...]
        turn_decode(rd_ref, kd_ref, wd_ref, *turned)

    table = table_ref[...]
    row = lax.broadcasted_iota(jnp.int32, (CH, 512), 0)
    low = lax.broadcasted_iota(jnp.int32, (CH, 128), 1) < 64
    arow = lax.broadcasted_iota(jnp.int32, (CH, 2 * CH), 0)
    acol = lax.broadcasted_iota(jnp.int32, (CH, 2 * CH), 1) & (CH - 1)
    diff = arow ^ acol
    causal = arow > acol
    same_head = (lax.broadcasted_iota(jnp.int32, (128, 128), 0) < 64) == (
        lax.broadcasted_iota(jnp.int32, (128, 128), 1) < 64
    )
    mean_of = head_mask(1.0 / 64)
    mean_two = jnp.concatenate([mean_of, mean_of], axis=0)
    reward, scale, offset = vec_ref[0:1], vec_ref[1:2], vec_ref[2:3]
    contract_lanes = (((1,), (1,)), ((), ()))
    contract_rows = (((0,), (0,)), ((), ()))

    def both_heads(a):
        zero = jnp.zeros_like(a)
        return jnp.concatenate([jnp.where(low, a, zero), jnp.where(low, zero, a)], axis=0)

    def lanes_dot(a, b):
        return lax.dot_general(a, b, contract_lanes, preferred_element_type=F32)

    def dot(a, b):
        return jnp.dot(a, b, preferred_element_type=F32)

    streams = [(p, q) for p in range(prompts) for q in range(4)]
    cols = [slice(128 * q, 128 * q + 128) for q in range(4)]
    keys, own, mixed, r_dec, k_dec, whole, values = {}, {}, {}, {}, {}, {}, {}
    for p in range(prompts):
        r_ref, k_ref, v_ref, w_ref, g_ref = ins[5 * p : 5 * p + 5]
        live = (row + (c * CH + t0)) < count_ref[p]
        r = r_ref[0].astype(F32)
        k = jnp.where(live, k_ref[0].astype(F32), 0.0)
        values[p] = v_ref[0]
        w = w_ref[...]
        w_hi = w.astype(BF)
        w_lo = (w - w_hi.astype(F32)).astype(BF)
        factors = jnp.exp(dot(table, jnp.concatenate([w_hi, w_lo], axis=0)))
        r_dec[p] = (r * factors[(LEVELS - 1) * CH : LEVELS * CH]).astype(BF)
        k_dec[p] = (k * factors[LEVELS * CH : (LEVELS + 1) * CH]).astype(BF)
        whole[p] = factors[(LEVELS + 1) * CH : (LEVELS + 1) * CH + 1]
        weighted = r * reward
        hi = weighted.astype(BF)
        own[p] = (hi, (weighted - hi.astype(F32)).astype(BF))
        keys[p] = k.astype(BF)
        mixed[p] = [jnp.where((row & 1) == 1, r, k).astype(BF)]
        for level in range(1, LEVELS):
            pick = jnp.where((row & (1 << level)) != 0, r, k)
            mixed[p].append((pick * factors[(level - 1) * CH : level * CH]).astype(BF))
    scores = {}
    for p, q in streams:
        key = both_heads(keys[p][:, cols[q]])
        s = lanes_dot(
            jnp.concatenate([half[:, cols[q]] for half in own[p]], axis=1),
            jnp.concatenate([key, key], axis=1),
        )
        scores[p, q] = jnp.where(diff == 0, s, 0.0)
    for level in range(LEVELS):
        here = jnp.logical_and(causal, (diff >> level) == 1)
        for p, q in streams:
            a = mixed[p][level][:, cols[q]]
            scores[p, q] = jnp.where(here, lanes_dot(a, both_heads(a)), scores[p, q])
    y = {}
    for p, q in streams:
        v = values[p][:, cols[q]]
        state = state_ref[p, q]
        y[p, q] = dot(scores[p, q].astype(BF), both_heads(v)) + lanes_dot(
            r_dec[p][:, cols[q]], state.astype(BF)
        )
        added = lax.dot_general(v, k_dec[p][:, cols[q]], contract_rows, preferred_element_type=F32)
        state_ref[p, q] = state * whole[p][:, cols[q]] + jnp.where(same_head, added, 0.0)
    center = {n: y[n] - dot(in_two(y[n]), mean_two) for n in streams}
    spread = {n: dot((center[n] * center[n]).astype(BF), mean_of) for n in streams}
    for p, q in streams:
        normed = center[p, q] * lax.rsqrt(spread[p, q] + NORM_EPS)
        gate = ins[5 * p + 4][:, cols[q]].astype(F32)
        at = pl.multiple_of(p * span + c * CH, CH)
        out_ref[pl.ds(at, CH), cols[q]] = (
            (normed * scale[:, cols[q]] + offset[:, cols[q]]) * gate
        ).astype(out_ref.dtype)

    done = decode_slots(
        slot0 + c * SLOT_BLOCK, keep_ref, slots_ref, rd_ref, kd_ref, vd_ref, gd_ref, vec_ref,
        next_ref, *turned, y_ref,
    )
    at = pl.multiple_of(prompts * span + c * SLOT_BLOCK, SLOT_BLOCK)
    out_ref[pl.ds(at, SLOT_BLOCK), :] = done

    if last:
        final_ref = refs[3]

        @pl.when(c == pl.num_programs(0) - 1)
        def _():
            for p, q in streams:
                whole_state = jnp.transpose(state_ref[p, q])
                final_ref[p, 2 * q] = whole_state[:64, :64]
                final_ref[p, 2 * q + 1] = whole_state[64:, 64:]


def wkv(counts, keep, rkv, log_decay, gate, vectors, start, states, earlier, t0, t1, length):
    prompts, slots = start.shape[0], states.shape[0]
    table = jnp.asarray(span_tables(), BF)
    c0, per, span = t0 // CH, length // CH, t1 - t0
    chunks = span // CH
    last, chained = t1 == length, earlier is not None
    at = prompts * length // slots

    def part(n, p):
        return pl.BlockSpec((1, CH, 512), lambda c, s, k: (n, p * per + c + c0, 0))

    def flat(p):
        return pl.BlockSpec((CH, 512), lambda c, s, k: (p * per + c + c0, 0))

    def slot_part(n):
        return pl.BlockSpec((1, slots, 512), lambda c, s, k: (n, at, 0))

    slot_flat = pl.BlockSpec((slots, 512), lambda c, s, k: (at, 0))
    big = pl.BlockSpec((SLOT_BLOCK, 8, 64, 64), lambda c, s, k: (c + c0, 0, 0, 0))
    held = pl.BlockSpec((prompts, 4, 128, 128), lambda c, s, k: (0, 0, 0, 0))
    rows = prompts * span + chunks * SLOT_BLOCK
    out_shape = [
        jax.ShapeDtypeStruct((rows, 512), BF),
        jax.ShapeDtypeStruct((prompts, 4, 128, 128), F32),
        jax.ShapeDtypeStruct(states.shape, F32),
    ]
    out_specs = [pl.BlockSpec((rows, 512), lambda c, s, k: (0, 0)), held, big]
    if last:
        out_shape.append(jax.ShapeDtypeStruct((prompts, 8, 64, 64), F32))
        out_specs.append(pl.BlockSpec((prompts, 8, 64, 64), lambda c, s, k: (0, 0, 0, 0)))
    ins, specs = [], []
    for p in range(prompts):
        ins += [rkv, rkv, rkv, log_decay, gate]
        specs += [part(0, p), part(1, p), part(2, p), flat(p), flat(p)]
    ins += [vectors, start, states, rkv, rkv, rkv, log_decay, gate]
    specs += [pl.BlockSpec((8, 512), lambda c, s, k: (0, 0)), held, big]
    specs += [slot_part(0), slot_part(1), slot_part(2), slot_flat, slot_flat]
    alias = {}
    if chained:
        ins.append(earlier)
        specs.append(ANY)
        alias = {2 + len(ins): 2}
    return pl.pallas_call(
        functools.partial(
            wkv_kernel,
            t0=t0,
            span=span,
            slot0=c0 * SLOT_BLOCK,
            last=last,
            chained=chained,
            prompts=prompts,
        ),
        out_shape=out_shape,
        grid_spec=pltpu.PrefetchScalarGridSpec(
            num_scalar_prefetch=2,
            grid=(chunks,),
            in_specs=[pl.BlockSpec(table.shape, lambda c, s, k: (0, 0))] + specs,
            out_specs=out_specs,
            scratch_shapes=[
                pltpu.VMEM((4, 64, 128), BF),
                pltpu.VMEM((4, 64, 128), BF),
                pltpu.VMEM((4, 64, 256), BF),
                pltpu.VMEM((SLOT_BLOCK, 512), F32),
            ],
        ),
        input_output_aliases=alias,
        compiler_params=params(1),
        cost_estimate=cost(span * 80_000_000, span << 17),
        name="wkv",
    )(counts, keep, table, *ins)


def on_device(
    learner_acceptance_matrix,
    learner_address_matrix,
    learner_content_matrix,
    learner_gating_matrix,
    learner_result_matrix,
    fading_narrowing_matrix,
    fading_widening_matrix,
    feature_fading_speed,
    current_reward,
    symbol_blending_factors,
    group_scaling_factor,
    group_scaling_offset,
    request_hidden_entries,
    request_valid_count,
    request_destination_place,
    newest_symbol_hidden,
    preceding_hidden_entry,
    place_memory_matrix,
    place_newness_marks,
):
    h = lax.axis_index("yh") * 2 + lax.axis_index("core")
    z, x, yl = lax.axis_index("z"), lax.axis_index("x"), lax.axis_index("yl")
    place = jnp.stack([h, z, x, yl]).astype(jnp.int32)
    prompts, length, width = request_hidden_entries.shape
    slots, groups, breadth = place_memory_matrix.shape[:3]
    tokens = prompts * length
    rows = tokens + slots
    counts = request_valid_count

    spots = request_destination_place
    parts, own, new_shift = split(
        place,
        place_newness_marks,
        counts,
        spots,
        [
            learner_acceptance_matrix,
            learner_address_matrix,
            learner_content_matrix,
            learner_gating_matrix,
            learner_result_matrix,
        ],
        request_hidden_entries.reshape(tokens, width),
        newest_symbol_hidden,
        preceding_hidden_entry,
    )
    blocks = [parts[0]] + [swap(parts[d], "head", d) for d in (1, 2, 3)]
    side = swap(own, "head", 1)
    far = swap(after(own, blocks[3]), "head", 2)
    stacked = jnp.stack(blocks)
    neighbour = swap(stacked, "yl", 1)
    far_side = swap(far, "head", 1)

    def mixes(piece, d, mixed, low):
        return mix(
            place,
            counts,
            piece,
            d,
            symbol_blending_factors,
            fading_narrowing_matrix.T,
            low,
            mixed,
            fading_widening_matrix,
            feature_fading_speed[None],
            slots,
            length,
        )

    every, first, second = slice(0, 5), slice(0, 3), slice(3, 5)
    mixed, low = mixes(own, 0, None, None)
    neighbour, side, low = lax.optimization_barrier((neighbour, side, low))
    by_row = in_order(stacked, neighbour, yl)
    held = [by_row[p][None, None] for p in range(4)]
    recv = swap_all(held, 0)
    held = pack(place, held, recv, 0, every)
    recv = swap_all(held, 1)
    mixed, low = mixes(side, 1, mixed, low)
    held = pack(place, held, after(recv, low), 1, every)
    recv = swap_all(held, 2)
    mixed, low = mixes(far, 2, mixed, low)
    recv = after(recv, low)
    early = pack(place, held, recv, 2, first)
    early_recv = swap_all(early, 3)
    mixed, log_decay = mixes(far_side, 3, mixed, low)
    late = pack(place, held, after(recv, log_decay), 2, second)
    early_recv = after(early_recv, log_decay)
    late_recv = swap_all(after(late, early_recv), 3)
    early = list(early) + early_recv
    late = list(late) + late_recv

    rkv = project_rkv(place, mixed, early, rows)
    gate = project_gate(place, mixed, late, rows // 2)
    small = jnp.stack([current_reward, group_scaling_factor, group_scaling_offset])
    vectors = jnp.concatenate([small, jnp.zeros((5, width), F32)])
    state = jnp.zeros((prompts, groups // 2, 128, 128), F32)
    sent = []
    t0 = 0
    new_state = None
    for t1 in (256, 384, 512):
        out = wkv(
            counts,
            place_newness_marks,
            rkv,
            log_decay,
            gate,
            vectors,
            state,
            place_memory_matrix,
            new_state,
            t0,
            t1,
            length,
        )
        normed, state, new_state = out[:3]
        n_side = swap(normed, "head", 1)
        n_far = swap(normed, "head", 2)
        if t1 == length:
            result = project_result(
                place, counts, spots, sent[0], late, (256,), 0, None, length, slots
            )
            n_far = after(n_far, result[1])
        n_far_side = swap(n_far, "head", 1)
        sent.append([normed, n_side, n_far, n_far_side])
        t0 = t1
    prompt_hidden, decode_hidden = project_result(
        place, counts, spots, sent[1] + sent[2], late, (128, 128), 256, result, length, slots
    )
    final_state = out[3]
    new_state = place_states(place, spots, final_state, new_state)
    return (prompt_hidden, decode_hidden, new_state, new_shift)


def solution(mesh):
    split = Mesh(mesh.devices.reshape(2, 2, 4, 4, 2), ("yh", "core", "z", "x", "yl"))
    head = ("yh", "core")
    req = ("z", "x", "yl")
    row_shard = P(head + req, None)
    in_specs = (
        row_shard,
        row_shard,
        row_shard,
        row_shard,
        row_shard,
        P(),
        P(None, head),
        P(head),
        P(head),
        P(),
        P(head),
        P(head),
        P(req, None, head),
        P(req),
        P(req),
        P(req, head),
        P(req, head),
        P(req, head, None, None),
        P(req),
    )
    out_specs = (
        P(req, None, head),
        P(req, head),
        P(req, head, None, None),
        P(req, head),
    )
    return jax.shard_map(
        on_device, mesh=split, in_specs=in_specs, out_specs=out_specs, check_vma=False
    )
```

```python
import functools

import jax
import jax.numpy as jnp
import numpy as np
from jax import lax
from jax.experimental import pallas as pl
from jax.experimental.pallas import tpu as pltpu
from jax.sharding import Mesh
from jax.sharding import PartitionSpec as P

NORM_EPS = 0.00064
N_HEAD = 4
CH = 64
BF = jnp.bfloat16
F32 = jnp.float32


STEPS = (("x", 1), ("z", 1), ("x", 3), ("z", 3))


def swap(a, axes, bits):
    sizes = {"x": 4, "z": 4, "yl": 2, "head": 4}
    names = ("yh", "core") if axes == "head" else axes
    return lax.ppermute(a, names, [(i, i ^ bits) for i in range(sizes[axes])])


def order_of(part):
    return [STEPS[(part + n) % 4] for n in range(4)]


def after(value, other):
    return lax.optimization_barrier((value, other))[0]


ANY = pl.BlockSpec(memory_space=pl.ANY)


def in_hbm(*arrays):
    return [pltpu.with_memory_space_constraint(a, pltpu.HBM) for a in arrays]


def cost(flops, nbytes, trans=0):
    return pl.CostEstimate(flops=flops, bytes_accessed=nbytes, transcendentals=trans)


def params(axes):
    return pltpu.CompilerParams(
        dimension_semantics=("arbitrary",) * axes, vmem_limit_bytes=48 << 20
    )


def kept_of(fresh_ref, n):
    return jnp.where(fresh_ref[n] == 1, 0.0, 1.0)


def slot_of(place_ref, spot_ref, p):
    return spot_ref[p] - (place_ref[1] * 8 + place_ref[2] * 2 + place_ref[3]) * 64


def split_kernel(place_ref, keep_ref, count_ref, spot_ref, *refs):
    mats, hid, newest, prior = refs[:5], refs[5], refs[6], refs[7]
    outs, own_ref, shift_ref = refs[8:12], refs[12], refs[13]
    buf, old, sem = refs[14:]
    tokens, slots = hid.shape[0], newest.shape[0]
    copies = [pltpu.make_async_copy(mats[m], buf.at[m], sem.at[m]) for m in range(5)]
    copies += [
        pltpu.make_async_copy(prior, old, sem.at[5]),
        pltpu.make_async_copy(newest, own_ref.at[pl.ds(tokens, slots)], sem.at[6]),
        pltpu.make_async_copy(hid, own_ref.at[pl.ds(0, tokens)], sem.at[7]),
    ]
    for copy in copies:
        copy.start()
    row = lax.broadcasted_iota(jnp.int32, (slots, 512), 0)
    keep = jnp.zeros((slots, 512), F32)
    for n in range(slots):
        keep = jnp.where(row == n, kept_of(keep_ref, n), keep)
    for m in range(5):
        copies[m].wait()
    for d in range(4):
        at = pl.multiple_of((place_ref[0] ^ d) * 512, 512)
        for m in range(5):
            outs[d][m] = buf[m, :, pl.ds(at, 512)].astype(BF)
    copies[5].wait()
    kept = jnp.where(keep > 0.5, old[...].astype(F32), 0.0)
    own_ref[tokens + slots :] = kept.astype(BF)
    copies[6].wait()
    copies[7].wait()
    shift = own_ref[tokens : tokens + slots].astype(F32)
    few = lax.broadcasted_iota(jnp.int32, (16, 512), 0)
    for p in range(2):
        at = p * (tokens // 2) + count_ref[p] - 1
        base = pl.multiple_of((at >> 4) << 4, 16)
        near = own_ref[pl.ds(base, 16)].astype(F32)
        last = jnp.sum(jnp.where(few == (at & 15), near, 0.0), axis=0, keepdims=True)
        shift = jnp.where(row == slot_of(place_ref, spot_ref, p), last, shift)
    shift_ref[...] = shift.astype(BF)


def split(place, keep, counts, spots, matrices, hidden, newest, prior):
    rows, width = matrices[0].shape[0], matrices[0].shape[1] // N_HEAD
    shape = (len(matrices), rows, width)
    total = hidden.shape[0] + 2 * newest.shape[0]
    hbm = pl.BlockSpec(memory_space=pltpu.HBM)
    out = pl.pallas_call(
        split_kernel,
        out_shape=[jax.ShapeDtypeStruct(shape, BF)] * 4
        + [jax.ShapeDtypeStruct((total, width), BF), jax.ShapeDtypeStruct(newest.shape, BF)],
        grid_spec=pltpu.PrefetchScalarGridSpec(
            num_scalar_prefetch=4,
            grid=(1,),
            in_specs=[hbm] * 8,
            out_specs=[pl.BlockSpec(shape, lambda i, *s: (0, 0, 0))] * 4
            + [
                pl.BlockSpec((total, width), lambda i, *s: (0, 0)),
                pl.BlockSpec(newest.shape, lambda i, *s: (0, 0)),
            ],
            scratch_shapes=[
                pltpu.VMEM((5,) + matrices[0].shape, F32),
                pltpu.VMEM(newest.shape, BF),
                pltpu.SemaphoreType.DMA((8,)),
            ],
        ),
        compiler_params=params(1),
        name="split",
    )(place, keep, counts, spots, *in_hbm(*matrices, hidden, newest, prior))
    return out[:4], out[4], out[5]


def in_order(own, other, yl):
    first = yl == 0
    return jnp.concatenate(
        [jnp.where(first, own, other), jnp.where(first, other, own)], axis=-2
    )


def axis_dim(axis):
    return 0 if axis == "z" else 1


def places(p, n, place_ref):
    axis, bits = order_of(p)[n]
    pos = place_ref[1] if axis == "z" else place_ref[2]
    seen = [b for name, b in order_of(p)[:n] if name == axis]
    offsets = [0] + seen
    return [pos ^ o for o in offsets], [pos ^ bits ^ o for o in offsets]


def part_of(ref, dim, i, lot):
    return ref.at[i, :, lot] if dim == 0 else ref.at[:, i, lot]


def pack_kernel(place_ref, *refs, n, lot):
    owns, recvs, outs, sem = refs[:4], refs[4:8], refs[8:12], refs[12]
    copies = []
    for p in range(4):
        dim = axis_dim(order_of(p)[n][0])
        own_at, recv_at = places(p, n, place_ref)
        if len(own_at) == 1:
            own_at, recv_at = [0], [1]
        for src, at in ((owns[p], own_at), (recvs[p], recv_at)):
            for i, j in enumerate(at):
                source = part_of(src, dim, i, lot)
                target = part_of(outs[p], dim, j, slice(None))
                copies.append(pltpu.make_async_copy(source, target, sem.at[len(copies)]))
    for copy in copies:
        copy.start()
    for copy in copies:
        copy.wait()


def pack(place, owns, recvs, n, lot):
    shapes = []
    for p in range(4):
        shape = list(owns[p].shape)
        shape[axis_dim(order_of(p)[n][0])] *= 2
        shape[2] = lot.stop - lot.start
        shapes.append(jax.ShapeDtypeStruct(tuple(shape), BF))
    return pl.pallas_call(
        functools.partial(pack_kernel, n=n, lot=lot),
        out_shape=shapes,
        grid_spec=pltpu.PrefetchScalarGridSpec(
            num_scalar_prefetch=1,
            grid=(1,),
            in_specs=[ANY] * 8,
            out_specs=[pl.BlockSpec(a.shape, lambda i, s: (0, 0, 0, 0, 0)) for a in shapes],
            scratch_shapes=[pltpu.SemaphoreType.DMA((16,))],
        ),
        compiler_params=params(1),
        cost_estimate=cost(0, 8 << 20),
        name="pack",
    )(place, *(in_hbm(*owns, *recvs) if n == 2 else (*owns, *recvs)))


def swap_all(owns, n):
    return [swap(owns[p], *order_of(p)[n]) for p in range(4)]


def copy_weights(pieces, m, place_ref, buf, sem):
    for p in range(4):
        dim = axis_dim(order_of(p)[3][0])
        own_at, recv_at = places(p, 3, place_ref)
        for src, at in ((pieces[p], own_at), (pieces[p + 4], recv_at)):
            for i, j in enumerate(at):
                target = buf.at[p * 4 + j] if dim == 0 else buf.at[pl.ds(p * 4, 4), j]
                pltpu.make_async_copy(part_of(src, dim, i, m), target, sem).start()


def wait_weights(buf, sem):
    pltpu.make_async_copy(buf, buf, sem).wait()


def mix_kernel(place_ref, count_ref, *refs, d, length):
    hid_ref, mu_ref, narrow_ref = refs[:3]
    refs = refs[3:]
    if d > 0:
        low_in, refs = refs[0], refs[2:]
    if d == 3:
        widen_ref, speed_ref, refs = refs[0], refs[1], refs[2:]
    x_ref, low_ref, cur_ref, step_ref = refs
    i = pl.program_id(0)
    rows = cur_ref.shape[0]
    slots = hid_ref.shape[0] - rows
    tokens = rows - slots

    @pl.when(i == 0)
    def _():
        cur = hid_ref[:rows].astype(F32)
        cur_ref[...] = cur
        seq = cur[:tokens]
        at = lax.broadcasted_iota(jnp.int32, seq.shape, 0)
        before = jnp.where((at & (length - 1)) == 0, 0.0, pltpu.roll(seq, 1, 0))
        step_ref[:tokens] = before - seq
        step_ref[tokens:] = hid_ref[rows:].astype(F32) - cur[tokens:]

    mixed = (cur_ref[...] + step_ref[...] * mu_ref[pl.ds(i, 1), :]).astype(BF)
    x_ref[0] = mixed

    @pl.when(i == 3)
    def _():
        low = lax.dot_general(
            mixed, narrow_ref[...], (((1,), (1,)), ((), ())), preferred_element_type=F32
        )
        if d > 0:
            low = low + low_in[...]
        if d < 3:
            low_ref[...] = low
        else:
            lowrank = jnp.tanh(low).astype(BF)
            rate = jnp.exp(jnp.dot(lowrank, widen_ref[...], preferred_element_type=F32))
            log_decay = -speed_ref[...] * rate
            at = lax.broadcasted_iota(jnp.int32, (rows, 512), 0)
            limit = jnp.where(
                at < length,
                count_ref[0],
                jnp.where(at < 2 * length, count_ref[1] + length, rows),
            )
            low_ref[...] = jnp.where(at < limit, log_decay, 0.0)


def mix(place, counts, hidden, d, mu, narrow, low, held, widen, speed, slots, length):
    rows = hidden.shape[0] - slots
    once = lambda i, s, c: (0, 0)
    args = [hidden] + in_hbm(mu, narrow)
    specs = [
        pl.BlockSpec(hidden.shape, once),
        pl.BlockSpec((5, 512), lambda i, s, c: (0, s[0] ^ d)),
        pl.BlockSpec((64, 512), lambda i, s, c: (0, s[0] ^ d)),
    ]
    alias = {}
    if d > 0:
        args += [low, held]
        specs += [pl.BlockSpec(low.shape, once), ANY]
        alias = {6: 0}
    wide = 64
    if d == 3:
        args += in_hbm(widen, speed)
        specs += [pl.BlockSpec(widen.shape, once), pl.BlockSpec(speed.shape, once)]
        wide = 512
    return pl.pallas_call(
        functools.partial(mix_kernel, d=d, length=length),
        out_shape=(
            jax.ShapeDtypeStruct((5, rows, 2048), BF),
            jax.ShapeDtypeStruct((rows, wide), F32),
        ),
        grid_spec=pltpu.PrefetchScalarGridSpec(
            num_scalar_prefetch=2,
            grid=(5,),
            in_specs=specs,
            out_specs=(
                pl.BlockSpec((1, rows, 512), lambda i, s, c: (i, 0, d)),
                pl.BlockSpec((rows, wide), once),
            ),
            scratch_shapes=[pltpu.VMEM((rows, 512), F32), pltpu.VMEM((rows, 512), F32)],
        ),
        input_output_aliases=alias,
        compiler_params=params(1),
        cost_estimate=cost(20 * rows * 512, 12 * rows * 512),
        name="mix",
    )(place, counts, *args)


def rkv_kernel(place_ref, x_ref, *refs):
    pieces = refs[:8]
    out_ref, buf, sem = refs[8:]
    i, j = pl.program_id(0), pl.program_id(1)
    slot = lax.rem(i, 2)

    @pl.when(jnp.logical_and(i == 0, j == 0))
    def _():
        copy_weights(pieces, 0, place_ref, buf.at[0], sem.at[0])

    @pl.when(j == 0)
    def _():
        @pl.when(i < 2)
        def _():
            copy_weights(pieces, i + 1, place_ref, buf.at[1 - slot], sem.at[1 - slot])

        wait_weights(buf.at[slot], sem.at[slot])

    w = buf[slot].reshape(2048, 512)
    out_ref[0] = jnp.dot(x_ref[0], w, preferred_element_type=F32).astype(out_ref.dtype)


def project_rkv(place, mixed, pieces, tile):
    rows = mixed.shape[1]
    return pl.pallas_call(
        rkv_kernel,
        out_shape=jax.ShapeDtypeStruct((3, rows, 512), BF),
        grid_spec=pltpu.PrefetchScalarGridSpec(
            num_scalar_prefetch=1,
            grid=(3, rows // tile),
            in_specs=[pl.BlockSpec((1, tile, 2048), lambda i, j, s: (i, j, 0))] + [ANY] * 8,
            out_specs=pl.BlockSpec((1, tile, 512), lambda i, j, s: (i, j, 0)),
            scratch_shapes=[
                pltpu.VMEM((2, 16, 4, 32, 512), BF),
                pltpu.SemaphoreType.DMA((2,)),
            ],
        ),
        compiler_params=params(2),
        cost_estimate=cost(6 * rows * 2048 * 512, 24 << 20),
        name="project_rkv",
    )(place, mixed, *pieces)


def gate_kernel(place_ref, x_ref, *refs):
    pieces = refs[:8]
    out_ref, buf, sem = refs[8:]

    @pl.when(pl.program_id(0) == 0)
    def _():
        copy_weights(pieces, 0, place_ref, buf, sem)
        wait_weights(buf, sem)

    total = jnp.dot(x_ref[0], buf[...].reshape(2048, 512), preferred_element_type=F32)
    out_ref[...] = (total / (1.0 + jnp.exp(-total))).astype(out_ref.dtype)


def project_gate(place, mixed, pieces, tile):
    rows = mixed.shape[1]
    return pl.pallas_call(
        gate_kernel,
        out_shape=jax.ShapeDtypeStruct((rows, 512), BF),
        grid_spec=pltpu.PrefetchScalarGridSpec(
            num_scalar_prefetch=1,
            grid=(rows // tile,),
            in_specs=[pl.BlockSpec((1, tile, 2048), lambda j, s: (4, j, 0))] + [ANY] * 8,
            out_specs=pl.BlockSpec((tile, 512), lambda j, s: (j, 0)),
            scratch_shapes=[pltpu.VMEM((16, 4, 32, 512), BF), pltpu.SemaphoreType.DMA(())],
        ),
        compiler_params=params(1),
        cost_estimate=cost(2 * rows * 2048 * 512, 8 << 20),
        name="project_gate",
    )(place, mixed, *pieces)


def result_kernel(place_ref, count_ref, spot_ref, *refs, spans, t0, slot0, chained):
    lots = len(spans)
    xs, pieces = refs[: 4 * lots], refs[4 * lots : 4 * lots + 8]
    rest = refs[4 * lots + 8 + (2 if chained else 0) :]
    out_ref, slot_ref, buf, sem = rest
    copy_weights(pieces, 1, place_ref, buf, sem)
    wait_weights(buf, sem)
    start = slot = 0
    for lot, span in enumerate(spans):
        total = None
        for d in range(4):
            w = buf[4 * d : 4 * d + 4].reshape(512, 512)
            term = jnp.dot(xs[4 * lot + d][...], w, preferred_element_type=F32)
            total = term if total is None else total + term
        at = lax.broadcasted_iota(jnp.int32, (span, 512), 0) + (t0 + start)
        for p in range(2):
            own = jnp.where(at < count_ref[p], total[p * span : (p + 1) * span], 0.0)
            out_ref[p, start : start + span] = own.astype(out_ref.dtype)
        start += span
        more = total.shape[0] - 2 * span
        which = lax.broadcasted_iota(jnp.int32, (more, 512), 0) + (slot0 + slot)
        taken = jnp.logical_or(
            which == slot_of(place_ref, spot_ref, 0), which == slot_of(place_ref, spot_ref, 1)
        )
        own = jnp.where(taken, 0.0, total[2 * span :])
        slot_ref[slot : slot + more] = own.astype(slot_ref.dtype)
        slot += more


def project_result(place, counts, spots, xs, pieces, spans, t0, earlier, length, all_slots):
    span = sum(spans)
    slots = sum(xs[4 * n].shape[0] - 2 * spans[n] for n in range(len(spans)))
    once = lambda i, *s: (0, 0)
    chained = earlier is not None
    block = t0 // span
    return pl.pallas_call(
        functools.partial(
            result_kernel, spans=spans, t0=t0, slot0=block * slots, chained=chained
        ),
        out_shape=[
            jax.ShapeDtypeStruct((2, length, 512), BF),
            jax.ShapeDtypeStruct((all_slots, 512), BF),
        ],
        grid_spec=pltpu.PrefetchScalarGridSpec(
            num_scalar_prefetch=3,
            grid=(1,),
            in_specs=[pl.BlockSpec(a.shape, once) for a in xs] + [ANY] * (10 if chained else 8),
            out_specs=[
                pl.BlockSpec((2, span, 512), lambda i, *s: (0, block, 0)),
                pl.BlockSpec((slots, 512), lambda i, *s: (block, 0)),
            ],
            scratch_shapes=[pltpu.VMEM((16, 4, 32, 512), BF), pltpu.SemaphoreType.DMA(())],
        ),
        input_output_aliases={3 + len(xs) + 8: 0, 3 + len(xs) + 9: 1} if chained else {},
        compiler_params=params(1),
        cost_estimate=cost(4 * span * 2048 * 512, 8 << 20),
        name="project_result",
    )(place, counts, spots, *xs, *in_hbm(*pieces), *(earlier if chained else []))


SLOT_BLOCK = 8


def head_mask(value):
    row = lax.broadcasted_iota(jnp.int32, (128, 128), 0) < 64
    col = lax.broadcasted_iota(jnp.int32, (128, 128), 1) < 64
    return jnp.where(row == col, value, 0.0).astype(BF)


def in_two(a):
    hi = a.astype(BF)
    return jnp.concatenate([hi, (a - hi.astype(F32)).astype(BF)], axis=1)


def turn_decode(r_ref, k_ref, w_ref, rt_ref, kt_ref, dt_ref):
    r = r_ref[0].astype(F32)
    k = k_ref[0].astype(F32)
    decay = jnp.exp(w_ref[...])
    for q in range(4):
        cols = slice(128 * q, 128 * q + 128)

        def turned(a):
            t = jnp.transpose(a[:, cols])
            return jnp.concatenate([t[:64], t[64:]], axis=1)

        rt_ref[q] = turned(r).astype(BF)
        kt_ref[q] = turned(k).astype(BF)
        dt_ref[q] = in_two(turned(decay))


def decode_slots(
    first, keep_ref, s_ref, r_ref, k_ref, v_ref, g_ref, vec_ref, next_ref, rt_ref, kt_ref, dt_ref,
    y_ref,
):
    here = pl.ds(pl.multiple_of(first, SLOT_BLOCK), SLOT_BLOCK)
    v = v_ref[0, here].astype(F32)
    row = lax.broadcasted_iota(jnp.int32, (128, 128), 0)
    low = lax.broadcasted_iota(jnp.int32, (128, 128), 1) < 64
    for s in range(SLOT_BLOCK):
        slot = first + s
        hit = row == jnp.where(low, slot, slot + 64)
        pick = jnp.where(hit, 1.0, 0.0).astype(BF)
        kept = jnp.where(hit, kept_of(keep_ref, slot), 0.0).astype(BF)
        r_b = jnp.dot(rt_ref[...].reshape(256, 128), kept, preferred_element_type=F32)
        k_b = jnp.dot(kt_ref[...].reshape(256, 128), pick, preferred_element_type=F32)
        d_b = jnp.dot(
            dt_ref[...].reshape(256, 256),
            jnp.concatenate([kept, kept], axis=0),
            preferred_element_type=F32,
        )
        for q in range(4):
            span = slice(64 * q, 64 * q + 64)
            cols = slice(128 * q, 128 * q + 128)
            state = jnp.concatenate([s_ref[s, 2 * q], s_ref[s, 2 * q + 1]], axis=1)
            after_it = d_b[span] * state + k_b[span] * v[s : s + 1, cols]
            next_ref[s, 2 * q] = after_it[:, :64]
            next_ref[s, 2 * q + 1] = after_it[:, 64:]
            y_ref[s : s + 1, cols] = jnp.sum(r_b[span] * state, axis=0, keepdims=True)
    r = r_ref[0, here].astype(F32)
    k = k_ref[0, here].astype(F32)
    reward, scale, offset = vec_ref[0:1], vec_ref[1:2], vec_ref[2:3]
    own = r * reward * k
    ones = jnp.concatenate([head_mask(1.0)] * 2, axis=0)
    mean_of = jnp.concatenate([head_mask(1.0 / 64)] * 2, axis=0)
    out = []
    for q in range(4):
        cols = slice(128 * q, 128 * q + 128)
        total = jnp.dot(in_two(own[:, cols]), ones, preferred_element_type=F32)
        y = y_ref[:, cols] + total * v[:, cols]
        center = y - jnp.dot(in_two(y), mean_of, preferred_element_type=F32)
        spread = jnp.dot(in_two(center * center), mean_of, preferred_element_type=F32)
        normed = center * lax.rsqrt(spread + NORM_EPS) * scale[:, cols] + offset[:, cols]
        out.append((normed * g_ref[here, cols].astype(F32)).astype(BF))
    return jnp.concatenate(out, axis=1)


def place_kernel(place_ref, spot_ref, final_ref, _, state_ref, sem):
    copies = [
        pltpu.make_async_copy(
            final_ref.at[p], state_ref.at[slot_of(place_ref, spot_ref, p)], sem.at[p]
        )
        for p in range(2)
    ]
    for copy in copies:
        copy.start()
    for copy in copies:
        copy.wait()


def place_states(place, spots, final, states):
    return pl.pallas_call(
        place_kernel,
        out_shape=jax.ShapeDtypeStruct(states.shape, F32),
        grid_spec=pltpu.PrefetchScalarGridSpec(
            num_scalar_prefetch=2,
            grid=(1,),
            in_specs=[pl.BlockSpec(final.shape, lambda i, *s: (0, 0, 0, 0)), ANY],
            out_specs=ANY,
            scratch_shapes=[pltpu.SemaphoreType.DMA((2,))],
        ),
        input_output_aliases={3: 0},
        compiler_params=params(1),
        cost_estimate=cost(0, 2 << 20),
        name="place_states",
    )(place, spots, final, states)


def span_tables():
    t = np.arange(CH)
    blocks = []
    size = 4
    while size <= CH:
        start = (t // size) * size
        mid = start + size // 2
        m = np.zeros((CH, CH), np.float32)
        for i in range(CH):
            if i >= mid[i]:
                m[i, mid[i] : i] = 1.0
            else:
                m[i, i + 1 : mid[i]] = 1.0
        blocks.append(m)
        size *= 2
    before = (t[None, :] < t[:, None]).astype(np.float32)
    after = (t[None, :] > t[:, None]).astype(np.float32)
    whole = np.ones((8, CH), np.float32)
    table = np.concatenate(blocks + [before, after, whole])
    return np.concatenate([table, table], axis=1)


LEVELS = int(np.log2(CH))


def wkv_kernel(
    count_ref, keep_ref, table_ref, *refs, t0, span, slot0, last, chained, prompts
):
    ins, refs = refs[: 5 * prompts], refs[5 * prompts :]
    vec_ref, start_ref, slots_ref, rd_ref, kd_ref, vd_ref, wd_ref, gd_ref = refs[:8]
    refs = refs[9:] if chained else refs[8:]
    out_ref, state_ref, next_ref = refs[:3]
    turned = refs[-4:-1]
    y_ref = refs[-1]
    c = pl.program_id(0)

    @pl.when(c == 0)
    def _():
        state_ref[...] = start_ref[...]
        turn_decode(rd_ref, kd_ref, wd_ref, *turned)

    table = table_ref[...]
    row = lax.broadcasted_iota(jnp.int32, (CH, 512), 0)
    low = lax.broadcasted_iota(jnp.int32, (CH, 128), 1) < 64
    arow = lax.broadcasted_iota(jnp.int32, (CH, 2 * CH), 0)
    acol = lax.broadcasted_iota(jnp.int32, (CH, 2 * CH), 1) & (CH - 1)
    diff = arow ^ acol
    causal = arow > acol
    same_head = (lax.broadcasted_iota(jnp.int32, (128, 128), 0) < 64) == (
        lax.broadcasted_iota(jnp.int32, (128, 128), 1) < 64
    )
    mean_of = head_mask(1.0 / 64)
    mean_two = jnp.concatenate([mean_of, mean_of], axis=0)
    reward, scale, offset = vec_ref[0:1], vec_ref[1:2], vec_ref[2:3]
    contract_lanes = (((1,), (1,)), ((), ()))
    contract_rows = (((0,), (0,)), ((), ()))

    def both_heads(a):
        zero = jnp.zeros_like(a)
        return jnp.concatenate([jnp.where(low, a, zero), jnp.where(low, zero, a)], axis=0)

    def lanes_dot(a, b):
        return lax.dot_general(a, b, contract_lanes, preferred_element_type=F32)

    def dot(a, b):
        return jnp.dot(a, b, preferred_element_type=F32)

    streams = [(p, q) for p in range(prompts) for q in range(4)]
    cols = [slice(128 * q, 128 * q + 128) for q in range(4)]
    keys, own, mixed, r_dec, k_dec, whole, values = {}, {}, {}, {}, {}, {}, {}
    for p in range(prompts):
        r_ref, k_ref, v_ref, w_ref, g_ref = ins[5 * p : 5 * p + 5]
        live = (row + (c * CH + t0)) < count_ref[p]
        r = r_ref[0].astype(F32)
        k = jnp.where(live, k_ref[0].astype(F32), 0.0)
        values[p] = v_ref[0]
        w = w_ref[...]
        w_hi = w.astype(BF)
        w_lo = (w - w_hi.astype(F32)).astype(BF)
        factors = jnp.exp(dot(table, jnp.concatenate([w_hi, w_lo], axis=0)))
        r_dec[p] = (r * factors[(LEVELS - 1) * CH : LEVELS * CH]).astype(BF)
        k_dec[p] = (k * factors[LEVELS * CH : (LEVELS + 1) * CH]).astype(BF)
        whole[p] = factors[(LEVELS + 1) * CH : (LEVELS + 1) * CH + 1]
        weighted = r * reward
        hi = weighted.astype(BF)
        own[p] = (hi, (weighted - hi.astype(F32)).astype(BF))
        keys[p] = k.astype(BF)
        mixed[p] = [jnp.where((row & 1) == 1, r, k).astype(BF)]
        for level in range(1, LEVELS):
            pick = jnp.where((row & (1 << level)) != 0, r, k)
            mixed[p].append((pick * factors[(level - 1) * CH : level * CH]).astype(BF))
    scores = {}
    for p, q in streams:
        key = both_heads(keys[p][:, cols[q]])
        s = lanes_dot(
            jnp.concatenate([half[:, cols[q]] for half in own[p]], axis=1),
            jnp.concatenate([key, key], axis=1),
        )
        scores[p, q] = jnp.where(diff == 0, s, 0.0)
    for level in range(LEVELS):
        here = jnp.logical_and(causal, (diff >> level) == 1)
        for p, q in streams:
            a = mixed[p][level][:, cols[q]]
            scores[p, q] = jnp.where(here, lanes_dot(a, both_heads(a)), scores[p, q])
    y = {}
    for p, q in streams:
        v = values[p][:, cols[q]]
        state = state_ref[p, q]
        y[p, q] = dot(scores[p, q].astype(BF), both_heads(v)) + lanes_dot(
            r_dec[p][:, cols[q]], state.astype(BF)
        )
        added = lax.dot_general(v, k_dec[p][:, cols[q]], contract_rows, preferred_element_type=F32)
        state_ref[p, q] = state * whole[p][:, cols[q]] + jnp.where(same_head, added, 0.0)
    center = {n: y[n] - dot(in_two(y[n]), mean_two) for n in streams}
    spread = {n: dot((center[n] * center[n]).astype(BF), mean_of) for n in streams}
    for p, q in streams:
        normed = center[p, q] * lax.rsqrt(spread[p, q] + NORM_EPS)
        gate = ins[5 * p + 4][:, cols[q]].astype(F32)
        at = pl.multiple_of(p * span + c * CH, CH)
        out_ref[pl.ds(at, CH), cols[q]] = (
            (normed * scale[:, cols[q]] + offset[:, cols[q]]) * gate
        ).astype(out_ref.dtype)

    done = decode_slots(
        slot0 + c * SLOT_BLOCK, keep_ref, slots_ref, rd_ref, kd_ref, vd_ref, gd_ref, vec_ref,
        next_ref, *turned, y_ref,
    )
    at = pl.multiple_of(prompts * span + c * SLOT_BLOCK, SLOT_BLOCK)
    out_ref[pl.ds(at, SLOT_BLOCK), :] = done

    if last:
        final_ref = refs[3]

        @pl.when(c == pl.num_programs(0) - 1)
        def _():
            for p, q in streams:
                whole_state = jnp.transpose(state_ref[p, q])
                final_ref[p, 2 * q] = whole_state[:64, :64]
                final_ref[p, 2 * q + 1] = whole_state[64:, 64:]


def wkv(counts, keep, rkv, log_decay, gate, vectors, start, states, earlier, t0, t1, length):
    prompts, slots = start.shape[0], states.shape[0]
    table = jnp.asarray(span_tables(), BF)
    c0, per, span = t0 // CH, length // CH, t1 - t0
    chunks = span // CH
    last, chained = t1 == length, earlier is not None
    at = prompts * length // slots

    def part(n, p):
        return pl.BlockSpec((1, CH, 512), lambda c, s, k: (n, p * per + c + c0, 0))

    def flat(p):
        return pl.BlockSpec((CH, 512), lambda c, s, k: (p * per + c + c0, 0))

    def slot_part(n):
        return pl.BlockSpec((1, slots, 512), lambda c, s, k: (n, at, 0))

    slot_flat = pl.BlockSpec((slots, 512), lambda c, s, k: (at, 0))
    big = pl.BlockSpec((SLOT_BLOCK, 8, 64, 64), lambda c, s, k: (c + c0, 0, 0, 0))
    held = pl.BlockSpec((prompts, 4, 128, 128), lambda c, s, k: (0, 0, 0, 0))
    rows = prompts * span + chunks * SLOT_BLOCK
    out_shape = [
        jax.ShapeDtypeStruct((rows, 512), BF),
        jax.ShapeDtypeStruct((prompts, 4, 128, 128), F32),
        jax.ShapeDtypeStruct(states.shape, F32),
    ]
    out_specs = [pl.BlockSpec((rows, 512), lambda c, s, k: (0, 0)), held, big]
    if last:
        out_shape.append(jax.ShapeDtypeStruct((prompts, 8, 64, 64), F32))
        out_specs.append(pl.BlockSpec((prompts, 8, 64, 64), lambda c, s, k: (0, 0, 0, 0)))
    ins, specs = [], []
    for p in range(prompts):
        ins += [rkv, rkv, rkv, log_decay, gate]
        specs += [part(0, p), part(1, p), part(2, p), flat(p), flat(p)]
    ins += [vectors, start, states, rkv, rkv, rkv, log_decay, gate]
    specs += [pl.BlockSpec((8, 512), lambda c, s, k: (0, 0)), held, big]
    specs += [slot_part(0), slot_part(1), slot_part(2), slot_flat, slot_flat]
    alias = {}
    if chained:
        ins.append(earlier)
        specs.append(ANY)
        alias = {2 + len(ins): 2}
    return pl.pallas_call(
        functools.partial(
            wkv_kernel,
            t0=t0,
            span=span,
            slot0=c0 * SLOT_BLOCK,
            last=last,
            chained=chained,
            prompts=prompts,
        ),
        out_shape=out_shape,
        grid_spec=pltpu.PrefetchScalarGridSpec(
            num_scalar_prefetch=2,
            grid=(chunks,),
            in_specs=[pl.BlockSpec(table.shape, lambda c, s, k: (0, 0))] + specs,
            out_specs=out_specs,
            scratch_shapes=[
                pltpu.VMEM((4, 64, 128), BF),
                pltpu.VMEM((4, 64, 128), BF),
                pltpu.VMEM((4, 64, 256), BF),
                pltpu.VMEM((SLOT_BLOCK, 512), F32),
            ],
        ),
        input_output_aliases=alias,
        compiler_params=params(1),
        cost_estimate=cost(span * 80_000_000, span << 17),
        name="wkv",
    )(counts, keep, table, *ins)


def on_device(
    learner_acceptance_matrix,
    learner_address_matrix,
    learner_content_matrix,
    learner_gating_matrix,
    learner_result_matrix,
    fading_narrowing_matrix,
    fading_widening_matrix,
    feature_fading_speed,
    current_reward,
    symbol_blending_factors,
    group_scaling_factor,
    group_scaling_offset,
    request_hidden_entries,
    request_valid_count,
    request_destination_place,
    newest_symbol_hidden,
    preceding_hidden_entry,
    place_memory_matrix,
    place_newness_marks,
):
    h = lax.axis_index("yh") * 2 + lax.axis_index("core")
    z, x, yl = lax.axis_index("z"), lax.axis_index("x"), lax.axis_index("yl")
    place = jnp.stack([h, z, x, yl]).astype(jnp.int32)
    prompts, length, width = request_hidden_entries.shape
    slots, groups, breadth = place_memory_matrix.shape[:3]
    tokens = prompts * length
    rows = tokens + slots
    counts, spots, marks = in_hbm(
        request_valid_count, request_destination_place, place_newness_marks
    )

    parts, own, new_shift = split(
        place,
        marks,
        counts,
        spots,
        [
            learner_acceptance_matrix,
            learner_address_matrix,
            learner_content_matrix,
            learner_gating_matrix,
            learner_result_matrix,
        ],
        request_hidden_entries.reshape(tokens, width),
        newest_symbol_hidden,
        preceding_hidden_entry,
    )
    blocks = [parts[0]] + [swap(parts[d], "head", d) for d in (1, 2, 3)]
    side = swap(own, "head", 1)
    far = swap(after(own, blocks[3]), "head", 2)
    stacked = jnp.stack(blocks)
    neighbour = swap(stacked, "yl", 1)
    far_side = swap(far, "head", 1)

    def mixes(piece, d, mixed, low):
        return mix(
            place,
            counts,
            piece,
            d,
            symbol_blending_factors,
            fading_narrowing_matrix.T,
            low,
            mixed,
            fading_widening_matrix,
            feature_fading_speed[None],
            slots,
            length,
        )

    every, first, second = slice(0, 5), slice(0, 3), slice(3, 5)
    mixed, low = mixes(own, 0, None, None)
    neighbour, side, low = lax.optimization_barrier((neighbour, side, low))
    by_row = in_order(stacked, neighbour, yl)
    held = [by_row[p][None, None] for p in range(4)]
    recv = swap_all(held, 0)
    held = pack(place, held, recv, 0, every)
    recv = swap_all(held, 1)
    mixed, low = mixes(side, 1, mixed, low)
    held = pack(place, held, after(recv, low), 1, every)
    recv = swap_all(held, 2)
    mixed, low = mixes(far, 2, mixed, low)
    recv = after(recv, low)
    early = pack(place, held, recv, 2, first)
    early_recv = swap_all(early, 3)
    mixed, log_decay = mixes(far_side, 3, mixed, low)
    late = pack(place, held, after(recv, log_decay), 2, second)
    early_recv = after(early_recv, log_decay)
    late_recv = swap_all(after(late, early_recv), 3)
    early = list(early) + early_recv
    late = list(late) + late_recv

    rkv = project_rkv(place, mixed, early, rows)
    gate = project_gate(place, mixed, late, rows // 2)
    small = jnp.stack([current_reward, group_scaling_factor, group_scaling_offset])
    vectors = jnp.concatenate([small, jnp.zeros((5, width), F32)])
    state = jnp.zeros((prompts, groups // 2, 128, 128), F32)
    sent = []
    t0 = 0
    new_state = None
    for t1 in (256, 448, 512):
        out = wkv(
            counts,
            marks,
            rkv,
            log_decay,
            gate,
            vectors,
            state,
            place_memory_matrix,
            new_state,
            t0,
            t1,
            length,
        )
        normed, state, new_state = out[:3]
        n_side = swap(normed, "head", 1)
        n_far = swap(normed, "head", 2)
        if t1 == length:
            result = project_result(
                place, counts, spots, sent[0], late, (256,), 0, None, length, slots
            )
            n_far = after(n_far, result[1])
        n_far_side = swap(n_far, "head", 1)
        sent.append([normed, n_side, n_far, n_far_side])
        t0 = t1
    prompt_hidden, decode_hidden = project_result(
        place, counts, spots, sent[1] + sent[2], late, (192, 64), 256, result, length, slots
    )
    final_state = out[3]
    new_state = place_states(place, spots, final_state, new_state)
    return (prompt_hidden, decode_hidden, new_state, new_shift)


def solution(mesh):
    split = Mesh(mesh.devices.reshape(2, 2, 4, 4, 2), ("yh", "core", "z", "x", "yl"))
    head = ("yh", "core")
    req = ("z", "x", "yl")
    row_shard = P(head + req, None)
    in_specs = (
        row_shard,
        row_shard,
        row_shard,
        row_shard,
        row_shard,
        P(),
        P(None, head),
        P(head),
        P(head),
        P(),
        P(head),
        P(head),
        P(req, None, head),
        P(req),
        P(req),
        P(req, head),
        P(req, head),
        P(req, head, None, None),
        P(req),
    )
    out_specs = (
        P(req, None, head),
        P(req, head),
        P(req, head, None, None),
        P(req, head),
    )
    return jax.shard_map(
        on_device, mesh=split, in_specs=in_specs, out_specs=out_specs, check_vma=False
    )
```

```python
import functools

import jax
import jax.numpy as jnp
import numpy as np
from jax import lax
from jax.experimental import pallas as pl
from jax.experimental.pallas import tpu as pltpu
from jax.sharding import Mesh
from jax.sharding import PartitionSpec as P

NORM_EPS = 0.00064
N_HEAD = 4
CH = 64
BF = jnp.bfloat16
F32 = jnp.float32


STEPS = (("x", 1), ("z", 1), ("x", 3), ("z", 3))


def swap(a, axes, bits):
    sizes = {"x": 4, "z": 4, "yl": 2, "head": 4}
    names = ("yh", "core") if axes == "head" else axes
    return lax.ppermute(a, names, [(i, i ^ bits) for i in range(sizes[axes])])


def order_of(part):
    return [STEPS[(part + n) % 4] for n in range(4)]


def after(value, other):
    return lax.optimization_barrier((value, other))[0]


ANY = pl.BlockSpec(memory_space=pl.ANY)


def in_hbm(*arrays):
    return [pltpu.with_memory_space_constraint(a, pltpu.HBM) for a in arrays]


def cost(flops, nbytes, trans=0):
    return pl.CostEstimate(flops=flops, bytes_accessed=nbytes, transcendentals=trans)


def params(axes):
    return pltpu.CompilerParams(
        dimension_semantics=("arbitrary",) * axes, vmem_limit_bytes=48 << 20
    )


def kept_of(fresh_ref, n):
    return jnp.where(fresh_ref[n] == 1, 0.0, 1.0)


def slot_of(place_ref, spot_ref, p):
    return spot_ref[p] - (place_ref[1] * 8 + place_ref[2] * 2 + place_ref[3]) * 64


def split_kernel(place_ref, keep_ref, count_ref, spot_ref, *refs):
    mats, hid, newest, prior = refs[:5], refs[5], refs[6], refs[7]
    outs, own_ref, shift_ref = refs[8:12], refs[12], refs[13]
    buf, old, sem = refs[14:]
    tokens, slots = hid.shape[0], newest.shape[0]
    copies = [pltpu.make_async_copy(mats[m], buf.at[m], sem.at[m]) for m in range(5)]
    copies += [
        pltpu.make_async_copy(prior, old, sem.at[5]),
        pltpu.make_async_copy(newest, own_ref.at[pl.ds(tokens, slots)], sem.at[6]),
        pltpu.make_async_copy(hid, own_ref.at[pl.ds(0, tokens)], sem.at[7]),
    ]
    for copy in copies:
        copy.start()
    row = lax.broadcasted_iota(jnp.int32, (slots, 512), 0)
    keep = jnp.zeros((slots, 512), F32)
    for n in range(slots):
        keep = jnp.where(row == n, kept_of(keep_ref, n), keep)
    for m in range(5):
        copies[m].wait()
    for d in range(4):
        at = pl.multiple_of((place_ref[0] ^ d) * 512, 512)
        for m in range(5):
            outs[d][m] = buf[m, :, pl.ds(at, 512)].astype(BF)
    copies[5].wait()
    kept = jnp.where(keep > 0.5, old[...].astype(F32), 0.0)
    own_ref[tokens + slots :] = kept.astype(BF)
    copies[6].wait()
    copies[7].wait()
    shift = own_ref[tokens : tokens + slots].astype(F32)
    few = lax.broadcasted_iota(jnp.int32, (16, 512), 0)
    for p in range(2):
        at = p * (tokens // 2) + count_ref[p] - 1
        base = pl.multiple_of((at >> 4) << 4, 16)
        near = own_ref[pl.ds(base, 16)].astype(F32)
        last = jnp.sum(jnp.where(few == (at & 15), near, 0.0), axis=0, keepdims=True)
        shift = jnp.where(row == slot_of(place_ref, spot_ref, p), last, shift)
    shift_ref[...] = shift.astype(BF)


def split(place, keep, counts, spots, matrices, hidden, newest, prior):
    rows, width = matrices[0].shape[0], matrices[0].shape[1] // N_HEAD
    shape = (len(matrices), rows, width)
    total = hidden.shape[0] + 2 * newest.shape[0]
    hbm = pl.BlockSpec(memory_space=pltpu.HBM)
    out = pl.pallas_call(
        split_kernel,
        out_shape=[jax.ShapeDtypeStruct(shape, BF)] * 4
        + [jax.ShapeDtypeStruct((total, width), BF), jax.ShapeDtypeStruct(newest.shape, BF)],
        grid_spec=pltpu.PrefetchScalarGridSpec(
            num_scalar_prefetch=4,
            grid=(1,),
            in_specs=[hbm] * 8,
            out_specs=[pl.BlockSpec(shape, lambda i, *s: (0, 0, 0))] * 4
            + [
                pl.BlockSpec((total, width), lambda i, *s: (0, 0)),
                pl.BlockSpec(newest.shape, lambda i, *s: (0, 0)),
            ],
            scratch_shapes=[
                pltpu.VMEM((5,) + matrices[0].shape, F32),
                pltpu.VMEM(newest.shape, BF),
                pltpu.SemaphoreType.DMA((8,)),
            ],
        ),
        compiler_params=params(1),
        name="split",
    )(place, keep, counts, spots, *in_hbm(*matrices, hidden, newest, prior))
    return out[:4], out[4], out[5]


def in_order(own, other, yl):
    first = yl == 0
    return jnp.concatenate(
        [jnp.where(first, own, other), jnp.where(first, other, own)], axis=-2
    )


def axis_dim(axis):
    return 0 if axis == "z" else 1


def places(p, n, place_ref):
    axis, bits = order_of(p)[n]
    pos = place_ref[1] if axis == "z" else place_ref[2]
    seen = [b for name, b in order_of(p)[:n] if name == axis]
    offsets = [0] + seen
    return [pos ^ o for o in offsets], [pos ^ bits ^ o for o in offsets]


def part_of(ref, dim, i, lot):
    return ref.at[i, :, lot] if dim == 0 else ref.at[:, i, lot]


def pack_kernel(place_ref, *refs, n, lot):
    owns, recvs, outs, sem = refs[:4], refs[4:8], refs[8:12], refs[12]
    copies = []
    for p in range(4):
        dim = axis_dim(order_of(p)[n][0])
        own_at, recv_at = places(p, n, place_ref)
        if len(own_at) == 1:
            own_at, recv_at = [0], [1]
        for src, at in ((owns[p], own_at), (recvs[p], recv_at)):
            for i, j in enumerate(at):
                source = part_of(src, dim, i, lot)
                target = part_of(outs[p], dim, j, slice(None))
                copies.append(pltpu.make_async_copy(source, target, sem.at[len(copies)]))
    for copy in copies:
        copy.start()
    for copy in copies:
        copy.wait()


def pack(place, owns, recvs, n, lot):
    shapes = []
    for p in range(4):
        shape = list(owns[p].shape)
        shape[axis_dim(order_of(p)[n][0])] *= 2
        shape[2] = lot.stop - lot.start
        shapes.append(jax.ShapeDtypeStruct(tuple(shape), BF))
    return pl.pallas_call(
        functools.partial(pack_kernel, n=n, lot=lot),
        out_shape=shapes,
        grid_spec=pltpu.PrefetchScalarGridSpec(
            num_scalar_prefetch=1,
            grid=(1,),
            in_specs=[ANY] * 8,
            out_specs=[pl.BlockSpec(a.shape, lambda i, s: (0, 0, 0, 0, 0)) for a in shapes],
            scratch_shapes=[pltpu.SemaphoreType.DMA((16,))],
        ),
        compiler_params=params(1),
        cost_estimate=cost(0, 8 << 20),
        name="pack",
    )(place, *(in_hbm(*owns, *recvs) if n == 2 else (*owns, *recvs)))


def swap_all(owns, n):
    return [swap(owns[p], *order_of(p)[n]) for p in range(4)]


def copy_weights(pieces, m, place_ref, buf, sem):
    for p in range(4):
        dim = axis_dim(order_of(p)[3][0])
        own_at, recv_at = places(p, 3, place_ref)
        for src, at in ((pieces[p], own_at), (pieces[p + 4], recv_at)):
            for i, j in enumerate(at):
                target = buf.at[p * 4 + j] if dim == 0 else buf.at[pl.ds(p * 4, 4), j]
                pltpu.make_async_copy(part_of(src, dim, i, m), target, sem).start()


def wait_weights(buf, sem):
    pltpu.make_async_copy(buf, buf, sem).wait()


def mix_kernel(place_ref, count_ref, *refs, d, length):
    hid_ref, mu_ref, narrow_ref = refs[:3]
    refs = refs[3:]
    if d > 0:
        low_in, refs = refs[0], refs[2:]
    if d == 3:
        widen_ref, speed_ref, refs = refs[0], refs[1], refs[2:]
    x_ref, low_ref, cur_ref, step_ref = refs
    i = pl.program_id(0)
    rows = cur_ref.shape[0]
    slots = hid_ref.shape[0] - rows
    tokens = rows - slots

    @pl.when(i == 0)
    def _():
        cur = hid_ref[:rows].astype(F32)
        cur_ref[...] = cur
        seq = cur[:tokens]
        at = lax.broadcasted_iota(jnp.int32, seq.shape, 0)
        before = jnp.where((at & (length - 1)) == 0, 0.0, pltpu.roll(seq, 1, 0))
        step_ref[:tokens] = before - seq
        step_ref[tokens:] = hid_ref[rows:].astype(F32) - cur[tokens:]

    mixed = (cur_ref[...] + step_ref[...] * mu_ref[pl.ds(i, 1), :]).astype(BF)
    x_ref[0] = mixed

    @pl.when(i == 3)
    def _():
        low = lax.dot_general(
            mixed, narrow_ref[...], (((1,), (1,)), ((), ())), preferred_element_type=F32
        )
        if d > 0:
            low = low + low_in[...]
        if d < 3:
            low_ref[...] = low
        else:
            lowrank = jnp.tanh(low).astype(BF)
            rate = jnp.exp(jnp.dot(lowrank, widen_ref[...], preferred_element_type=F32))
            log_decay = -speed_ref[...] * rate
            at = lax.broadcasted_iota(jnp.int32, (rows, 512), 0)
            limit = jnp.where(
                at < length,
                count_ref[0],
                jnp.where(at < 2 * length, count_ref[1] + length, rows),
            )
            low_ref[...] = jnp.where(at < limit, log_decay, 0.0)


def mix(place, counts, hidden, d, mu, narrow, low, held, widen, speed, slots, length):
    rows = hidden.shape[0] - slots
    once = lambda i, s, c: (0, 0)
    args = [hidden] + in_hbm(mu, narrow)
    specs = [
        pl.BlockSpec(hidden.shape, once),
        pl.BlockSpec((5, 512), lambda i, s, c: (0, s[0] ^ d)),
        pl.BlockSpec((64, 512), lambda i, s, c: (0, s[0] ^ d)),
    ]
    alias = {}
    if d > 0:
        args += [low, held]
        specs += [pl.BlockSpec(low.shape, once), ANY]
        alias = {6: 0}
    wide = 64
    if d == 3:
        args += in_hbm(widen, speed)
        specs += [pl.BlockSpec(widen.shape, once), pl.BlockSpec(speed.shape, once)]
        wide = 512
    return pl.pallas_call(
        functools.partial(mix_kernel, d=d, length=length),
        out_shape=(
            jax.ShapeDtypeStruct((5, rows, 2048), BF),
            jax.ShapeDtypeStruct((rows, wide), F32),
        ),
        grid_spec=pltpu.PrefetchScalarGridSpec(
            num_scalar_prefetch=2,
            grid=(5,),
            in_specs=specs,
            out_specs=(
                pl.BlockSpec((1, rows, 512), lambda i, s, c: (i, 0, d)),
                pl.BlockSpec((rows, wide), once),
            ),
            scratch_shapes=[pltpu.VMEM((rows, 512), F32), pltpu.VMEM((rows, 512), F32)],
        ),
        input_output_aliases=alias,
        compiler_params=params(1),
        cost_estimate=cost(20 * rows * 512, 12 * rows * 512),
        name="mix",
    )(place, counts, *args)


def rkv_kernel(place_ref, x_ref, *refs):
    pieces = refs[:8]
    out_ref, buf, sem = refs[8:]
    i, j = pl.program_id(0), pl.program_id(1)
    slot = lax.rem(i, 2)

    @pl.when(jnp.logical_and(i == 0, j == 0))
    def _():
        copy_weights(pieces, 0, place_ref, buf.at[0], sem.at[0])

    @pl.when(j == 0)
    def _():
        @pl.when(i < 2)
        def _():
            copy_weights(pieces, i + 1, place_ref, buf.at[1 - slot], sem.at[1 - slot])

        wait_weights(buf.at[slot], sem.at[slot])

    w = buf[slot].reshape(2048, 512)
    out_ref[0] = jnp.dot(x_ref[0], w, preferred_element_type=F32).astype(out_ref.dtype)


def project_rkv(place, mixed, pieces, tile):
    rows = mixed.shape[1]
    return pl.pallas_call(
        rkv_kernel,
        out_shape=jax.ShapeDtypeStruct((3, rows, 512), BF),
        grid_spec=pltpu.PrefetchScalarGridSpec(
            num_scalar_prefetch=1,
            grid=(3, rows // tile),
            in_specs=[pl.BlockSpec((1, tile, 2048), lambda i, j, s: (i, j, 0))] + [ANY] * 8,
            out_specs=pl.BlockSpec((1, tile, 512), lambda i, j, s: (i, j, 0)),
            scratch_shapes=[
                pltpu.VMEM((2, 16, 4, 32, 512), BF),
                pltpu.SemaphoreType.DMA((2,)),
            ],
        ),
        compiler_params=params(2),
        cost_estimate=cost(6 * rows * 2048 * 512, 24 << 20),
        name="project_rkv",
    )(place, mixed, *pieces)


def gate_kernel(place_ref, x_ref, *refs):
    pieces = refs[:8]
    out_ref, buf, sem = refs[8:]

    @pl.when(pl.program_id(0) == 0)
    def _():
        copy_weights(pieces, 0, place_ref, buf, sem)
        wait_weights(buf, sem)

    total = jnp.dot(x_ref[0], buf[...].reshape(2048, 512), preferred_element_type=F32)
    out_ref[...] = (total / (1.0 + jnp.exp(-total))).astype(out_ref.dtype)


def project_gate(place, mixed, pieces, tile):
    rows = mixed.shape[1]
    return pl.pallas_call(
        gate_kernel,
        out_shape=jax.ShapeDtypeStruct((rows, 512), BF),
        grid_spec=pltpu.PrefetchScalarGridSpec(
            num_scalar_prefetch=1,
            grid=(rows // tile,),
            in_specs=[pl.BlockSpec((1, tile, 2048), lambda j, s: (4, j, 0))] + [ANY] * 8,
            out_specs=pl.BlockSpec((tile, 512), lambda j, s: (j, 0)),
            scratch_shapes=[pltpu.VMEM((16, 4, 32, 512), BF), pltpu.SemaphoreType.DMA(())],
        ),
        compiler_params=params(1),
        cost_estimate=cost(2 * rows * 2048 * 512, 8 << 20),
        name="project_gate",
    )(place, mixed, *pieces)


def result_kernel(place_ref, count_ref, spot_ref, *refs, spans, t0, slot0, chained):
    lots = len(spans)
    xs, pieces = refs[: 4 * lots], refs[4 * lots : 4 * lots + 8]
    rest = refs[4 * lots + 8 + (2 if chained else 0) :]
    out_ref, slot_ref, buf, sem = rest
    copy_weights(pieces, 1, place_ref, buf, sem)
    wait_weights(buf, sem)
    start = slot = 0
    for lot, span in enumerate(spans):
        total = None
        for d in range(4):
            w = buf[4 * d : 4 * d + 4].reshape(512, 512)
            term = jnp.dot(xs[4 * lot + d][...], w, preferred_element_type=F32)
            total = term if total is None else total + term
        at = lax.broadcasted_iota(jnp.int32, (span, 512), 0) + (t0 + start)
        for p in range(2):
            own = jnp.where(at < count_ref[p], total[p * span : (p + 1) * span], 0.0)
            out_ref[p, start : start + span] = own.astype(out_ref.dtype)
        start += span
        more = total.shape[0] - 2 * span
        which = lax.broadcasted_iota(jnp.int32, (more, 512), 0) + (slot0 + slot)
        taken = jnp.logical_or(
            which == slot_of(place_ref, spot_ref, 0), which == slot_of(place_ref, spot_ref, 1)
        )
        own = jnp.where(taken, 0.0, total[2 * span :])
        slot_ref[slot : slot + more] = own.astype(slot_ref.dtype)
        slot += more


def project_result(place, counts, spots, xs, pieces, spans, t0, earlier, length, all_slots):
    span = sum(spans)
    slots = sum(xs[4 * n].shape[0] - 2 * spans[n] for n in range(len(spans)))
    once = lambda i, *s: (0, 0)
    chained = earlier is not None
    block = t0 // span
    return pl.pallas_call(
        functools.partial(
            result_kernel, spans=spans, t0=t0, slot0=block * slots, chained=chained
        ),
        out_shape=[
            jax.ShapeDtypeStruct((2, length, 512), BF),
            jax.ShapeDtypeStruct((all_slots, 512), BF),
        ],
        grid_spec=pltpu.PrefetchScalarGridSpec(
            num_scalar_prefetch=3,
            grid=(1,),
            in_specs=[pl.BlockSpec(a.shape, once) for a in xs] + [ANY] * (10 if chained else 8),
            out_specs=[
                pl.BlockSpec((2, span, 512), lambda i, *s: (0, block, 0)),
                pl.BlockSpec((slots, 512), lambda i, *s: (block, 0)),
            ],
            scratch_shapes=[pltpu.VMEM((16, 4, 32, 512), BF), pltpu.SemaphoreType.DMA(())],
        ),
        input_output_aliases={3 + len(xs) + 8: 0, 3 + len(xs) + 9: 1} if chained else {},
        compiler_params=params(1),
        cost_estimate=cost(4 * span * 2048 * 512, 8 << 20),
        name="project_result",
    )(place, counts, spots, *xs, *in_hbm(*pieces), *(earlier if chained else []))


SLOT_BLOCK = 8


def head_mask(value):
    row = lax.broadcasted_iota(jnp.int32, (128, 128), 0) < 64
    col = lax.broadcasted_iota(jnp.int32, (128, 128), 1) < 64
    return jnp.where(row == col, value, 0.0).astype(BF)


def in_two(a):
    hi = a.astype(BF)
    return jnp.concatenate([hi, (a - hi.astype(F32)).astype(BF)], axis=1)


def turn_decode(r_ref, k_ref, w_ref, rt_ref, kt_ref, dt_ref):
    r = r_ref[0].astype(F32)
    k = k_ref[0].astype(F32)
    decay = jnp.exp(w_ref[...])
    for q in range(4):
        cols = slice(128 * q, 128 * q + 128)

        def turned(a):
            t = jnp.transpose(a[:, cols])
            return jnp.concatenate([t[:64], t[64:]], axis=1)

        rt_ref[q] = turned(r).astype(BF)
        kt_ref[q] = turned(k).astype(BF)
        dt_ref[q] = in_two(turned(decay))


def decode_slots(
    first, keep_ref, s_ref, r_ref, k_ref, v_ref, g_ref, vec_ref, next_ref, rt_ref, kt_ref, dt_ref,
    y_ref,
):
    here = pl.ds(pl.multiple_of(first, SLOT_BLOCK), SLOT_BLOCK)
    v = v_ref[0, here].astype(F32)
    row = lax.broadcasted_iota(jnp.int32, (128, 128), 0)
    low = lax.broadcasted_iota(jnp.int32, (128, 128), 1) < 64
    for s in range(SLOT_BLOCK):
        slot = first + s
        hit = row == jnp.where(low, slot, slot + 64)
        pick = jnp.where(hit, 1.0, 0.0).astype(BF)
        kept = jnp.where(hit, kept_of(keep_ref, slot), 0.0).astype(BF)
        r_b = jnp.dot(rt_ref[...].reshape(256, 128), kept, preferred_element_type=F32)
        k_b = jnp.dot(kt_ref[...].reshape(256, 128), pick, preferred_element_type=F32)
        d_b = jnp.dot(
            dt_ref[...].reshape(256, 256),
            jnp.concatenate([kept, kept], axis=0),
            preferred_element_type=F32,
        )
        for q in range(4):
            span = slice(64 * q, 64 * q + 64)
            cols = slice(128 * q, 128 * q + 128)
            state = jnp.concatenate([s_ref[s, 2 * q], s_ref[s, 2 * q + 1]], axis=1)
            after_it = d_b[span] * state + k_b[span] * v[s : s + 1, cols]
            next_ref[s, 2 * q] = after_it[:, :64]
            next_ref[s, 2 * q + 1] = after_it[:, 64:]
            y_ref[s : s + 1, cols] = jnp.sum(r_b[span] * state, axis=0, keepdims=True)
    r = r_ref[0, here].astype(F32)
    k = k_ref[0, here].astype(F32)
    reward, scale, offset = vec_ref[0:1], vec_ref[1:2], vec_ref[2:3]
    own = r * reward * k
    ones = jnp.concatenate([head_mask(1.0)] * 2, axis=0)
    mean_of = jnp.concatenate([head_mask(1.0 / 64)] * 2, axis=0)
    out = []
    for q in range(4):
        cols = slice(128 * q, 128 * q + 128)
        total = jnp.dot(in_two(own[:, cols]), ones, preferred_element_type=F32)
        y = y_ref[:, cols] + total * v[:, cols]
        center = y - jnp.dot(in_two(y), mean_of, preferred_element_type=F32)
        spread = jnp.dot(in_two(center * center), mean_of, preferred_element_type=F32)
        normed = center * lax.rsqrt(spread + NORM_EPS) * scale[:, cols] + offset[:, cols]
        out.append((normed * g_ref[here, cols].astype(F32)).astype(BF))
    return jnp.concatenate(out, axis=1)


def place_kernel(place_ref, spot_ref, final_ref, _, state_ref, sem):
    copies = [
        pltpu.make_async_copy(
            final_ref.at[p], state_ref.at[slot_of(place_ref, spot_ref, p)], sem.at[p]
        )
        for p in range(2)
    ]
    for copy in copies:
        copy.start()
    for copy in copies:
        copy.wait()


def place_states(place, spots, final, states):
    return pl.pallas_call(
        place_kernel,
        out_shape=jax.ShapeDtypeStruct(states.shape, F32),
        grid_spec=pltpu.PrefetchScalarGridSpec(
            num_scalar_prefetch=2,
            grid=(1,),
            in_specs=[pl.BlockSpec(final.shape, lambda i, *s: (0, 0, 0, 0)), ANY],
            out_specs=ANY,
            scratch_shapes=[pltpu.SemaphoreType.DMA((2,))],
        ),
        input_output_aliases={3: 0},
        compiler_params=params(1),
        cost_estimate=cost(0, 2 << 20),
        name="place_states",
    )(place, spots, final, states)


def span_tables():
    t = np.arange(CH)
    blocks = []
    size = 4
    while size <= CH:
        start = (t // size) * size
        mid = start + size // 2
        m = np.zeros((CH, CH), np.float32)
        for i in range(CH):
            if i >= mid[i]:
                m[i, mid[i] : i] = 1.0
            else:
                m[i, i + 1 : mid[i]] = 1.0
        blocks.append(m)
        size *= 2
    before = (t[None, :] < t[:, None]).astype(np.float32)
    after = (t[None, :] > t[:, None]).astype(np.float32)
    whole = np.ones((8, CH), np.float32)
    table = np.concatenate(blocks + [before, after, whole])
    return np.concatenate([table, table], axis=1)


LEVELS = int(np.log2(CH))


def wkv_kernel(
    count_ref, keep_ref, table_ref, *refs, t0, span, slot0, last, chained, prompts
):
    ins, refs = refs[: 5 * prompts], refs[5 * prompts :]
    vec_ref, start_ref, slots_ref, rd_ref, kd_ref, vd_ref, wd_ref, gd_ref = refs[:8]
    refs = refs[9:] if chained else refs[8:]
    out_ref, state_ref, next_ref = refs[:3]
    turned = refs[-4:-1]
    y_ref = refs[-1]
    c = pl.program_id(0)

    @pl.when(c == 0)
    def _():
        state_ref[...] = start_ref[...]
        turn_decode(rd_ref, kd_ref, wd_ref, *turned)

    table = table_ref[...]
    row = lax.broadcasted_iota(jnp.int32, (CH, 512), 0)
    low = lax.broadcasted_iota(jnp.int32, (CH, 128), 1) < 64
    arow = lax.broadcasted_iota(jnp.int32, (CH, 2 * CH), 0)
    acol = lax.broadcasted_iota(jnp.int32, (CH, 2 * CH), 1) & (CH - 1)
    diff = arow ^ acol
    causal = arow > acol
    same_head = (lax.broadcasted_iota(jnp.int32, (128, 128), 0) < 64) == (
        lax.broadcasted_iota(jnp.int32, (128, 128), 1) < 64
    )
    mean_of = head_mask(1.0 / 64)
    mean_two = jnp.concatenate([mean_of, mean_of], axis=0)
    reward, scale, offset = vec_ref[0:1], vec_ref[1:2], vec_ref[2:3]
    contract_lanes = (((1,), (1,)), ((), ()))
    contract_rows = (((0,), (0,)), ((), ()))

    def both_heads(a):
        zero = jnp.zeros_like(a)
        return jnp.concatenate([jnp.where(low, a, zero), jnp.where(low, zero, a)], axis=0)

    def lanes_dot(a, b):
        return lax.dot_general(a, b, contract_lanes, preferred_element_type=F32)

    def dot(a, b):
        return jnp.dot(a, b, preferred_element_type=F32)

    streams = [(p, q) for p in range(prompts) for q in range(4)]
    cols = [slice(128 * q, 128 * q + 128) for q in range(4)]
    keys, own, mixed, r_dec, k_dec, whole, values = {}, {}, {}, {}, {}, {}, {}
    for p in range(prompts):
        r_ref, k_ref, v_ref, w_ref, g_ref = ins[5 * p : 5 * p + 5]
        live = (row + (c * CH + t0)) < count_ref[p]
        r = r_ref[0].astype(F32)
        k = jnp.where(live, k_ref[0].astype(F32), 0.0)
        values[p] = v_ref[0]
        w = w_ref[...]
        w_hi = w.astype(BF)
        w_lo = (w - w_hi.astype(F32)).astype(BF)
        factors = jnp.exp(dot(table, jnp.concatenate([w_hi, w_lo], axis=0)))
        r_dec[p] = (r * factors[(LEVELS - 1) * CH : LEVELS * CH]).astype(BF)
        k_dec[p] = (k * factors[LEVELS * CH : (LEVELS + 1) * CH]).astype(BF)
        whole[p] = factors[(LEVELS + 1) * CH : (LEVELS + 1) * CH + 1]
        weighted = r * reward
        hi = weighted.astype(BF)
        own[p] = (hi, (weighted - hi.astype(F32)).astype(BF))
        keys[p] = k.astype(BF)
        mixed[p] = [jnp.where((row & 1) == 1, r, k).astype(BF)]
        for level in range(1, LEVELS):
            pick = jnp.where((row & (1 << level)) != 0, r, k)
            mixed[p].append((pick * factors[(level - 1) * CH : level * CH]).astype(BF))
    scores = {}
    for p, q in streams:
        key = both_heads(keys[p][:, cols[q]])
        s = lanes_dot(
            jnp.concatenate([half[:, cols[q]] for half in own[p]], axis=1),
            jnp.concatenate([key, key], axis=1),
        )
        scores[p, q] = jnp.where(diff == 0, s, 0.0)
    for level in range(LEVELS):
        here = jnp.logical_and(causal, (diff >> level) == 1)
        for p, q in streams:
            a = mixed[p][level][:, cols[q]]
            scores[p, q] = jnp.where(here, lanes_dot(a, both_heads(a)), scores[p, q])
    y = {}
    for p, q in streams:
        v = values[p][:, cols[q]]
        state = state_ref[p, q]
        y[p, q] = dot(scores[p, q].astype(BF), both_heads(v)) + lanes_dot(
            r_dec[p][:, cols[q]], state.astype(BF)
        )
        added = lax.dot_general(v, k_dec[p][:, cols[q]], contract_rows, preferred_element_type=F32)
        state_ref[p, q] = state * whole[p][:, cols[q]] + jnp.where(same_head, added, 0.0)
    center = {n: y[n] - dot(in_two(y[n]), mean_two) for n in streams}
    spread = {n: dot((center[n] * center[n]).astype(BF), mean_of) for n in streams}
    for p, q in streams:
        normed = center[p, q] * lax.rsqrt(spread[p, q] + NORM_EPS)
        gate = ins[5 * p + 4][:, cols[q]].astype(F32)
        at = pl.multiple_of(p * span + c * CH, CH)
        out_ref[pl.ds(at, CH), cols[q]] = (
            (normed * scale[:, cols[q]] + offset[:, cols[q]]) * gate
        ).astype(out_ref.dtype)

    done = decode_slots(
        slot0 + c * SLOT_BLOCK, keep_ref, slots_ref, rd_ref, kd_ref, vd_ref, gd_ref, vec_ref,
        next_ref, *turned, y_ref,
    )
    at = pl.multiple_of(prompts * span + c * SLOT_BLOCK, SLOT_BLOCK)
    out_ref[pl.ds(at, SLOT_BLOCK), :] = done

    if last:
        final_ref = refs[3]

        @pl.when(c == pl.num_programs(0) - 1)
        def _():
            for p, q in streams:
                whole_state = jnp.transpose(state_ref[p, q])
                final_ref[p, 2 * q] = whole_state[:64, :64]
                final_ref[p, 2 * q + 1] = whole_state[64:, 64:]


def wkv(counts, keep, rkv, log_decay, gate, vectors, start, states, earlier, t0, t1, length):
    prompts, slots = start.shape[0], states.shape[0]
    table = jnp.asarray(span_tables(), BF)
    c0, per, span = t0 // CH, length // CH, t1 - t0
    chunks = span // CH
    last, chained = t1 == length, earlier is not None
    at = prompts * length // slots

    def part(n, p):
        return pl.BlockSpec((1, CH, 512), lambda c, s, k: (n, p * per + c + c0, 0))

    def flat(p):
        return pl.BlockSpec((CH, 512), lambda c, s, k: (p * per + c + c0, 0))

    def slot_part(n):
        return pl.BlockSpec((1, slots, 512), lambda c, s, k: (n, at, 0))

    slot_flat = pl.BlockSpec((slots, 512), lambda c, s, k: (at, 0))
    big = pl.BlockSpec((SLOT_BLOCK, 8, 64, 64), lambda c, s, k: (c + c0, 0, 0, 0))
    held = pl.BlockSpec((prompts, 4, 128, 128), lambda c, s, k: (0, 0, 0, 0))
    rows = prompts * span + chunks * SLOT_BLOCK
    out_shape = [
        jax.ShapeDtypeStruct((rows, 512), BF),
        jax.ShapeDtypeStruct((prompts, 4, 128, 128), F32),
        jax.ShapeDtypeStruct(states.shape, F32),
    ]
    out_specs = [pl.BlockSpec((rows, 512), lambda c, s, k: (0, 0)), held, big]
    if last:
        out_shape.append(jax.ShapeDtypeStruct((prompts, 8, 64, 64), F32))
        out_specs.append(pl.BlockSpec((prompts, 8, 64, 64), lambda c, s, k: (0, 0, 0, 0)))
    ins, specs = [], []
    for p in range(prompts):
        ins += [rkv, rkv, rkv, log_decay, gate]
        specs += [part(0, p), part(1, p), part(2, p), flat(p), flat(p)]
    ins += [vectors, start, states, rkv, rkv, rkv, log_decay, gate]
    specs += [pl.BlockSpec((8, 512), lambda c, s, k: (0, 0)), held, big]
    specs += [slot_part(0), slot_part(1), slot_part(2), slot_flat, slot_flat]
    alias = {}
    if chained:
        ins.append(earlier)
        specs.append(ANY)
        alias = {2 + len(ins): 2}
    return pl.pallas_call(
        functools.partial(
            wkv_kernel,
            t0=t0,
            span=span,
            slot0=c0 * SLOT_BLOCK,
            last=last,
            chained=chained,
            prompts=prompts,
        ),
        out_shape=out_shape,
        grid_spec=pltpu.PrefetchScalarGridSpec(
            num_scalar_prefetch=2,
            grid=(chunks,),
            in_specs=[pl.BlockSpec(table.shape, lambda c, s, k: (0, 0))] + specs,
            out_specs=out_specs,
            scratch_shapes=[
                pltpu.VMEM((4, 64, 128), BF),
                pltpu.VMEM((4, 64, 128), BF),
                pltpu.VMEM((4, 64, 256), BF),
                pltpu.VMEM((SLOT_BLOCK, 512), F32),
            ],
        ),
        input_output_aliases=alias,
        compiler_params=params(1),
        cost_estimate=cost(span * 80_000_000, span << 17),
        name="wkv",
    )(counts, keep, table, *ins)


def on_device(
    learner_acceptance_matrix,
    learner_address_matrix,
    learner_content_matrix,
    learner_gating_matrix,
    learner_result_matrix,
    fading_narrowing_matrix,
    fading_widening_matrix,
    feature_fading_speed,
    current_reward,
    symbol_blending_factors,
    group_scaling_factor,
    group_scaling_offset,
    request_hidden_entries,
    request_valid_count,
    request_destination_place,
    newest_symbol_hidden,
    preceding_hidden_entry,
    place_memory_matrix,
    place_newness_marks,
):
    h = lax.axis_index("yh") * 2 + lax.axis_index("core")
    z, x, yl = lax.axis_index("z"), lax.axis_index("x"), lax.axis_index("yl")
    place = jnp.stack([h, z, x, yl]).astype(jnp.int32)
    prompts, length, width = request_hidden_entries.shape
    slots, groups, breadth = place_memory_matrix.shape[:3]
    tokens = prompts * length
    rows = tokens + slots
    counts, spots, marks = in_hbm(
        request_valid_count, request_destination_place, place_newness_marks
    )

    parts, own, new_shift = split(
        place,
        marks,
        counts,
        spots,
        [
            learner_acceptance_matrix,
            learner_address_matrix,
            learner_content_matrix,
            learner_gating_matrix,
            learner_result_matrix,
        ],
        request_hidden_entries.reshape(tokens, width),
        newest_symbol_hidden,
        preceding_hidden_entry,
    )
    blocks = [parts[0]] + [swap(parts[d], "head", d) for d in (1, 2, 3)]
    side = swap(own, "head", 1)
    far = swap(after(own, blocks[3]), "head", 2)
    stacked = jnp.stack(blocks)
    neighbour = swap(stacked, "yl", 1)
    far_side = swap(far, "head", 1)

    def mixes(piece, d, mixed, low):
        return mix(
            place,
            counts,
            piece,
            d,
            symbol_blending_factors,
            fading_narrowing_matrix.T,
            low,
            mixed,
            fading_widening_matrix,
            feature_fading_speed[None],
            slots,
            length,
        )

    every, first, second = slice(0, 5), slice(0, 3), slice(3, 5)
    mixed, low = mixes(own, 0, None, None)
    neighbour, side, low = lax.optimization_barrier((neighbour, side, low))
    by_row = in_order(stacked, neighbour, yl)
    held = [by_row[p][None, None] for p in range(4)]
    recv = swap_all(held, 0)
    held = pack(place, held, recv, 0, every)
    recv = swap_all(held, 1)
    mixed, low = mixes(side, 1, mixed, low)
    held = pack(place, held, after(recv, low), 1, every)
    recv = swap_all(held, 2)
    mixed, low = mixes(far, 2, mixed, low)
    recv = after(recv, low)
    early = pack(place, held, recv, 2, first)
    early_recv = swap_all(early, 3)
    mixed, log_decay = mixes(far_side, 3, mixed, low)
    late = pack(place, held, after(recv, log_decay), 2, second)
    early_recv = after(early_recv, log_decay)
    late_recv = swap_all(after(late, early_recv), 3)
    early = list(early) + early_recv
    late = list(late) + late_recv

    rkv = project_rkv(place, mixed, early, rows)
    gate = project_gate(place, mixed, late, rows // 2)
    small = jnp.stack([current_reward, group_scaling_factor, group_scaling_offset])
    vectors = jnp.concatenate([small, jnp.zeros((5, width), F32)])
    state = jnp.zeros((prompts, groups // 2, 128, 128), F32)
    sent = []
    t0 = 0
    new_state = None
    for t1 in (256, 448, 512):
        out = wkv(
            counts,
            marks,
            rkv,
            log_decay,
            gate,
            vectors,
            state,
            place_memory_matrix,
            new_state,
            t0,
            t1,
            length,
        )
        normed, state, new_state = out[:3]
        n_side = swap(normed, "head", 1)
        n_far = swap(normed, "head", 2)
        if t1 == length:
            sent[1][2] = after(sent[1][2], normed)
            sent[1].append(swap(sent[1][2], "head", 1))
            result = project_result(
                place, counts, spots, sent[0], late, (256,), 0, None, length, slots
            )
            n_far = after(n_far, result[1])
        sent.append([normed, n_side, n_far])
        if t0 == 0 or t1 == length:
            sent[-1].append(swap(n_far, "head", 1))
        t0 = t1
    prompt_hidden, decode_hidden = project_result(
        place, counts, spots, sent[1] + sent[2], late, (192, 64), 256, result, length, slots
    )
    final_state = out[3]
    new_state = place_states(place, spots, final_state, new_state)
    return (prompt_hidden, decode_hidden, new_state, new_shift)


def solution(mesh):
    split = Mesh(mesh.devices.reshape(2, 2, 4, 4, 2), ("yh", "core", "z", "x", "yl"))
    head = ("yh", "core")
    req = ("z", "x", "yl")
    row_shard = P(head + req, None)
    in_specs = (
        row_shard,
        row_shard,
        row_shard,
        row_shard,
        row_shard,
        P(),
        P(None, head),
        P(head),
        P(head),
        P(),
        P(head),
        P(head),
        P(req, None, head),
        P(req),
        P(req),
        P(req, head),
        P(req, head),
        P(req, head, None, None),
        P(req),
    )
    out_specs = (
        P(req, None, head),
        P(req, head),
        P(req, head, None, None),
        P(req, head),
    )
    return jax.shard_map(
        on_device, mesh=split, in_specs=in_specs, out_specs=out_specs, check_vma=False
    )
```

```python
import functools

import jax
import jax.numpy as jnp
import numpy as np
from jax import lax
from jax.experimental import pallas as pl
from jax.experimental.pallas import tpu as pltpu
from jax.sharding import Mesh
from jax.sharding import PartitionSpec as P

NORM_EPS = 0.00064
N_HEAD = 4
CH = 64
BF = jnp.bfloat16
F32 = jnp.float32


STEPS = (("x", 1), ("z", 1), ("x", 3), ("z", 3))


def swap(a, axes, bits):
    sizes = {"x": 4, "z": 4, "yl": 2, "head": 4}
    names = ("yh", "core") if axes == "head" else axes
    return lax.ppermute(a, names, [(i, i ^ bits) for i in range(sizes[axes])])


def order_of(part):
    return [STEPS[(part + n) % 4] for n in range(4)]


def after(value, other):
    return lax.optimization_barrier((value, other))[0]


ANY = pl.BlockSpec(memory_space=pl.ANY)


def in_hbm(*arrays):
    return [pltpu.with_memory_space_constraint(a, pltpu.HBM) for a in arrays]


def cost(flops, nbytes, trans=0):
    return pl.CostEstimate(flops=flops, bytes_accessed=nbytes, transcendentals=trans)


def params(axes):
    return pltpu.CompilerParams(
        dimension_semantics=("arbitrary",) * axes, vmem_limit_bytes=48 << 20
    )


def kept_of(fresh_ref, n):
    return jnp.where(fresh_ref[n] == 1, 0.0, 1.0)


def slot_of(place_ref, spot_ref, p):
    return spot_ref[p] - (place_ref[1] * 8 + place_ref[2] * 2 + place_ref[3]) * 64


def split_kernel(place_ref, keep_ref, count_ref, spot_ref, *refs):
    mats, hid, newest, prior = refs[:5], refs[5], refs[6], refs[7]
    outs, own_ref, shift_ref = refs[8:12], refs[12], refs[13]
    buf, old, sem = refs[14:]
    tokens, slots = hid.shape[0], newest.shape[0]
    copies = [pltpu.make_async_copy(mats[m], buf.at[m], sem.at[m]) for m in range(5)]
    copies += [
        pltpu.make_async_copy(prior, old, sem.at[5]),
        pltpu.make_async_copy(newest, own_ref.at[pl.ds(tokens, slots)], sem.at[6]),
        pltpu.make_async_copy(hid, own_ref.at[pl.ds(0, tokens)], sem.at[7]),
    ]
    for copy in copies:
        copy.start()
    row = lax.broadcasted_iota(jnp.int32, (slots, 512), 0)
    keep = jnp.zeros((slots, 512), F32)
    for n in range(slots):
        keep = jnp.where(row == n, kept_of(keep_ref, n), keep)
    for m in range(5):
        copies[m].wait()
    for d in range(4):
        at = pl.multiple_of((place_ref[0] ^ d) * 512, 512)
        for m in range(5):
            outs[d][m] = buf[m, :, pl.ds(at, 512)].astype(BF)
    copies[5].wait()
    kept = jnp.where(keep > 0.5, old[...].astype(F32), 0.0)
    own_ref[tokens + slots :] = kept.astype(BF)
    copies[6].wait()
    copies[7].wait()
    shift = own_ref[tokens : tokens + slots].astype(F32)
    few = lax.broadcasted_iota(jnp.int32, (16, 512), 0)
    for p in range(2):
        at = p * (tokens // 2) + count_ref[p] - 1
        base = pl.multiple_of((at >> 4) << 4, 16)
        near = own_ref[pl.ds(base, 16)].astype(F32)
        last = jnp.sum(jnp.where(few == (at & 15), near, 0.0), axis=0, keepdims=True)
        shift = jnp.where(row == slot_of(place_ref, spot_ref, p), last, shift)
    shift_ref[...] = shift.astype(BF)


def split(place, keep, counts, spots, matrices, hidden, newest, prior):
    rows, width = matrices[0].shape[0], matrices[0].shape[1] // N_HEAD
    shape = (len(matrices), rows, width)
    total = hidden.shape[0] + 2 * newest.shape[0]
    hbm = pl.BlockSpec(memory_space=pltpu.HBM)
    out = pl.pallas_call(
        split_kernel,
        out_shape=[jax.ShapeDtypeStruct(shape, BF)] * 4
        + [jax.ShapeDtypeStruct((total, width), BF), jax.ShapeDtypeStruct(newest.shape, BF)],
        grid_spec=pltpu.PrefetchScalarGridSpec(
            num_scalar_prefetch=4,
            grid=(1,),
            in_specs=[hbm] * 8,
            out_specs=[pl.BlockSpec(shape, lambda i, *s: (0, 0, 0))] * 4
            + [
                pl.BlockSpec((total, width), lambda i, *s: (0, 0)),
                pl.BlockSpec(newest.shape, lambda i, *s: (0, 0)),
            ],
            scratch_shapes=[
                pltpu.VMEM((5,) + matrices[0].shape, F32),
                pltpu.VMEM(newest.shape, BF),
                pltpu.SemaphoreType.DMA((8,)),
            ],
        ),
        compiler_params=params(1),
        name="split",
    )(place, keep, counts, spots, *in_hbm(*matrices, hidden, newest, prior))
    return out[:4], out[4], out[5]


def in_order(own, other, yl):
    first = yl == 0
    return jnp.concatenate(
        [jnp.where(first, own, other), jnp.where(first, other, own)], axis=-2
    )


def axis_dim(axis):
    return 0 if axis == "z" else 1


def places(p, n, place_ref):
    axis, bits = order_of(p)[n]
    pos = place_ref[1] if axis == "z" else place_ref[2]
    seen = [b for name, b in order_of(p)[:n] if name == axis]
    offsets = [0] + seen
    return [pos ^ o for o in offsets], [pos ^ bits ^ o for o in offsets]


def part_of(ref, dim, i, lot):
    return ref.at[i, :, lot] if dim == 0 else ref.at[:, i, lot]


def pack_kernel(place_ref, *refs, n, lot):
    owns, recvs, outs, sem = refs[:4], refs[4:8], refs[8:12], refs[12]
    copies = []
    for p in range(4):
        dim = axis_dim(order_of(p)[n][0])
        own_at, recv_at = places(p, n, place_ref)
        if len(own_at) == 1:
            own_at, recv_at = [0], [1]
        for src, at in ((owns[p], own_at), (recvs[p], recv_at)):
            for i, j in enumerate(at):
                source = part_of(src, dim, i, lot)
                target = part_of(outs[p], dim, j, slice(None))
                copies.append(pltpu.make_async_copy(source, target, sem.at[len(copies)]))
    for copy in copies:
        copy.start()
    for copy in copies:
        copy.wait()


def pack(place, owns, recvs, n, lot):
    shapes = []
    for p in range(4):
        shape = list(owns[p].shape)
        shape[axis_dim(order_of(p)[n][0])] *= 2
        shape[2] = lot.stop - lot.start
        shapes.append(jax.ShapeDtypeStruct(tuple(shape), BF))
    return pl.pallas_call(
        functools.partial(pack_kernel, n=n, lot=lot),
        out_shape=shapes,
        grid_spec=pltpu.PrefetchScalarGridSpec(
            num_scalar_prefetch=1,
            grid=(1,),
            in_specs=[ANY] * 8,
            out_specs=[pl.BlockSpec(a.shape, lambda i, s: (0, 0, 0, 0, 0)) for a in shapes],
            scratch_shapes=[pltpu.SemaphoreType.DMA((16,))],
        ),
        compiler_params=params(1),
        cost_estimate=cost(0, 8 << 20),
        name="pack",
    )(place, *(in_hbm(*owns, *recvs) if n == 2 else (*owns, *recvs)))


def swap_all(owns, n):
    return [swap(owns[p], *order_of(p)[n]) for p in range(4)]


def copy_weights(pieces, m, place_ref, buf, sem):
    for p in range(4):
        dim = axis_dim(order_of(p)[3][0])
        own_at, recv_at = places(p, 3, place_ref)
        for src, at in ((pieces[p], own_at), (pieces[p + 4], recv_at)):
            for i, j in enumerate(at):
                target = buf.at[p * 4 + j] if dim == 0 else buf.at[pl.ds(p * 4, 4), j]
                pltpu.make_async_copy(part_of(src, dim, i, m), target, sem).start()


def wait_weights(buf, sem):
    pltpu.make_async_copy(buf, buf, sem).wait()


def mix_kernel(place_ref, count_ref, *refs, d, length):
    hid_ref, mu_ref, narrow_ref = refs[:3]
    refs = refs[3:]
    if d > 0:
        low_in, refs = refs[0], refs[2:]
    if d == 3:
        widen_ref, speed_ref, refs = refs[0], refs[1], refs[2:]
    x_ref, low_ref, cur_ref, step_ref = refs
    i = pl.program_id(0)
    rows = cur_ref.shape[0]
    slots = hid_ref.shape[0] - rows
    tokens = rows - slots

    @pl.when(i == 0)
    def _():
        cur = hid_ref[:rows].astype(F32)
        cur_ref[...] = cur
        seq = cur[:tokens]
        at = lax.broadcasted_iota(jnp.int32, seq.shape, 0)
        before = jnp.where((at & (length - 1)) == 0, 0.0, pltpu.roll(seq, 1, 0))
        step_ref[:tokens] = before - seq
        step_ref[tokens:] = hid_ref[rows:].astype(F32) - cur[tokens:]

    mixed = (cur_ref[...] + step_ref[...] * mu_ref[pl.ds(i, 1), :]).astype(BF)
    x_ref[0] = mixed

    @pl.when(i == 3)
    def _():
        low = lax.dot_general(
            mixed, narrow_ref[...], (((1,), (1,)), ((), ())), preferred_element_type=F32
        )
        if d > 0:
            low = low + low_in[...]
        if d < 3:
            low_ref[...] = low
        else:
            lowrank = jnp.tanh(low).astype(BF)
            rate = jnp.exp(jnp.dot(lowrank, widen_ref[...], preferred_element_type=F32))
            log_decay = -speed_ref[...] * rate
            at = lax.broadcasted_iota(jnp.int32, (rows, 512), 0)
            limit = jnp.where(
                at < length,
                count_ref[0],
                jnp.where(at < 2 * length, count_ref[1] + length, rows),
            )
            low_ref[...] = jnp.where(at < limit, log_decay, 0.0)


def mix(place, counts, hidden, d, mu, narrow, low, held, widen, speed, slots, length):
    rows = hidden.shape[0] - slots
    once = lambda i, s, c: (0, 0)
    args = [hidden] + in_hbm(mu, narrow)
    specs = [
        pl.BlockSpec(hidden.shape, once),
        pl.BlockSpec((5, 512), lambda i, s, c: (0, s[0] ^ d)),
        pl.BlockSpec((64, 512), lambda i, s, c: (0, s[0] ^ d)),
    ]
    alias = {}
    if d > 0:
        args += [low, held]
        specs += [pl.BlockSpec(low.shape, once), ANY]
        alias = {6: 0}
    wide = 64
    if d == 3:
        args += in_hbm(widen, speed)
        specs += [pl.BlockSpec(widen.shape, once), pl.BlockSpec(speed.shape, once)]
        wide = 512
    return pl.pallas_call(
        functools.partial(mix_kernel, d=d, length=length),
        out_shape=(
            jax.ShapeDtypeStruct((5, rows, 2048), BF),
            jax.ShapeDtypeStruct((rows, wide), F32),
        ),
        grid_spec=pltpu.PrefetchScalarGridSpec(
            num_scalar_prefetch=2,
            grid=(5,),
            in_specs=specs,
            out_specs=(
                pl.BlockSpec((1, rows, 512), lambda i, s, c: (i, 0, d)),
                pl.BlockSpec((rows, wide), once),
            ),
            scratch_shapes=[pltpu.VMEM((rows, 512), F32), pltpu.VMEM((rows, 512), F32)],
        ),
        input_output_aliases=alias,
        compiler_params=params(1),
        cost_estimate=cost(20 * rows * 512, 12 * rows * 512),
        name="mix",
    )(place, counts, *args)


def rkv_kernel(place_ref, x_ref, *refs):
    pieces = refs[:8]
    out_ref, buf, sem = refs[8:]
    i, j = pl.program_id(0), pl.program_id(1)
    slot = lax.rem(i, 2)

    @pl.when(jnp.logical_and(i == 0, j == 0))
    def _():
        copy_weights(pieces, 0, place_ref, buf.at[0], sem.at[0])

    @pl.when(j == 0)
    def _():
        @pl.when(i < 2)
        def _():
            copy_weights(pieces, i + 1, place_ref, buf.at[1 - slot], sem.at[1 - slot])

        wait_weights(buf.at[slot], sem.at[slot])

    w = buf[slot].reshape(2048, 512)
    out_ref[0] = jnp.dot(x_ref[0], w, preferred_element_type=F32).astype(out_ref.dtype)


def project_rkv(place, mixed, pieces, tile):
    rows = mixed.shape[1]
    return pl.pallas_call(
        rkv_kernel,
        out_shape=jax.ShapeDtypeStruct((3, rows, 512), BF),
        grid_spec=pltpu.PrefetchScalarGridSpec(
            num_scalar_prefetch=1,
            grid=(3, rows // tile),
            in_specs=[pl.BlockSpec((1, tile, 2048), lambda i, j, s: (i, j, 0))] + [ANY] * 8,
            out_specs=pl.BlockSpec((1, tile, 512), lambda i, j, s: (i, j, 0)),
            scratch_shapes=[
                pltpu.VMEM((2, 16, 4, 32, 512), BF),
                pltpu.SemaphoreType.DMA((2,)),
            ],
        ),
        compiler_params=params(2),
        cost_estimate=cost(6 * rows * 2048 * 512, 24 << 20),
        name="project_rkv",
    )(place, mixed, *pieces)


def gate_kernel(place_ref, x_ref, *refs):
    pieces = refs[:8]
    out_ref, buf, sem = refs[8:]

    @pl.when(pl.program_id(0) == 0)
    def _():
        copy_weights(pieces, 0, place_ref, buf, sem)
        wait_weights(buf, sem)

    total = jnp.dot(x_ref[0], buf[...].reshape(2048, 512), preferred_element_type=F32)
    out_ref[...] = (total / (1.0 + jnp.exp(-total))).astype(out_ref.dtype)


def project_gate(place, mixed, pieces, tile):
    rows = mixed.shape[1]
    return pl.pallas_call(
        gate_kernel,
        out_shape=jax.ShapeDtypeStruct((rows, 512), BF),
        grid_spec=pltpu.PrefetchScalarGridSpec(
            num_scalar_prefetch=1,
            grid=(rows // tile,),
            in_specs=[pl.BlockSpec((1, tile, 2048), lambda j, s: (4, j, 0))] + [ANY] * 8,
            out_specs=pl.BlockSpec((tile, 512), lambda j, s: (j, 0)),
            scratch_shapes=[pltpu.VMEM((16, 4, 32, 512), BF), pltpu.SemaphoreType.DMA(())],
        ),
        compiler_params=params(1),
        cost_estimate=cost(2 * rows * 2048 * 512, 8 << 20),
        name="project_gate",
    )(place, mixed, *pieces)


def result_kernel(place_ref, count_ref, spot_ref, *refs, spans, t0, slot0, chained):
    lots = len(spans)
    xs, pieces = refs[: 4 * lots], refs[4 * lots : 4 * lots + 8]
    rest = refs[4 * lots + 8 + (2 if chained else 0) :]
    out_ref, slot_ref, buf, sem = rest
    copy_weights(pieces, 1, place_ref, buf, sem)
    wait_weights(buf, sem)
    start = slot = 0
    for lot, span in enumerate(spans):
        total = None
        for d in range(4):
            w = buf[4 * d : 4 * d + 4].reshape(512, 512)
            term = jnp.dot(xs[4 * lot + d][...], w, preferred_element_type=F32)
            total = term if total is None else total + term
        at = lax.broadcasted_iota(jnp.int32, (span, 512), 0) + (t0 + start)
        for p in range(2):
            own = jnp.where(at < count_ref[p], total[p * span : (p + 1) * span], 0.0)
            out_ref[p, start : start + span] = own.astype(out_ref.dtype)
        start += span
        more = total.shape[0] - 2 * span
        which = lax.broadcasted_iota(jnp.int32, (more, 512), 0) + (slot0 + slot)
        taken = jnp.logical_or(
            which == slot_of(place_ref, spot_ref, 0), which == slot_of(place_ref, spot_ref, 1)
        )
        own = jnp.where(taken, 0.0, total[2 * span :])
        slot_ref[slot : slot + more] = own.astype(slot_ref.dtype)
        slot += more


def project_result(place, counts, spots, xs, pieces, spans, t0, earlier, length, all_slots):
    span = sum(spans)
    slots = sum(xs[4 * n].shape[0] - 2 * spans[n] for n in range(len(spans)))
    once = lambda i, *s: (0, 0)
    chained = earlier is not None
    block = t0 // span
    return pl.pallas_call(
        functools.partial(
            result_kernel, spans=spans, t0=t0, slot0=block * slots, chained=chained
        ),
        out_shape=[
            jax.ShapeDtypeStruct((2, length, 512), BF),
            jax.ShapeDtypeStruct((all_slots, 512), BF),
        ],
        grid_spec=pltpu.PrefetchScalarGridSpec(
            num_scalar_prefetch=3,
            grid=(1,),
            in_specs=[pl.BlockSpec(a.shape, once) for a in xs] + [ANY] * (10 if chained else 8),
            out_specs=[
                pl.BlockSpec((2, span, 512), lambda i, *s: (0, block, 0)),
                pl.BlockSpec((slots, 512), lambda i, *s: (block, 0)),
            ],
            scratch_shapes=[pltpu.VMEM((16, 4, 32, 512), BF), pltpu.SemaphoreType.DMA(())],
        ),
        input_output_aliases={3 + len(xs) + 8: 0, 3 + len(xs) + 9: 1} if chained else {},
        compiler_params=params(1),
        cost_estimate=cost(4 * span * 2048 * 512, 8 << 20),
        name="project_result",
    )(place, counts, spots, *xs, *in_hbm(*pieces), *(earlier if chained else []))


SLOT_BLOCK = 8


def head_mask(value):
    row = lax.broadcasted_iota(jnp.int32, (128, 128), 0) < 64
    col = lax.broadcasted_iota(jnp.int32, (128, 128), 1) < 64
    return jnp.where(row == col, value, 0.0).astype(BF)


def in_two(a):
    hi = a.astype(BF)
    return jnp.concatenate([hi, (a - hi.astype(F32)).astype(BF)], axis=1)


def turn_decode(r_ref, k_ref, w_ref, rt_ref, kt_ref, dt_ref):
    r = r_ref[0].astype(F32)
    k = k_ref[0].astype(F32)
    decay = jnp.exp(w_ref[...])
    for q in range(4):
        cols = slice(128 * q, 128 * q + 128)

        def turned(a):
            t = jnp.transpose(a[:, cols])
            return jnp.concatenate([t[:64], t[64:]], axis=1)

        rt_ref[q] = turned(r).astype(BF)
        kt_ref[q] = turned(k).astype(BF)
        dt_ref[q] = in_two(turned(decay))


def decode_slots(
    first, keep_ref, s_ref, r_ref, k_ref, v_ref, g_ref, vec_ref, next_ref, rt_ref, kt_ref, dt_ref,
    y_ref,
):
    here = pl.ds(pl.multiple_of(first, SLOT_BLOCK), SLOT_BLOCK)
    v = v_ref[0, here].astype(F32)
    row = lax.broadcasted_iota(jnp.int32, (128, 128), 0)
    low = lax.broadcasted_iota(jnp.int32, (128, 128), 1) < 64
    for s in range(SLOT_BLOCK):
        slot = first + s
        hit = row == jnp.where(low, slot, slot + 64)
        pick = jnp.where(hit, 1.0, 0.0).astype(BF)
        kept = jnp.where(hit, kept_of(keep_ref, slot), 0.0).astype(BF)
        r_b = jnp.dot(rt_ref[...].reshape(256, 128), kept, preferred_element_type=F32)
        k_b = jnp.dot(kt_ref[...].reshape(256, 128), pick, preferred_element_type=F32)
        d_b = jnp.dot(
            dt_ref[...].reshape(256, 256),
            jnp.concatenate([kept, kept], axis=0),
            preferred_element_type=F32,
        )
        for q in range(4):
            span = slice(64 * q, 64 * q + 64)
            cols = slice(128 * q, 128 * q + 128)
            state = jnp.concatenate([s_ref[s, 2 * q], s_ref[s, 2 * q + 1]], axis=1)
            after_it = d_b[span] * state + k_b[span] * v[s : s + 1, cols]
            next_ref[s, 2 * q] = after_it[:, :64]
            next_ref[s, 2 * q + 1] = after_it[:, 64:]
            y_ref[s : s + 1, cols] = jnp.sum(r_b[span] * state, axis=0, keepdims=True)
    r = r_ref[0, here].astype(F32)
    k = k_ref[0, here].astype(F32)
    reward, scale, offset = vec_ref[0:1], vec_ref[1:2], vec_ref[2:3]
    own = r * reward * k
    ones = jnp.concatenate([head_mask(1.0)] * 2, axis=0)
    mean_of = jnp.concatenate([head_mask(1.0 / 64)] * 2, axis=0)
    out = []
    for q in range(4):
        cols = slice(128 * q, 128 * q + 128)
        total = jnp.dot(in_two(own[:, cols]), ones, preferred_element_type=F32)
        y = y_ref[:, cols] + total * v[:, cols]
        center = y - jnp.dot(in_two(y), mean_of, preferred_element_type=F32)
        spread = jnp.dot(in_two(center * center), mean_of, preferred_element_type=F32)
        normed = center * lax.rsqrt(spread + NORM_EPS) * scale[:, cols] + offset[:, cols]
        out.append((normed * g_ref[here, cols].astype(F32)).astype(BF))
    return jnp.concatenate(out, axis=1)


def place_kernel(place_ref, spot_ref, final_ref, _, state_ref, sem):
    copies = [
        pltpu.make_async_copy(
            final_ref.at[p], state_ref.at[slot_of(place_ref, spot_ref, p)], sem.at[p]
        )
        for p in range(2)
    ]
    for copy in copies:
        copy.start()
    for copy in copies:
        copy.wait()


def place_states(place, spots, final, states):
    return pl.pallas_call(
        place_kernel,
        out_shape=jax.ShapeDtypeStruct(states.shape, F32),
        grid_spec=pltpu.PrefetchScalarGridSpec(
            num_scalar_prefetch=2,
            grid=(1,),
            in_specs=[pl.BlockSpec(final.shape, lambda i, *s: (0, 0, 0, 0)), ANY],
            out_specs=ANY,
            scratch_shapes=[pltpu.SemaphoreType.DMA((2,))],
        ),
        input_output_aliases={3: 0},
        compiler_params=params(1),
        cost_estimate=cost(0, 2 << 20),
        name="place_states",
    )(place, spots, final, states)


def span_tables():
    t = np.arange(CH)
    blocks = []
    size = 4
    while size <= CH:
        start = (t // size) * size
        mid = start + size // 2
        m = np.zeros((CH, CH), np.float32)
        for i in range(CH):
            if i >= mid[i]:
                m[i, mid[i] : i] = 1.0
            else:
                m[i, i + 1 : mid[i]] = 1.0
        blocks.append(m)
        size *= 2
    before = (t[None, :] < t[:, None]).astype(np.float32)
    after = (t[None, :] > t[:, None]).astype(np.float32)
    whole = np.ones((8, CH), np.float32)
    table = np.concatenate(blocks + [before, after, whole])
    return np.concatenate([table, table], axis=1)


LEVELS = int(np.log2(CH))


def wkv_kernel(
    count_ref, keep_ref, table_ref, *refs, t0, span, slot0, last, chained, prompts
):
    ins, refs = refs[: 5 * prompts], refs[5 * prompts :]
    vec_ref, start_ref, slots_ref, rd_ref, kd_ref, vd_ref, wd_ref, gd_ref = refs[:8]
    refs = refs[9:] if chained else refs[8:]
    out_ref, state_ref, next_ref = refs[:3]
    turned = refs[-4:-1]
    y_ref = refs[-1]
    c = pl.program_id(0)

    @pl.when(c == 0)
    def _():
        state_ref[...] = start_ref[...]
        turn_decode(rd_ref, kd_ref, wd_ref, *turned)

    table = table_ref[...]
    row = lax.broadcasted_iota(jnp.int32, (CH, 512), 0)
    low = lax.broadcasted_iota(jnp.int32, (CH, 128), 1) < 64
    arow = lax.broadcasted_iota(jnp.int32, (CH, 2 * CH), 0)
    acol = lax.broadcasted_iota(jnp.int32, (CH, 2 * CH), 1) & (CH - 1)
    diff = arow ^ acol
    causal = arow > acol
    same_head = (lax.broadcasted_iota(jnp.int32, (128, 128), 0) < 64) == (
        lax.broadcasted_iota(jnp.int32, (128, 128), 1) < 64
    )
    mean_of = head_mask(1.0 / 64)
    mean_two = jnp.concatenate([mean_of, mean_of], axis=0)
    reward, scale, offset = vec_ref[0:1], vec_ref[1:2], vec_ref[2:3]
    contract_lanes = (((1,), (1,)), ((), ()))
    contract_rows = (((0,), (0,)), ((), ()))

    def both_heads(a):
        zero = jnp.zeros_like(a)
        return jnp.concatenate([jnp.where(low, a, zero), jnp.where(low, zero, a)], axis=0)

    def lanes_dot(a, b):
        return lax.dot_general(a, b, contract_lanes, preferred_element_type=F32)

    def dot(a, b):
        return jnp.dot(a, b, preferred_element_type=F32)

    streams = [(p, q) for p in range(prompts) for q in range(4)]
    cols = [slice(128 * q, 128 * q + 128) for q in range(4)]
    keys, own, mixed, r_dec, k_dec, whole, values = {}, {}, {}, {}, {}, {}, {}
    for p in range(prompts):
        r_ref, k_ref, v_ref, w_ref, g_ref = ins[5 * p : 5 * p + 5]
        live = (row + (c * CH + t0)) < count_ref[p]
        r = r_ref[0].astype(F32)
        k = jnp.where(live, k_ref[0].astype(F32), 0.0)
        values[p] = v_ref[0]
        w = w_ref[...]
        w_hi = w.astype(BF)
        w_lo = (w - w_hi.astype(F32)).astype(BF)
        factors = jnp.exp(dot(table, jnp.concatenate([w_hi, w_lo], axis=0)))
        r_dec[p] = (r * factors[(LEVELS - 1) * CH : LEVELS * CH]).astype(BF)
        k_dec[p] = (k * factors[LEVELS * CH : (LEVELS + 1) * CH]).astype(BF)
        whole[p] = factors[(LEVELS + 1) * CH : (LEVELS + 1) * CH + 1]
        weighted = r * reward
        hi = weighted.astype(BF)
        own[p] = (hi, (weighted - hi.astype(F32)).astype(BF))
        keys[p] = k.astype(BF)
        mixed[p] = [jnp.where((row & 1) == 1, r, k).astype(BF)]
        for level in range(1, LEVELS):
            pick = jnp.where((row & (1 << level)) != 0, r, k)
            mixed[p].append((pick * factors[(level - 1) * CH : level * CH]).astype(BF))
    scores = {}
    for p, q in streams:
        key = both_heads(keys[p][:, cols[q]])
        s = lanes_dot(
            jnp.concatenate([half[:, cols[q]] for half in own[p]], axis=1),
            jnp.concatenate([key, key], axis=1),
        )
        scores[p, q] = jnp.where(diff == 0, s, 0.0)
    for level in range(LEVELS):
        here = jnp.logical_and(causal, (diff >> level) == 1)
        for p, q in streams:
            a = mixed[p][level][:, cols[q]]
            scores[p, q] = jnp.where(here, lanes_dot(a, both_heads(a)), scores[p, q])
    y = {}
    for p, q in streams:
        v = values[p][:, cols[q]]
        state = state_ref[p, q]
        y[p, q] = dot(scores[p, q].astype(BF), both_heads(v)) + lanes_dot(
            r_dec[p][:, cols[q]], state.astype(BF)
        )
        added = lax.dot_general(v, k_dec[p][:, cols[q]], contract_rows, preferred_element_type=F32)
        state_ref[p, q] = state * whole[p][:, cols[q]] + jnp.where(same_head, added, 0.0)
    center = {n: y[n] - dot(in_two(y[n]), mean_two) for n in streams}
    spread = {n: dot((center[n] * center[n]).astype(BF), mean_of) for n in streams}
    for p, q in streams:
        normed = center[p, q] * lax.rsqrt(spread[p, q] + NORM_EPS)
        gate = ins[5 * p + 4][:, cols[q]].astype(F32)
        at = pl.multiple_of(p * span + c * CH, CH)
        out_ref[pl.ds(at, CH), cols[q]] = (
            (normed * scale[:, cols[q]] + offset[:, cols[q]]) * gate
        ).astype(out_ref.dtype)

    done = decode_slots(
        slot0 + c * SLOT_BLOCK, keep_ref, slots_ref, rd_ref, kd_ref, vd_ref, gd_ref, vec_ref,
        next_ref, *turned, y_ref,
    )
    at = pl.multiple_of(prompts * span + c * SLOT_BLOCK, SLOT_BLOCK)
    out_ref[pl.ds(at, SLOT_BLOCK), :] = done

    if last:
        final_ref = refs[3]

        @pl.when(c == pl.num_programs(0) - 1)
        def _():
            for p, q in streams:
                whole_state = jnp.transpose(state_ref[p, q])
                final_ref[p, 2 * q] = whole_state[:64, :64]
                final_ref[p, 2 * q + 1] = whole_state[64:, 64:]


def wkv(counts, keep, rkv, log_decay, gate, vectors, start, states, earlier, t0, t1, length):
    prompts, slots = start.shape[0], states.shape[0]
    table = jnp.asarray(span_tables(), BF)
    c0, per, span = t0 // CH, length // CH, t1 - t0
    chunks = span // CH
    last, chained = t1 == length, earlier is not None
    at = prompts * length // slots

    def part(n, p):
        return pl.BlockSpec((1, CH, 512), lambda c, s, k: (n, p * per + c + c0, 0))

    def flat(p):
        return pl.BlockSpec((CH, 512), lambda c, s, k: (p * per + c + c0, 0))

    def slot_part(n):
        return pl.BlockSpec((1, slots, 512), lambda c, s, k: (n, at, 0))

    slot_flat = pl.BlockSpec((slots, 512), lambda c, s, k: (at, 0))
    big = pl.BlockSpec((SLOT_BLOCK, 8, 64, 64), lambda c, s, k: (c + c0, 0, 0, 0))
    held = pl.BlockSpec((prompts, 4, 128, 128), lambda c, s, k: (0, 0, 0, 0))
    rows = prompts * span + chunks * SLOT_BLOCK
    out_shape = [
        jax.ShapeDtypeStruct((rows, 512), BF),
        jax.ShapeDtypeStruct((prompts, 4, 128, 128), F32),
        jax.ShapeDtypeStruct(states.shape, F32),
    ]
    out_specs = [pl.BlockSpec((rows, 512), lambda c, s, k: (0, 0)), held, big]
    if last:
        out_shape.append(jax.ShapeDtypeStruct((prompts, 8, 64, 64), F32))
        out_specs.append(pl.BlockSpec((prompts, 8, 64, 64), lambda c, s, k: (0, 0, 0, 0)))
    ins, specs = [], []
    for p in range(prompts):
        ins += [rkv, rkv, rkv, log_decay, gate]
        specs += [part(0, p), part(1, p), part(2, p), flat(p), flat(p)]
    ins += [vectors, start, states, rkv, rkv, rkv, log_decay, gate]
    specs += [pl.BlockSpec((8, 512), lambda c, s, k: (0, 0)), held, big]
    specs += [slot_part(0), slot_part(1), slot_part(2), slot_flat, slot_flat]
    alias = {}
    if chained:
        ins.append(earlier)
        specs.append(ANY)
        alias = {2 + len(ins): 2}
    return pl.pallas_call(
        functools.partial(
            wkv_kernel,
            t0=t0,
            span=span,
            slot0=c0 * SLOT_BLOCK,
            last=last,
            chained=chained,
            prompts=prompts,
        ),
        out_shape=out_shape,
        grid_spec=pltpu.PrefetchScalarGridSpec(
            num_scalar_prefetch=2,
            grid=(chunks,),
            in_specs=[pl.BlockSpec(table.shape, lambda c, s, k: (0, 0))] + specs,
            out_specs=out_specs,
            scratch_shapes=[
                pltpu.VMEM((4, 64, 128), BF),
                pltpu.VMEM((4, 64, 128), BF),
                pltpu.VMEM((4, 64, 256), BF),
                pltpu.VMEM((SLOT_BLOCK, 512), F32),
            ],
        ),
        input_output_aliases=alias,
        compiler_params=params(1),
        cost_estimate=cost(span * 80_000_000, span << 17),
        name="wkv",
    )(counts, keep, table, *ins)


def on_device(
    learner_acceptance_matrix,
    learner_address_matrix,
    learner_content_matrix,
    learner_gating_matrix,
    learner_result_matrix,
    fading_narrowing_matrix,
    fading_widening_matrix,
    feature_fading_speed,
    current_reward,
    symbol_blending_factors,
    group_scaling_factor,
    group_scaling_offset,
    request_hidden_entries,
    request_valid_count,
    request_destination_place,
    newest_symbol_hidden,
    preceding_hidden_entry,
    place_memory_matrix,
    place_newness_marks,
):
    h = lax.axis_index("yh") * 2 + lax.axis_index("core")
    z, x, yl = lax.axis_index("z"), lax.axis_index("x"), lax.axis_index("yl")
    place = jnp.stack([h, z, x, yl]).astype(jnp.int32)
    prompts, length, width = request_hidden_entries.shape
    slots, groups, breadth = place_memory_matrix.shape[:3]
    tokens = prompts * length
    rows = tokens + slots
    counts, spots, marks = in_hbm(
        request_valid_count, request_destination_place, place_newness_marks
    )

    parts, own, new_shift = split(
        place,
        marks,
        counts,
        spots,
        [
            learner_acceptance_matrix,
            learner_address_matrix,
            learner_content_matrix,
            learner_gating_matrix,
            learner_result_matrix,
        ],
        request_hidden_entries.reshape(tokens, width),
        newest_symbol_hidden,
        preceding_hidden_entry,
    )
    blocks = [parts[0]] + [swap(parts[d], "head", d) for d in (1, 2, 3)]
    side = swap(own, "head", 1)
    far = swap(after(own, blocks[3]), "head", 2)
    stacked = jnp.stack(blocks)
    neighbour = swap(stacked, "yl", 1)
    far_side = swap(far, "head", 1)

    def mixes(piece, d, mixed, low):
        return mix(
            place,
            counts,
            piece,
            d,
            symbol_blending_factors,
            fading_narrowing_matrix.T,
            low,
            mixed,
            fading_widening_matrix,
            feature_fading_speed[None],
            slots,
            length,
        )

    every, first, second = slice(0, 5), slice(0, 3), slice(3, 5)
    mixed, low = mixes(own, 0, None, None)
    neighbour, side, low = lax.optimization_barrier((neighbour, side, low))
    by_row = in_order(stacked, neighbour, yl)
    held = [by_row[p][None, None] for p in range(4)]
    recv = swap_all(held, 0)
    held = pack(place, held, recv, 0, every)
    recv = swap_all(held, 1)
    mixed, low = mixes(side, 1, mixed, low)
    held = pack(place, held, after(recv, low), 1, every)
    recv = swap_all(held, 2)
    mixed, low = mixes(far, 2, mixed, low)
    recv = after(recv, low)
    early = pack(place, held, recv, 2, first)
    early_recv = swap_all(early, 3)
    mixed, log_decay = mixes(far_side, 3, mixed, low)
    late = pack(place, held, after(recv, log_decay), 2, second)
    early_recv = after(early_recv, log_decay)
    late_recv = swap_all(after(late, early_recv), 3)
    early = list(early) + early_recv
    late = list(late) + late_recv

    rkv = project_rkv(place, mixed, early, rows)
    gate = project_gate(place, mixed, late, rows // 2)
    small = jnp.stack([current_reward, group_scaling_factor, group_scaling_offset])
    vectors = jnp.concatenate([small, jnp.zeros((5, width), F32)])
    state = jnp.zeros((prompts, groups // 2, 128, 128), F32)
    sent = []
    t0 = 0
    new_state = None
    for t1 in (256, 448, 512):
        out = wkv(
            counts,
            marks,
            rkv,
            log_decay,
            gate,
            vectors,
            state,
            place_memory_matrix,
            new_state,
            t0,
            t1,
            length,
        )
        normed, state, new_state = out[:3]
        n_side = swap(normed, "head", 1)
        n_far = swap(normed, "head", 2)
        if t1 == length:
            result = project_result(
                place, counts, spots, sent[0], late, (256,), 0, None, length, slots
            )
            sent[1][2] = after(sent[1][2], (normed, result[1]))
            sent[1].append(swap(sent[1][2], "head", 1))
        sent.append([normed, n_side, n_far])
        if t0 == 0 or t1 == length:
            sent[-1].append(swap(n_far, "head", 1))
        t0 = t1
    prompt_hidden, decode_hidden = project_result(
        place, counts, spots, sent[1] + sent[2], late, (192, 64), 256, result, length, slots
    )
    final_state = out[3]
    new_state = place_states(place, spots, final_state, new_state)
    return (prompt_hidden, decode_hidden, new_state, new_shift)


def solution(mesh):
    split = Mesh(mesh.devices.reshape(2, 2, 4, 4, 2), ("yh", "core", "z", "x", "yl"))
    head = ("yh", "core")
    req = ("z", "x", "yl")
    row_shard = P(head + req, None)
    in_specs = (
        row_shard,
        row_shard,
        row_shard,
        row_shard,
        row_shard,
        P(),
        P(None, head),
        P(head),
        P(head),
        P(),
        P(head),
        P(head),
        P(req, None, head),
        P(req),
        P(req),
        P(req, head),
        P(req, head),
        P(req, head, None, None),
        P(req),
    )
    out_specs = (
        P(req, None, head),
        P(req, head),
        P(req, head, None, None),
        P(req, head),
    )
    return jax.shard_map(
        on_device, mesh=split, in_specs=in_specs, out_specs=out_specs, check_vma=False
    )
```
